32 devices in a mesh: wide: 8 (over z, y), narrow: 4 (over x, core).
Axes of the slice: x: 2, y: 2, z: 4, core: 2. Of those that a mesh axis runs over, the one named last changes fastest.
Arguments:
- tokens: bfloat16 [16384, 1024], P(('wide', 'narrow')), may hold values from -6 to 6
- gain_one: float32 [1024], replicated, may hold values from 0.5 to 1.5
- query_weight: bfloat16 [1024, 1024], P(('wide', 'narrow')), may hold values from -0.046875 to 0.046875
- key_weight: bfloat16 [1024, 1024], P(('wide', 'narrow')), may hold values from -0.1875 to 0.1875
- value_weight: bfloat16 [1024, 1024], P(('wide', 'narrow')), may hold values from -0.1875 to 0.1875
- out_weight: bfloat16 [1024, 1024], P(('wide', 'narrow')), may hold values from -0.5 to 0.5
- gain_two: float32 [1024], replicated, may hold values from 0.5 to 1.5
- gate_weight: bfloat16 [1024, 2816], P(('wide', 'narrow')), may hold values from -0.1875 to 0.1875
- up_weight: bfloat16 [1024, 2816], P(('wide', 'narrow')), may hold values from -0.1875 to 0.1875
- down_weight: bfloat16 [2816, 1024], P(('wide', 'narrow')), may hold values from -0.109375 to 0.109375
- relative_bias_table: float32 [32, 16], replicated, may hold values from -3 to 3
- layout_bias_table: float32 [64, 16], replicated, may hold values from -3 to 3
- doc_lengths: int32 [32, 9], P(('wide', 'narrow')), may hold values from 0 to 512, as said below
- box_x: int32 [16384], P(('wide', 'narrow')), may hold values from 0 to 63
- box_y: int32 [16384], P(('wide', 'narrow')), may hold values from 0 to 63
- cotangent: bfloat16 [16384, 1024], P(('wide', 'narrow')), may hold values from -6 to 6
Outputs:
- block_out: bfloat16 [16384, 1024], P(('wide', 'narrow'))
- grad_tokens: float32 [16384, 1024], P(('wide', 'narrow'))
- grad_gain_one: float32 [1024], replicated
- grad_query_weight: float32 [1024, 1024], P(('wide', 'narrow'))
- grad_key_weight: float32 [1024, 1024], P(('wide', 'narrow'))
- grad_value_weight: float32 [1024, 1024], P(('wide', 'narrow'))
- grad_out_weight: float32 [1024, 1024], P(('wide', 'narrow'))
- grad_gain_two: float32 [1024], replicated
- grad_gate_weight: float32 [1024, 2816], P(('wide', 'narrow'))
- grad_up_weight: float32 [1024, 2816], P(('wide', 'narrow'))
- grad_down_weight: float32 [2816, 1024], P(('wide', 'narrow'))
- grad_rel_table: float32 [32, 16], replicated
- grad_layout_table: float32 [64, 16], replicated
The draws below stay inside these ranges and needn't reach their ends.
Inputs may be any that keep to these rules, and one draw needn't show every extreme that they name: `doc_lengths`: row r lists, in order, the lengths of the documents packed into the 512 tokens of device r along wide+narrow, zeros after the last; a row sums to at most 512 and the rest of the pack is padding. Nonzero lengths are forms of 60 to 300 tokens or tables of 512 tokens, and row 0 starts with a table.
All inputs are finite; a program needn't handle non-finite values.
Results may differ from the reference program's by a relative error of at most 0.014.
The reference program's roundings to bfloat16 on the way count: a program that leaves them out, or rounds other values in their place, can miss the bound.
Values may be sent and summed in bfloat16 or wider, within the bound.
No kernel may reach another device: no remote copies, remote signals or barrier semaphores. Data moves between devices by JAX's collectives and lax.ppermute only.
A program may use at most 256 MiB of HBM per device.

```python
import jax
import jax.numpy as jnp
from jax import lax

D = 1024
HEADS = 16
HEAD = 64
FF = 2816
DISTANCE_BUCKETS = 32
GRID = 64
FORM_MIN = 60
FORM_MAX = 300
TOK_DEV = 512
PACKS = 32
TOKENS = 16384
HD = 1024
DOCS = 9
LONGEST = 512


def draw_doc_lengths(key, part):
    raw_lengths = jax.random.randint(jax.random.fold_in(key, 11), (PACKS, DOCS), FORM_MIN, FORM_MAX + 1, dtype=jnp.int32)
    table_flag = jax.random.randint(jax.random.fold_in(key, 12), (PACKS,), 0, 8, dtype=jnp.int32) == 0
    table_flag = table_flag | (jnp.arange(PACKS, dtype=jnp.int32) == 0)
    first_column = (jnp.arange(DOCS, dtype=jnp.int32) == 0)[None, :]
    raw_lengths = jnp.where(table_flag[:, None] & first_column, LONGEST, raw_lengths)
    running = jnp.cumsum(raw_lengths, axis=1)
    return jnp.where(running <= TOK_DEV, raw_lengths, 0).astype(jnp.int32)


def place_ends(array, own_key, smallest, top_value):
    index_at = [jax.random.randint(jax.random.fold_in(own_key, axis), (), 0, length) for axis, length in enumerate(array.shape)]
    longest = array.shape.index(max(array.shape))
    neighbour = index_at[:longest] + [(index_at[longest] + 1) % array.shape[longest]] + index_at[longest + 1:]
    return array.at[tuple(index_at)].set(smallest).at[tuple(neighbour)].set(top_value)


def steps_of(rng, extent, shards, smallest, top_value):
    factor_of, own = 1.0, jax.random.fold_in(rng, 6)
    for dim, blocks in shards:
        heights = jnp.exp(jax.random.uniform(jax.random.fold_in(own, dim), (blocks,), jnp.float32, smallest / len(shards), top_value / len(shards)))
        factor_of = factor_of * jnp.repeat(heights, extent[dim] // blocks).reshape([-1 if axis == dim else 1 for axis in range(len(extent))])
    return factor_of


def gaussian(own_key, shape, width, limit, shards=(), kind=jnp.bfloat16):
    drawn = jax.random.normal(own_key, shape, jnp.float32) * width
    if len(shards) > 0:
        drawn = steps_of(own_key, shape, shards, -0.22, 0.18) * drawn
    return jnp.clip(drawn, min=-limit, max=limit).astype(kind)


def setup_inputs(seed: int = 0) -> dict:
    seeds = jax.random.split(jax.random.key(seed), 17)
    return {
        "tokens": gaussian(seeds[0], (TOKENS, D), 1.0, 6.0, ((0, 32),)),
        "gain_one": jnp.clip(1.0 + 0.1 * jax.random.normal(seeds[1], (D,), jnp.float32), 0.5, 1.5),
        "query_weight": gaussian(seeds[2], (D, HD), (16 * D) ** -0.5, 0.046875, ((0, 32),)),
        "key_weight": gaussian(seeds[3], (D, HD), D ** -0.5, 0.1875, ((0, 32),)),
        "value_weight": gaussian(seeds[4], (D, HD), D ** -0.5, 0.1875, ((0, 32),)),
        "out_weight": gaussian(seeds[5], (HD, D), (HD // 8) ** -0.5, 0.5, ((0, 32),)),
        "gain_two": jnp.clip(1.0 + 0.1 * jax.random.normal(seeds[6], (D,), jnp.float32), 0.5, 1.5),
        "gate_weight": gaussian(seeds[7], (D, FF), D ** -0.5, 0.1875, ((0, 32),)),
        "up_weight": gaussian(seeds[8], (D, FF), D ** -0.5, 0.1875, ((0, 32),)),
        "down_weight": gaussian(seeds[9], (FF, D), FF ** -0.5, 0.109375, ((0, 32),)),
        "relative_bias_table": gaussian(seeds[10], (DISTANCE_BUCKETS, HEADS), 0.5, 3.0, (), jnp.float32),
        "layout_bias_table": gaussian(seeds[11], (2 * DISTANCE_BUCKETS, HEADS), 0.5, 3.0, (), jnp.float32),
        "doc_lengths": draw_doc_lengths(jax.random.fold_in(seeds[16], 71), 0),
        "box_x": place_ends(jax.random.randint(seeds[13], (TOKENS,), 0, GRID), jax.random.fold_in(seeds[13], 1), 0, GRID - 1).astype(jnp.int32),
        "box_y": place_ends(jax.random.randint(seeds[14], (TOKENS,), 0, GRID), jax.random.fold_in(seeds[14], 1), 0, GRID - 1).astype(jnp.int32),
        "cotangent": gaussian(seeds[15], (TOKENS, D), 1.0, 6.0, ((0, 32),)),
    }


@jax.custom_vjp
def low(v):
    return lax.optimization_barrier(v.astype(jnp.bfloat16)).astype(jnp.float32)

@jax.custom_vjp
def low_back(v):
    return v

def low_keep(v):
    return (low(v), None)

def low_pass(kept, grad):
    return (grad,)

def back_keep(v):
    return (v, None)

def back_low(kept, grad):
    return (low(grad),)
low.defvjp(low_keep, low_pass)
low_back.defvjp(back_keep, back_low)
epsilon = 1e-06
masked_score = -1e+30
bucket_edges = (1, 2, 3, 4, 5, 6, 7, 8, 12, 16, 23, 32, 46, 64, 91)

def bucket_of(offsets):
    magnitude = jnp.abs(offsets)
    bucket_ids = jnp.zeros(offsets.shape, jnp.int32)
    for border in bucket_edges:
        bucket_ids = bucket_ids + (magnitude >= border).astype(jnp.int32)
    return bucket_ids + (offsets > 0).astype(jnp.int32) * (DISTANCE_BUCKETS // 2)

def one_hot_first(buckets, levels):
    return (buckets[None, :, :] == jnp.arange(levels, dtype=jnp.int32)[:, None, None]).astype(jnp.float32)

def matmul(first_op, second_op):
    return jnp.dot(first_op, second_op, precision=lax.Precision.HIGHEST)

def rms_norm(values, gains):
    factor = lax.rsqrt(lax.optimization_barrier(jnp.mean(values * values, axis=-1, keepdims=True)) + epsilon)
    return values * factor * gains

def pair_bias(relative_bias_table, layout_bias_table, positions, pack_x, pack_y):
    relative_onehot = one_hot_first(bucket_of(positions[:, None] - positions[None, :]), DISTANCE_BUCKETS)
    across_onehot = one_hot_first(bucket_of(pack_x[:, None] - pack_x[None, :]), DISTANCE_BUCKETS)
    vertical_onehot = one_hot_first(bucket_of(pack_y[:, None] - pack_y[None, :]), DISTANCE_BUCKETS)
    relative_terms = jnp.einsum('ptj,pa->atj', relative_onehot, relative_bias_table, precision=lax.Precision.HIGHEST)
    horizontal_terms = jnp.einsum('ptj,pa->atj', across_onehot, layout_bias_table[:DISTANCE_BUCKETS], precision=lax.Precision.HIGHEST)
    vertical_terms = jnp.einsum('ptj,pa->atj', vertical_onehot, layout_bias_table[DISTANCE_BUCKETS:], precision=lax.Precision.HIGHEST)
    return relative_terms + horizontal_terms + vertical_terms

def layer_pack(params, pack_inputs):
    gain_one, query_weight, key_weight, value_weight, out_weight, gain_two, gate_weight, up_weight, down_weight, relative_bias_table, layout_bias_table = params
    tokens, pack_lengths, pack_x, pack_y = pack_inputs
    row_count = tokens.shape[0]
    positions = jnp.arange(row_count, dtype=jnp.int32)
    doc_ends = jnp.cumsum(pack_lengths).astype(jnp.int32)
    live_rows = positions < doc_ends[-1]
    doc_ids = lax.optimization_barrier(jnp.sum((positions[:, None] >= doc_ends[None, :]).astype(jnp.int32), axis=1))
    seg_ids = jnp.where(live_rows, doc_ids, pack_lengths.shape[0] + positions)
    allowed = seg_ids[:, None] == seg_ids[None, :]
    live_mask = live_rows.astype(jnp.float32)[:, None]
    normed = low(rms_norm(tokens, gain_one))
    query_rows = low_back(low(matmul(normed, query_weight))).reshape(row_count, HEADS, HEAD)
    key_rows = low_back(low(matmul(normed, key_weight))).reshape(row_count, HEADS, HEAD)
    value_rows = low_back(low(matmul(normed, value_weight))).reshape(row_count, HEADS, HEAD)
    dot_terms = low_back(jnp.einsum('qhe,khe->hqk', query_rows, key_rows, precision=lax.Precision.HIGHEST))
    pair_terms = pair_bias(relative_bias_table, layout_bias_table, positions, pack_x, pack_y)
    scores = jnp.where(allowed[None], dot_terms + pair_terms, masked_score)
    attn_probs = jax.nn.softmax(scores, axis=-1)
    mixed_rows = jnp.einsum('hqk,khe->qhe', low(attn_probs), value_rows, precision=lax.Precision.HIGHEST)
    attended = low_back(low(mixed_rows.reshape(row_count, HEADS * HEAD)))
    branch = low_back(matmul(attended, out_weight))
    hidden = tokens + live_mask * branch
    normed_two = low(rms_norm(hidden, gain_two))
    gate_rows = low_back(matmul(normed_two, gate_weight))
    up_rows = low_back(matmul(normed_two, up_weight))
    inner_rows = low(jax.nn.gelu(gate_rows, approximate=True) * up_rows)
    ffn_rows = low_back(matmul(inner_rows, down_weight))
    return hidden + live_mask * ffn_rows

def forward(params, tokens, doc_lengths, box_x, box_y):
    packed = tokens.reshape(PACKS, TOK_DEV, D)

    def pack_step(unused_carry, pack_inputs):
        return (unused_carry, jax.checkpoint(layer_pack)(params, pack_inputs))
    unused_carry, results = lax.scan(pack_step, jnp.zeros((), jnp.float32), (packed, doc_lengths, box_x.reshape(PACKS, TOK_DEV), box_y.reshape(PACKS, TOK_DEV)))
    return results.reshape(TOKENS, D)

def reference(tokens, gain_one, query_weight, key_weight, value_weight, out_weight, gain_two, gate_weight, up_weight, down_weight, relative_bias_table, layout_bias_table, doc_lengths, box_x, box_y, cotangent):
    params = tuple((weight.astype(jnp.float32) for weight in (gain_one, query_weight, key_weight, value_weight, out_weight, gain_two, gate_weight, up_weight, down_weight, relative_bias_table, layout_bias_table)))
    tokens_wide = tokens.astype(jnp.float32)

    def run_layer(param_set, token_set):
        return forward(param_set, token_set, doc_lengths, box_x, box_y)
    output, pullback = jax.vjp(run_layer, params, tokens_wide)
    param_grads, token_grads = pullback(cotangent.astype(jnp.float32))
    return (output.astype(jnp.bfloat16), token_grads, param_grads[0], param_grads[1], param_grads[2], param_grads[3], param_grads[4], param_grads[5], param_grads[6], param_grads[7], param_grads[8], param_grads[9], param_grads[10])
```

```python
import numpy as np
import jax
import jax.numpy as jnp
from jax import lax
from jax.experimental import pallas as pl
from jax.experimental.pallas import tpu as pltpu
from jax.sharding import PartitionSpec as P

bf = jnp.bfloat16
f4 = jnp.float32

HEADS,HEAD=16,64
bucket_edges=(1,2,3,4,5,6,7,8,12,16,23,32,46,64,91)
GRID=64
def np_bucket(n):
    n=np.asarray(n); m=np.abs(n)
    b=np.zeros(n.shape,np.int32)
    for e in bucket_edges: b+=(m>=e)
    return b+(n>0)*16
BLK=128
NT=(((1,),(1,)),((),()))
NN=(((1,),(0,)),((),()))
def dot(a,b,dims=NN): return lax.dot_general(a,b,dims,preferred_element_type=f4)

def fwd_kernel(q_ref,k_ref,v_ref,oh_ref,ff_ref,w_ref,far_ref,mask_ref,o_ref,p_ref):
    t=q_ref.shape[0]; nb=t//BLK
    lane=lax.broadcasted_iota(jnp.int32,(t,2*HEAD),1)
    q=q_ref[...]; oh=oh_ref[...]; v=v_ref[...]
    oht=oh.T; ka=jnp.concatenate([k_ref[...].T,oht,oht],axis=0)
    for j in range(2):
        mine=(lane<HEAD) if j==0 else (lane>=HEAD)
        band=pltpu.roll(jnp.broadcast_to(w_ref[0,j:j+1,:],(BLK,4*BLK)),0,1,stride=1,stride_axis=0)
        near=far_ref[0,j:j+1,0:BLK]; past=far_ref[0,j:j+1,BLK:2*BLK]
        rows=dot(oh,ff_ref[j]).astype(bf)
        qa=jnp.concatenate([jnp.where(mine,q,jnp.zeros_like(q)),rows],axis=1)
        for s in range(nb):
            sc=dot(qa[s*BLK:(s+1)*BLK],ka)
            rel=[]
            for c in range(nb):
                if c<s-1: rel.append(jnp.broadcast_to(past,(BLK,BLK)))
                elif c>s+1: rel.append(jnp.broadcast_to(near,(BLK,BLK)))
                else: rel.append(band[:,(c-s+1)*BLK:(c-s+2)*BLK])
            sc=(sc+jnp.concatenate(rel,axis=1))+mask_ref[s*BLK:(s+1)*BLK,:]
            top=jnp.max(sc,axis=1,keepdims=True)
            e=jnp.exp(sc-top)
            p=e*(1.0/jnp.sum(e,axis=1,keepdims=True))
            p_ref[j,s*BLK:(s+1)*BLK,:]=p
            o=dot(p.astype(bf),v).astype(bf)
            o_ref[s*BLK:(s+1)*BLK,j*HEAD:(j+1)*HEAD]=o[:,j*HEAD:(j+1)*HEAD]

def bwd_kernel(q_ref,k_ref,v_ref,g_ref,oh_ref,oht_ref,p_ref,d_ref,rel_ref,lay_ref,ds_s,pb_s):
    t=q_ref.shape[0]; nb=t//BLK
    lane=lax.broadcasted_iota(jnp.int32,(t,2*HEAD),1)
    q=q_ref[...]; k=k_ref[...]; v=v_ref[...]; g=g_ref[...]; oh=oh_ref[...]
    koh=jnp.concatenate([k,oh],axis=1)
    qt=q.T; gt=g.T; vt=v.T
    outs=[]
    for j in range(2):
        mine=(lane<HEAD) if j==0 else (lane>=HEAD)
        gm=jnp.where(mine,g,jnp.zeros_like(g))
        band=[jnp.zeros((BLK,BLK),f4) for _ in range(3)]
        past=jnp.zeros((BLK,BLK),f4); near=jnp.zeros((BLK,BLK),f4)
        dq=[]
        for s in range(nb):
            rows=slice(s*BLK,(s+1)*BLK)
            dp=dot(gm[rows],vt)
            p=p_ref[j,rows,:]
            ds=p*(dp-jnp.sum(p*dp,axis=1,keepdims=True))
            for c in range(nb):
                tile=ds[:,c*BLK:(c+1)*BLK]
                if c<s-1: past=past+tile
                elif c>s+1: near=near+tile
                else: band[c-s+1]=band[c-s+1]+tile
            dsb=ds.astype(bf)
            ds_s[rows,:]=dsb; pb_s[rows,:]=p.astype(bf)
            dq.append(dot(dsb,koh))
        dq=jnp.concatenate(dq,axis=0)
        dkt=dot(qt,ds_s[...]); dvt=dot(gt,pb_s[...])
        outs.append((dq[:,:2*HEAD],dkt,dvt))
        r=dq[:,2*HEAD:]
        hi=r.astype(bf); lo=(r-hi.astype(f4)).astype(bf)
        gl=dot(oht_ref[...],jnp.concatenate([hi,lo],axis=1))
        gl=gl[:,:2*GRID]+gl[:,2*GRID:]
        for i in range(2):
            part=gl[i*GRID:(i+1)*GRID,i*GRID:(i+1)*GRID]
            part=pltpu.roll(jnp.concatenate([part,jnp.zeros((GRID,GRID),f4)],axis=1),0,1,stride=1,stride_axis=0)
            lay_ref[0,2*j+i:2*j+i+1,:]=jnp.sum(part,axis=0,keepdims=True)
        wide=jnp.concatenate(band+[jnp.zeros((BLK,BLK),f4)],axis=1)
        acc=wide[0:8]
        for i in range(1,BLK//8):
            acc=acc+pltpu.roll(wide[8*i:8*i+8],4*BLK-8*i,1)
        line=acc[0:1]
        for i in range(1,8):
            line=line+pltpu.roll(acc[i:i+1],4*BLK-i,1)
        rel_ref[0,j:j+1,0:4*BLK]=line
        rel_ref[0,j:j+1,4*BLK:5*BLK]=jnp.sum(near,axis=0,keepdims=True)
        rel_ref[0,j:j+1,5*BLK:6*BLK]=jnp.sum(past,axis=0,keepdims=True)
    d_ref[0]=jnp.where(lane<HEAD,outs[0][0],outs[1][0]).astype(bf)
    sub=lax.broadcasted_iota(jnp.int32,(2*HEAD,t),0)
    d_ref[1]=jnp.where(sub<HEAD,outs[0][1],outs[1][1]).astype(bf).T
    d_ref[2]=jnp.where(sub<HEAD,outs[0][2],outs[1][2]).astype(bf).T

def fwd(qkv,oh,ff,w,far,mask):
    t=qkv.shape[0]; pairs=HEADS//2
    col=lambda off: pl.BlockSpec((t,2*HEAD),lambda i,off=off:(0,off+i))
    return pl.pallas_call(fwd_kernel,grid=(pairs,),
        in_specs=[col(0),col(pairs),col(2*pairs),pl.BlockSpec((t,2*GRID),lambda i:(0,0)),
          pl.BlockSpec((2,2*GRID,4*GRID),lambda i:(i,0,0)),pl.BlockSpec((1,2,4*BLK),lambda i:(i,0,0)),
          pl.BlockSpec((1,2,2*BLK),lambda i:(i,0,0)),pl.BlockSpec((t,t),lambda i:(0,0))],
        out_specs=[pl.BlockSpec((t,2*HEAD),lambda i:(0,i)),pl.BlockSpec((2,t,t),lambda i:(i,0,0))],
        out_shape=[jax.ShapeDtypeStruct((t,HEADS*HEAD),bf),jax.ShapeDtypeStruct((HEADS,t,t),f4)],
        compiler_params=pltpu.CompilerParams(vmem_limit_bytes=48<<20),
        cost_estimate=pl.CostEstimate(flops=7_000_000_000,bytes_accessed=24_000_000,transcendentals=4_200_000),
        name="attend_forward")(qkv,qkv,qkv,oh,ff,w,far,mask)

def bwd(qkv,g,oh,oht,p,lo,n):
    t=qkv.shape[0]; pairs=HEADS//2
    col=lambda off: pl.BlockSpec((t,2*HEAD),lambda i,off=off:(0,off+lo+i))
    return pl.pallas_call(bwd_kernel,grid=(n,),
        in_specs=[col(0),col(pairs),col(2*pairs),col(0),pl.BlockSpec((t,2*GRID),lambda i:(0,0)),pl.BlockSpec((2*GRID,t),lambda i:(0,0)),
          pl.BlockSpec((2,t,t),lambda i:(lo+i,0,0))],
        out_specs=[pl.BlockSpec((3,t,2*HEAD),lambda i:(0,0,i)),pl.BlockSpec((1,2,6*BLK),lambda i:(i,0,0)),pl.BlockSpec((1,4,2*GRID),lambda i:(i,0,0))],
        out_shape=[jax.ShapeDtypeStruct((3,t,2*HEAD*n),bf),jax.ShapeDtypeStruct((n,2,6*BLK),f4),jax.ShapeDtypeStruct((n,4,2*GRID),f4)],
        scratch_shapes=[pltpu.VMEM((t,t),bf),pltpu.VMEM((t,t),bf)],
        compiler_params=pltpu.CompilerParams(vmem_limit_bytes=48<<20),
        cost_estimate=pl.CostEstimate(flops=9_000_000_000*n//8,bytes_accessed=24_000_000*n//8,transcendentals=0),
        name="attend_backward")(qkv,qkv,qkv,g,oh,oht,p)

HI=lax.Precision.HIGHEST
def hot(n):
    return (np_bucket(n)[None,:]==np.arange(32)[:,None]).astype(np.float32)
N_GRID=(np.arange(GRID)[:,None]-np.arange(GRID)[None,:]).reshape(-1)
_m=np.arange(512); N_BAND=128-np.where(_m>=385,_m-512,_m)
def tables(rel,lay):
    w=jnp.einsum("bh,bn->hn",rel,jnp.asarray(hot(N_BAND)),precision=HI).reshape(8,2,512)
    far=jnp.concatenate([jnp.broadcast_to(rel[15][:,None],(16,128)),jnp.broadcast_to(rel[31][:,None],(16,128))],1).reshape(8,2,256)
    f=[jnp.einsum("bh,bn->hn",lay[32*i:32*i+32],jnp.asarray(hot(N_GRID)),precision=HI).reshape(16,64,64) for i in range(2)]
    z=jnp.zeros((16,64,64),f4)
    full=jnp.concatenate([jnp.concatenate([f[0],z],2),jnp.concatenate([z,f[1]],2)],1)
    hi=full.astype(bf)
    hi32=lax.reduce_precision(full,8,7)
    lo=(full-hi32).astype(bf)
    return w,far,jnp.concatenate([hi,lo],2)
def table_grads(relsum,laysum):
    rs=relsum.reshape(16,768); ls=laysum.reshape(16,2,128)
    oh=hot(N_BAND); oh[:,384]=0
    e15=np.zeros((32,128),np.float32); e15[15]=1
    e31=np.zeros((32,128),np.float32); e31[31]=1
    C=np.concatenate([oh,e15,e31],1)
    grel=jnp.einsum("bn,hn->bh",jnp.asarray(C),rs,precision=HI)
    m=np.arange(128); nn=63-m
    oh2=hot(nn); oh2[:,127]=0
    glay=jnp.einsum("bn,hxn->xbh",jnp.asarray(oh2),ls,precision=HI).reshape(64,16)
    return grel,glay

epsilon = 1e-06
masked_score = -1e30
AXES = ("wide", "narrow")


def devices_of(mesh):
    return mesh.shape["wide"] * mesh.shape["narrow"]


class Cube:
    def __init__(self, mesh):
        self.n = devices_of(mesh)
        self.bits = self.n.bit_length() - 1
        self.per_wide = mesh.shape["narrow"]
        far = list(range(self.bits - 1, 2, -1))
        self.gather_orders = (far + [1, 2, 0], far + [2, 1, 0])
        self.scatter_orders = ([0, 2, 1] + far[::-1], [0, 1, 2] + far[::-1])

    def me(self):
        return (lax.axis_index("wide") * self.per_wide + lax.axis_index("narrow")).astype(jnp.int32)

    def swap(self, x, b):
        return lax.ppermute(x, AXES, [(i, i ^ (1 << b)) for i in range(self.n)])

    def gather(self, own, order):
        cur, rel = own[None], [0]
        for b in order[:-1]:
            cur = jnp.concatenate([cur, self.swap(cur, b)], 0)
            rel = rel + [d ^ (1 << b) for d in rel]
        b = order[-1]
        return [(cur, rel), (self.swap(cur, b), [d ^ (1 << b) for d in rel])]

    def gather_both(self, own):
        half = own.shape[1] // 2
        return [
            self.gather(own[:, :half], self.gather_orders[0]),
            self.gather(own[:, half:], self.gather_orders[1]),
        ]

    def assemble(self, parts):
        flat, plan, col = [], [], 0
        for pieces in parts:
            for arr, rel in pieces:
                plan.append((len(flat), rel, col, arr.shape[2]))
                flat.append(arr)
            col += pieces[0][0].shape[2]
        r = flat[0].shape[1]
        count = sum(len(p[1]) for p in plan)

        def kernel(me_ref, *refs):
            out, sem = refs[len(flat)], refs[len(flat) + 1]
            copies = []
            for at, rel, c0, w in plan:
                for j, d in enumerate(rel):
                    copies.append(
                        pltpu.make_async_copy(
                            refs[at].at[j],
                            out.at[me_ref[0] ^ d, :, pl.ds(c0, w)],
                            sem.at[len(copies)],
                        )
                    )
            for c in copies:
                c.start()
            for c in copies:
                c.wait()

        out = pl.pallas_call(
            kernel,
            grid_spec=pltpu.PrefetchScalarGridSpec(
                num_scalar_prefetch=1,
                grid=(1,),
                in_specs=[pl.BlockSpec(memory_space=pl.ANY)] * len(flat),
                out_specs=pl.BlockSpec((self.n, r, col), lambda i, m: (0, 0, 0)),
                scratch_shapes=[pltpu.SemaphoreType.DMA((count,))],
            ),
            out_shape=jax.ShapeDtypeStruct((self.n, r, col), flat[0].dtype),
            compiler_params=pltpu.CompilerParams(vmem_limit_bytes=56 << 20),
            cost_estimate=pl.CostEstimate(flops=0, bytes_accessed=4 * self.n * r * col, transcendentals=0),
            name="assemble",
        )(self.me()[None], *flat)
        return out.reshape(self.n * r, col)

    def scatter(self, terms, order):
        r, c = terms.shape[1:]
        me = self.me()
        cur = terms.reshape((2,) * self.bits + (r, c))
        left = list(range(self.bits - 1, -1, -1))
        for b in order:
            axis = left.index(b)
            bit = (me >> b) & 1
            send = lax.dynamic_index_in_dim(cur, 1 - bit, axis, keepdims=False).astype(bf)
            keep = lax.dynamic_index_in_dim(cur, bit, axis, keepdims=False)
            cur = keep.astype(f4) + self.swap(send, b).astype(f4)
            left.remove(b)
        return cur

    def scatter_both(self, terms):
        g = terms.reshape(self.n, -1, terms.shape[1])
        half = g.shape[2] // 2
        return jnp.concatenate(
            [
                self.scatter(g[:, :, :half], self.scatter_orders[0]),
                self.scatter(g[:, :, half:], self.scatter_orders[1]),
            ],
            axis=1,
        )

    def all_sum(self, x):
        for b in range(self.bits):
            x = x + self.swap(x, b)
        return x


def rms_norm(values, gains):
    factor = lax.rsqrt(jnp.mean(values * values, axis=-1, keepdims=True) + epsilon)
    return values * factor * gains


def gelu_tanh(values):
    return jax.nn.gelu(values, approximate=True)


def make_body(cube):
    def body(
        tokens, gain_one, query_weight, key_weight, value_weight, out_weight, gain_two, gate_weight,
        up_weight, down_weight, relative_bias_table, layout_bias_table, doc_lengths, box_x, box_y, cotangent,
    ):
        row_count = tokens.shape[0]
        g_qkv = cube.gather_both(jnp.concatenate([query_weight, key_weight, value_weight], 1))
        g_out = cube.gather_both(out_weight)
        g_gu = cube.gather_both(jnp.concatenate([gate_weight, up_weight], 1))
        g_down = cube.gather_both(down_weight)

        positions = jnp.arange(row_count, dtype=jnp.int32)
        slots = jnp.arange(doc_lengths.shape[1], dtype=jnp.int32)
        doc_ends = jnp.sum(jnp.where(slots[:, None] <= slots[None, :], doc_lengths[0][:, None], 0), axis=0)
        live_rows = positions < doc_ends[-1]
        doc_ids = jnp.sum((positions[:, None] >= doc_ends[None, :]).astype(jnp.int32), axis=1)
        seg_ids = jnp.where(live_rows, doc_ids, doc_lengths.shape[1] + positions)
        live_mask = live_rows.astype(f4)[:, None]
        mask = jnp.where(seg_ids[:, None] == seg_ids[None, :], 0.0, masked_score).astype(f4)
        levels = jnp.arange(GRID, dtype=jnp.int32)
        hots = jnp.concatenate([box_x[:, None] == levels, box_y[:, None] == levels], 1).astype(bf)
        down_hots = jnp.concatenate(
            [box_x[None] == levels[::-1, None], box_y[None] == levels[::-1, None]], 0
        ).astype(bf)
        bands, far, values = tables(relative_bias_table, layout_bias_table)

        inputs_wide = tokens.astype(f4)
        normed_wide, norm_one_back = jax.vjp(rms_norm, inputs_wide, gain_one)
        normed = normed_wide.astype(bf)
        qkv_full = cube.assemble(g_qkv)
        qkv = jnp.dot(normed, qkv_full, preferred_element_type=f4).astype(bf)
        attended, probs = fwd(qkv, hots, values, bands, far, mask)
        out_full = cube.assemble(g_out)
        branch = jnp.dot(attended, out_full, preferred_element_type=f4)
        hidden = inputs_wide + live_mask * branch
        normed_two_wide, norm_two_back = jax.vjp(rms_norm, hidden, gain_two)
        normed_two = normed_two_wide.astype(bf)
        gu_full = cube.assemble(g_gu)
        gu = jnp.dot(normed_two, gu_full, preferred_element_type=f4)
        ff = gate_weight.shape[1]
        gate_rows, up_rows = gu[:, :ff], gu[:, ff:]
        gelu_gate, gelu_back = jax.vjp(gelu_tanh, gate_rows)
        inner_rows = (gelu_gate * up_rows).astype(bf)
        down_full = cube.assemble(g_down)
        ffn_rows = jnp.dot(inner_rows, down_full, preferred_element_type=f4)
        block_out = (hidden + live_mask * ffn_rows).astype(bf)

        grad_output = cotangent.astype(f4)
        grad_ffn = (live_mask * grad_output).astype(bf)
        grad_inner = jnp.einsum("td,fd->tf", grad_ffn, down_full, preferred_element_type=f4)
        grad_down_weight = jnp.einsum("tf,td->fd", inner_rows, grad_ffn, preferred_element_type=f4).astype(bf)
        grad_gate = gelu_back(grad_inner * up_rows)[0].astype(bf)
        grad_up = (grad_inner * gelu_gate).astype(bf)
        grad_gu = jnp.concatenate([grad_gate, grad_up], 1)
        grad_gu_weight = jnp.einsum("td,tf->df", normed_two, grad_gu, preferred_element_type=f4).astype(bf)
        share_gu = cube.scatter_both(grad_gu_weight)
        share_down = cube.scatter_both(grad_down_weight)
        grad_normed_two = jnp.einsum("tf,df->td", grad_gu, gu_full, preferred_element_type=f4)
        grad_hidden_part, grad_gain_two = norm_two_back(grad_normed_two)
        grad_hidden = grad_output + grad_hidden_part
        grad_branch = (live_mask * grad_hidden).astype(bf)
        grad_attended = jnp.einsum("td,ed->te", grad_branch, out_full, preferred_element_type=f4).astype(bf)
        grad_out_weight = jnp.einsum("te,td->ed", attended, grad_branch, preferred_element_type=f4).astype(bf)
        share_out = cube.scatter_both(grad_out_weight)

        grads, rel_sums, lay_sums = bwd(qkv, grad_attended, hots, down_hots, probs, 0, HEADS // 2)
        grad_rel_table, grad_layout_table = table_grads(rel_sums, lay_sums)
        grad_qkv = jnp.concatenate([grads[0], grads[1], grads[2]], 1)
        grad_qkv_weight = jnp.einsum("td,te->de", normed, grad_qkv, preferred_element_type=f4).astype(bf)
        share_qkv = cube.scatter_both(grad_qkv_weight)
        grad_normed = jnp.einsum("te,de->td", grad_qkv, qkv_full, preferred_element_type=f4)
        grad_input_part, grad_gain_one = norm_one_back(grad_normed)
        grad_tokens = grad_hidden + grad_input_part
        d = tokens.shape[1]
        small = cube.all_sum(
            jnp.concatenate(
                [grad_gain_one, grad_gain_two, grad_rel_table.reshape(-1), grad_layout_table.reshape(-1)]
            ).reshape(-1, 128)
        ).reshape(-1)
        rel_n, lay_n = relative_bias_table.size, layout_bias_table.size
        return (
            block_out,
            grad_tokens,
            small[:d],
            share_qkv[:, :d],
            share_qkv[:, d : 2 * d],
            share_qkv[:, 2 * d :],
            share_out,
            small[d : 2 * d],
            share_gu[:, :ff],
            share_gu[:, ff:],
            share_down,
            small[2 * d : 2 * d + rel_n].reshape(relative_bias_table.shape),
            small[2 * d + rel_n : 2 * d + rel_n + lay_n].reshape(layout_bias_table.shape),
        )

    return body


def solution(mesh):
    rows = P(AXES, None)
    line = P(AXES)
    whole = P()
    return jax.shard_map(
        make_body(Cube(mesh)),
        mesh=mesh,
        in_specs=(
            rows, whole, rows, rows, rows, rows, whole, rows, rows, rows, whole, whole, rows, line, line, rows,
        ),
        out_specs=(
            rows, rows, whole, rows, rows, rows, rows, whole, rows, rows, rows, whole, whole,
        ),
        check_vma=False,
    )
```

```python
import numpy as np
import jax
import jax.numpy as jnp
from jax import lax
from jax.experimental import pallas as pl
from jax.experimental.pallas import tpu as pltpu
from jax.sharding import PartitionSpec as P

bf = jnp.bfloat16
f4 = jnp.float32

HEADS,HEAD=16,64
bucket_edges=(1,2,3,4,5,6,7,8,12,16,23,32,46,64,91)
GRID=64
def np_bucket(n):
    n=np.asarray(n); m=np.abs(n)
    b=np.zeros(n.shape,np.int32)
    for e in bucket_edges: b+=(m>=e)
    return b+(n>0)*16
BLK=128
NT=(((1,),(1,)),((),()))
NN=(((1,),(0,)),((),()))
def dot(a,b,dims=NN): return lax.dot_general(a,b,dims,preferred_element_type=f4)

def fwd_kernel(q_ref,k_ref,v_ref,oh_ref,ff_ref,w_ref,far_ref,mask_ref,o_ref,p_ref):
    t=q_ref.shape[0]; nb=t//BLK
    lane=lax.broadcasted_iota(jnp.int32,(t,2*HEAD),1)
    q=q_ref[...]; oh=oh_ref[...]; v=v_ref[...]
    oht=oh.T; ka=jnp.concatenate([k_ref[...].T,oht,oht],axis=0)
    for j in range(2):
        mine=(lane<HEAD) if j==0 else (lane>=HEAD)
        band=pltpu.roll(jnp.broadcast_to(w_ref[0,j:j+1,:],(BLK,4*BLK)),0,1,stride=1,stride_axis=0)
        near=far_ref[0,j:j+1,0:BLK]; past=far_ref[0,j:j+1,BLK:2*BLK]
        rows=dot(oh,ff_ref[j]).astype(bf)
        qa=jnp.concatenate([jnp.where(mine,q,jnp.zeros_like(q)),rows],axis=1)
        whole=dot(qa,ka)
        for s in range(nb):
            sc=whole[s*BLK:(s+1)*BLK]
            rel=[]
            for c in range(nb):
                if c<s-1: rel.append(jnp.broadcast_to(past,(BLK,BLK)))
                elif c>s+1: rel.append(jnp.broadcast_to(near,(BLK,BLK)))
                else: rel.append(band[:,(c-s+1)*BLK:(c-s+2)*BLK])
            sc=(sc+jnp.concatenate(rel,axis=1))+mask_ref[s*BLK:(s+1)*BLK,:]
            top=jnp.max(sc,axis=1,keepdims=True)
            e=jnp.exp(sc-top)
            p=e*(1.0/jnp.sum(e,axis=1,keepdims=True))
            p_ref[j,s*BLK:(s+1)*BLK,:]=p
            o=dot(p.astype(bf),v).astype(bf)
            o_ref[s*BLK:(s+1)*BLK,j*HEAD:(j+1)*HEAD]=o[:,j*HEAD:(j+1)*HEAD]

def bwd_kernel(q_ref,k_ref,v_ref,g_ref,oh_ref,oht_ref,p_ref,d_ref,rel_ref,lay_ref,ds_s,pb_s):
    t=q_ref.shape[0]; nb=t//BLK
    lane=lax.broadcasted_iota(jnp.int32,(t,2*HEAD),1)
    q=q_ref[...]; k=k_ref[...]; v=v_ref[...]; g=g_ref[...]; oh=oh_ref[...]
    koh=jnp.concatenate([k,oh],axis=1)
    qt=q.T; gt=g.T; vt=v.T
    outs=[]
    for j in range(2):
        mine=(lane<HEAD) if j==0 else (lane>=HEAD)
        gm=jnp.where(mine,g,jnp.zeros_like(g))
        band=[jnp.zeros((BLK,BLK),f4) for _ in range(3)]
        past=jnp.zeros((BLK,BLK),f4); near=jnp.zeros((BLK,BLK),f4)
        whole=dot(gm,vt)
        for s in range(nb):
            rows=slice(s*BLK,(s+1)*BLK)
            dp=whole[rows]
            p=p_ref[j,rows,:]
            ds=p*(dp-jnp.sum(p*dp,axis=1,keepdims=True))
            for c in range(nb):
                tile=ds[:,c*BLK:(c+1)*BLK]
                if c<s-1: past=past+tile
                elif c>s+1: near=near+tile
                else: band[c-s+1]=band[c-s+1]+tile
            dsb=ds.astype(bf)
            ds_s[rows,:]=dsb; pb_s[rows,:]=p.astype(bf)
        dq=dot(ds_s[...],koh)
        dkt=dot(qt,ds_s[...]); dvt=dot(gt,pb_s[...])
        outs.append((dq[:,:2*HEAD],dkt,dvt))
        r=dq[:,2*HEAD:]
        hi=r.astype(bf); lo=(r-hi.astype(f4)).astype(bf)
        gl=dot(oht_ref[...],jnp.concatenate([hi,lo],axis=1))
        gl=gl[:,:2*GRID]+gl[:,2*GRID:]
        for i in range(2):
            part=gl[i*GRID:(i+1)*GRID,i*GRID:(i+1)*GRID]
            part=pltpu.roll(jnp.concatenate([part,jnp.zeros((GRID,GRID),f4)],axis=1),0,1,stride=1,stride_axis=0)
            lay_ref[0,2*j+i:2*j+i+1,:]=jnp.sum(part,axis=0,keepdims=True)
        wide=jnp.concatenate(band+[jnp.zeros((BLK,BLK),f4)],axis=1)
        acc=wide[0:8]
        for i in range(1,BLK//8):
            acc=acc+pltpu.roll(wide[8*i:8*i+8],4*BLK-8*i,1)
        line=acc[0:1]
        for i in range(1,8):
            line=line+pltpu.roll(acc[i:i+1],4*BLK-i,1)
        rel_ref[0,j:j+1,0:4*BLK]=line
        rel_ref[0,j:j+1,4*BLK:5*BLK]=jnp.sum(near,axis=0,keepdims=True)
        rel_ref[0,j:j+1,5*BLK:6*BLK]=jnp.sum(past,axis=0,keepdims=True)
    d_ref[0]=jnp.where(lane<HEAD,outs[0][0],outs[1][0]).astype(bf)
    sub=lax.broadcasted_iota(jnp.int32,(2*HEAD,t),0)
    d_ref[1]=jnp.where(sub<HEAD,outs[0][1],outs[1][1]).astype(bf).T
    d_ref[2]=jnp.where(sub<HEAD,outs[0][2],outs[1][2]).astype(bf).T

def fwd(qkv,oh,ff,w,far,mask,lo,n):
    t=qkv.shape[0]; pairs=HEADS//2
    col=lambda off: pl.BlockSpec((t,2*HEAD),lambda i,off=off:(0,off+lo+i))
    return pl.pallas_call(fwd_kernel,grid=(n,),
        in_specs=[col(0),col(pairs),col(2*pairs),pl.BlockSpec((t,2*GRID),lambda i:(0,0)),
          pl.BlockSpec((2,2*GRID,4*GRID),lambda i:(lo+i,0,0)),pl.BlockSpec((1,2,4*BLK),lambda i:(lo+i,0,0)),
          pl.BlockSpec((1,2,2*BLK),lambda i:(lo+i,0,0)),pl.BlockSpec((t,t),lambda i:(0,0))],
        out_specs=[pl.BlockSpec((t,2*HEAD),lambda i:(0,i)),pl.BlockSpec((2,t,t),lambda i:(i,0,0))],
        out_shape=[jax.ShapeDtypeStruct((t,2*HEAD*n),bf),jax.ShapeDtypeStruct((2*n,t,t),f4)],
        compiler_params=pltpu.CompilerParams(vmem_limit_bytes=48<<20),
        cost_estimate=pl.CostEstimate(flops=7_000_000_000*n//8,bytes_accessed=24_000_000*n//8,transcendentals=4_200_000*n//8),
        name="attend_forward")(qkv,qkv,qkv,oh,ff,w,far,mask)

def bwd(qkv,g,oh,oht,p,lo,n):
    t=qkv.shape[0]; pairs=HEADS//2
    col=lambda off: pl.BlockSpec((t,2*HEAD),lambda i,off=off:(0,off+lo+i))
    return pl.pallas_call(bwd_kernel,grid=(n,),
        in_specs=[col(0),col(pairs),col(2*pairs),col(0),pl.BlockSpec((t,2*GRID),lambda i:(0,0)),pl.BlockSpec((2*GRID,t),lambda i:(0,0)),
          pl.BlockSpec((2,t,t),lambda i:(i,0,0))],
        out_specs=[pl.BlockSpec((3,t,2*HEAD),lambda i:(0,0,i)),pl.BlockSpec((1,2,6*BLK),lambda i:(i,0,0)),pl.BlockSpec((1,4,2*GRID),lambda i:(i,0,0))],
        out_shape=[jax.ShapeDtypeStruct((3,t,2*HEAD*n),bf),jax.ShapeDtypeStruct((n,2,6*BLK),f4),jax.ShapeDtypeStruct((n,4,2*GRID),f4)],
        scratch_shapes=[pltpu.VMEM((t,t),bf),pltpu.VMEM((t,t),bf)],
        compiler_params=pltpu.CompilerParams(vmem_limit_bytes=48<<20),
        cost_estimate=pl.CostEstimate(flops=9_000_000_000*n//8,bytes_accessed=24_000_000*n//8,transcendentals=0),
        name="attend_backward")(qkv,qkv,qkv,g,oh,oht,p)

HI=lax.Precision.HIGHEST
def hot(n):
    return (np_bucket(n)[None,:]==np.arange(32)[:,None]).astype(np.float32)
N_GRID=(np.arange(GRID)[:,None]-np.arange(GRID)[None,:]).reshape(-1)
_m=np.arange(512); N_BAND=128-np.where(_m>=385,_m-512,_m)
def tables(rel,lay):
    w=jnp.einsum("bh,bn->hn",rel,jnp.asarray(hot(N_BAND)),precision=HI).reshape(8,2,512)
    far=jnp.concatenate([jnp.broadcast_to(rel[15][:,None],(16,128)),jnp.broadcast_to(rel[31][:,None],(16,128))],1).reshape(8,2,256)
    f=[jnp.einsum("bh,bn->hn",lay[32*i:32*i+32],jnp.asarray(hot(N_GRID)),precision=HI).reshape(16,64,64) for i in range(2)]
    z=jnp.zeros((16,64,64),f4)
    full=jnp.concatenate([jnp.concatenate([f[0],z],2),jnp.concatenate([z,f[1]],2)],1)
    hi=full.astype(bf)
    hi32=lax.reduce_precision(full,8,7)
    lo=(full-hi32).astype(bf)
    return w,far,jnp.concatenate([hi,lo],2)
def table_grads(relsum,laysum):
    rs=relsum.reshape(16,768); ls=laysum.reshape(16,2,128)
    oh=hot(N_BAND); oh[:,384]=0
    e15=np.zeros((32,128),np.float32); e15[15]=1
    e31=np.zeros((32,128),np.float32); e31[31]=1
    C=np.concatenate([oh,e15,e31],1)
    grel=jnp.einsum("bn,hn->bh",jnp.asarray(C),rs,precision=HI)
    m=np.arange(128); nn=63-m
    oh2=hot(nn); oh2[:,127]=0
    glay=jnp.einsum("bn,hxn->xbh",jnp.asarray(oh2),ls,precision=HI).reshape(64,16)
    return grel,glay

epsilon = 1e-06
masked_score = -1e30
AXES = ("wide", "narrow")
VMEM_LIMIT = 58 << 20


def tie(values, *after):
    return lax.optimization_barrier((values, after))[0]


class Cube:
    def __init__(self, mesh):
        self.n = mesh.shape["wide"] * mesh.shape["narrow"]
        self.bits = self.n.bit_length() - 1
        self.per_wide = mesh.shape["narrow"]
        self.far = self.n // 8

    def me(self):
        return (lax.axis_index("wide") * self.per_wide + lax.axis_index("narrow")).astype(jnp.int32)

    def swap(self, x, mask):
        return lax.ppermute(x, AXES, [(i, i ^ mask) for i in range(self.n)])

    def far_swaps(self, own):
        return [own] + [self.swap(own, f * 8) for f in range(1, self.far)]

    def halves(self, blocks):
        half = blocks[0].shape[1] // 2
        return [jnp.stack([x[:, :half] for x in blocks]), jnp.stack([x[:, half:] for x in blocks])]

    def step_a(self, pair):
        return [self.swap(pair[0], 2), self.swap(pair[1], 4)]

    def step_b(self, pair):
        return [self.swap(pair[0], 4), self.swap(pair[1], 2)]

    def joined(self, pair, got):
        return [jnp.concatenate([x, g], 0) for x, g in zip(pair, got)]

    def step_core(self, pair, got):
        return [[self.swap(x, 1), self.swap(g, 1)] for x, g in zip(pair, got)]

    def pieces(self, pair, got, cores):
        out = []
        for x, g, (cx, cg), (ma, mb) in zip(pair, got, cores, ((2, 4), (4, 2))):
            rel = [f * 8 for f in range(self.far)]
            rel = rel + [d ^ ma for d in rel]
            more = [d ^ mb for d in rel]
            out.append([(x, rel), (g, more), (cx, [d ^ 1 for d in rel]), (cg, [d ^ 1 for d in more])])
        return out

    def plan(self, parts, bands):
        flat, steps, col = [], [], 0
        for pieces in parts:
            mine = []
            for arr, rel in pieces:
                for j, d in enumerate(rel):
                    for k, (r0, r) in enumerate(bands):
                        mine.append((len(flat), j, d, r0, r, k, col, arr.shape[2]))
                flat.append(arr)
            col += pieces[0][0].shape[2]
            steps.append(mine)
        return flat, steps, col

    def assemble(self, parts, bands):
        flat, steps, col = self.plan(parts, bands)
        count = sum(len(x) for x in steps)

        def kernel(me_ref, *refs):
            outs, sem = refs[len(flat) : len(flat) + len(bands)], refs[-1]
            copies = []
            for at, j, d, r0, r, k, c0, w in [x for mine in steps for x in mine]:
                copies.append(
                    pltpu.make_async_copy(
                        refs[at].at[j, pl.ds(r0, r)],
                        outs[k].at[me_ref[0] ^ d, :, pl.ds(c0, w)],
                        sem.at[len(copies)],
                    )
                )
            for c in copies:
                c.start()
            for c in copies:
                c.wait()

        outs = pl.pallas_call(
            kernel,
            grid_spec=pltpu.PrefetchScalarGridSpec(
                num_scalar_prefetch=1,
                grid=(1,),
                in_specs=[pl.BlockSpec(memory_space=pl.ANY)] * len(flat),
                out_specs=[pl.BlockSpec((self.n, r, col), lambda i, m: (0, 0, 0)) for _, r in bands],
                scratch_shapes=[pltpu.SemaphoreType.DMA((count,))],
            ),
            out_shape=[jax.ShapeDtypeStruct((self.n, r, col), bf) for _, r in bands],
            compiler_params=pltpu.CompilerParams(vmem_limit_bytes=VMEM_LIMIT),
            cost_estimate=pl.CostEstimate(
                flops=0, bytes_accessed=4 * self.n * col * sum(r for _, r in bands), transcendentals=0
            ),
            name="assemble",
        )(self.me()[None], *flat)
        return [o.reshape(-1, col) for o in outs]

    def project(self, x, parts):
        r = parts[0][0][0].shape[1]
        t, d = x.shape
        if r % 16:
            [whole] = self.assemble(parts, [(0, r)])
            return jnp.dot(x, whole, preferred_element_type=f4).astype(bf), whole
        flat, steps, col = self.plan(parts, [(0, r)])
        count = sum(len(m) for m in steps)
        tile = 512

        def kernel(me_ref, x_ref, *refs):
            y_ref, w_ref, held, sem, out_sem = refs[len(flat) :]
            todo, k = [], 0
            for mine in steps:
                copies = []
                for at, j, d_, _, _, _, c0, w in mine:
                    copies.append(
                        pltpu.make_async_copy(
                            refs[at].at[j], held.at[me_ref[0] ^ d_, :, pl.ds(c0, w)], sem.at[k]
                        )
                    )
                    k += 1
                for c in copies:
                    c.start()
                todo.append(copies)
            writes = []
            for mine, copies in zip(steps, todo):
                c0, w = mine[0][6], mine[0][7]
                for c in copies:
                    c.wait()
                write = pltpu.make_async_copy(
                    held.at[:, :, pl.ds(c0, w)], w_ref.at[:, :, pl.ds(c0, w)], out_sem.at[len(writes)]
                )
                write.start()
                writes.append(write)
                for c in range(c0, c0 + w, tile):
                    block = held[:, :, c : c + tile].reshape(d, tile)
                    y_ref[:, c : c + tile] = dot(x_ref[...], block).astype(bf)
            for write in writes:
                write.wait()

        y, whole = pl.pallas_call(
            kernel,
            grid_spec=pltpu.PrefetchScalarGridSpec(
                num_scalar_prefetch=1,
                grid=(1,),
                in_specs=[pl.BlockSpec((t, d), lambda i, m: (0, 0))]
                + [pl.BlockSpec(memory_space=pl.ANY)] * len(flat),
                out_specs=[pl.BlockSpec((t, col), lambda i, m: (0, 0)), pl.BlockSpec(memory_space=pl.ANY)],
                scratch_shapes=[
                    pltpu.VMEM((self.n, r, col), bf),
                    pltpu.SemaphoreType.DMA((count,)),
                    pltpu.SemaphoreType.DMA((len(steps),)),
                ],
            ),
            out_shape=[jax.ShapeDtypeStruct((t, col), bf), jax.ShapeDtypeStruct((self.n, r, col), bf)],
            compiler_params=pltpu.CompilerParams(vmem_limit_bytes=VMEM_LIMIT),
            cost_estimate=pl.CostEstimate(
                flops=2 * t * d * col, bytes_accessed=4 * d * col + 2 * t * (d + col), transcendentals=0
            ),
            name="project",
        )(self.me()[None], x, *flat)
        return y, whole.reshape(d, col)

    def gated(self, x, parts, grad_inner):
        r = parts[0][0][0].shape[1]
        t, d = x.shape
        ff = grad_inner.shape[1]
        if r % 16:
            [whole] = self.assemble(parts, [(0, r)])
            both = jnp.dot(x, whole, preferred_element_type=f4)
            inner, grad_gate, grad_up = gate_math(both[:, :ff], both[:, ff:], grad_inner)
            return inner, grad_gate, grad_up, whole
        flat, steps, col = self.plan(parts, [(0, r)])
        count = sum(len(m) for m in steps)
        tile = 256

        def kernel(me_ref, x_ref, g_ref, *refs):
            inner_ref, gate_ref, up_ref, w_ref, held, sem, out_sem = refs[len(flat) :]
            write = pltpu.make_async_copy(held, w_ref, out_sem.at[0])

            @pl.when(pl.program_id(0) == 0)
            def _():
                copies = []
                for at, j, d_, _, _, _, c0, w in [m for mine in steps for m in mine]:
                    copies.append(
                        pltpu.make_async_copy(
                            refs[at].at[j], held.at[me_ref[0] ^ d_, :, pl.ds(c0, w)], sem.at[len(copies)]
                        )
                    )
                for c in copies:
                    c.start()
                for c in copies:
                    c.wait()
                write.start()

            at = pl.multiple_of(pl.program_id(0) * tile, tile)
            x_ = x_ref[...]
            gate = dot(x_, held[:, :, pl.ds(at, tile)].reshape(d, tile))
            up = dot(x_, held[:, :, pl.ds(pl.multiple_of(ff + at, tile), tile)].reshape(d, tile))
            inner_ref[...], gate_ref[...], up_ref[...] = gate_math(gate, up, g_ref[...])

            @pl.when(pl.program_id(0) == pl.num_programs(0) - 1)
            def _():
                write.wait()

        block = pl.BlockSpec((t, tile), lambda i, m: (0, i))
        wide = jax.ShapeDtypeStruct((t, ff), bf)
        inner, grad_gate, grad_up, whole = pl.pallas_call(
            kernel,
            grid_spec=pltpu.PrefetchScalarGridSpec(
                num_scalar_prefetch=1,
                grid=(ff // tile,),
                in_specs=[pl.BlockSpec((t, d), lambda i, m: (0, 0)), block]
                + [pl.BlockSpec(memory_space=pl.ANY)] * len(flat),
                out_specs=[block, block, block, pl.BlockSpec(memory_space=pl.ANY)],
                scratch_shapes=[
                    pltpu.VMEM((self.n, r, col), bf),
                    pltpu.SemaphoreType.DMA((count,)),
                    pltpu.SemaphoreType.DMA((1,)),
                ],
            ),
            out_shape=[wide, wide, wide, jax.ShapeDtypeStruct((self.n, r, col), bf)],
            compiler_params=pltpu.CompilerParams(vmem_limit_bytes=VMEM_LIMIT),
            cost_estimate=pl.CostEstimate(
                flops=2 * t * d * col, bytes_accessed=4 * d * col + 14 * t * ff, transcendentals=t * ff
            ),
            name="gated",
        )(self.me()[None], x, grad_inner, *flat)
        return inner, grad_gate, grad_up, whole.reshape(d, col)

    def places(self, p):
        hi, lo = ((4, 2), (2, 4))[p]
        return [c + y * hi + x * lo + f * 8 for c in (0, 1) for y in (0, 1) for x in (0, 1) for f in range(self.far)]

    def terms(self, x, dy):
        t, rows = x.shape
        r, half = rows // self.n, dy.shape[1] // 2
        n = self.n
        if r % 8:
            g = jnp.einsum("tf,td->fd", x, dy, preferred_element_type=f4).astype(bf).reshape(n, r, -1)
            g = g.reshape((2,) * self.bits + g.shape[1:])
            for b in range(self.bits):
                g = jnp.where((self.me() >> b) & 1 == 1, jnp.flip(g, self.bits - 1 - b), g)
            last = self.bits - 1
            both = []
            for p, near in enumerate(((last - 2, last - 1), (last - 1, last - 2))):
                order = (last, *near, *range(last - 2), last + 1, last + 2)
                part = jnp.transpose(g[..., p * half : (p + 1) * half], order)
                both.append(part.reshape(n, r, half))
            both = jnp.stack(both)
            return both[:, n // 2 :], both[:, : n // 2]
        tile = max(c for c in range(128, half + 1, 128) if half % c == 0 and c * rows <= 1500000)
        chunk = 256

        def kernel(me_ref, x_ref, y_ref, send_ref, keep_ref, turned, acc):
            @pl.when((pl.program_id(0) == 0) & (pl.program_id(1) == 0))
            def _():
                for c in range(0, rows, chunk):
                    turned[c : c + chunk, :] = x_ref[:, c : c + chunk].T

            y_ = y_ref[...]
            for c in range(0, rows, chunk):
                acc[c : c + chunk, :] = dot(turned[c : c + chunk, :], y_)
            first = pl.program_id(0) == 0
            for at, (d0, d1) in enumerate(zip(self.places(0), self.places(1))):
                who = me_ref[0] ^ jnp.where(first, d0, d1)
                block = acc[pl.ds(pl.multiple_of(who * r, 8), r), :].astype(bf)
                if at < n // 2:
                    keep_ref[0, at] = block
                else:
                    send_ref[0, at - n // 2] = block

        per = half // tile
        out = pl.BlockSpec((1, n // 2, r, tile), lambda p, j, m: (p, 0, 0, j))
        shape = jax.ShapeDtypeStruct((2, n // 2, r, half), bf)
        return pl.pallas_call(
            kernel,
            grid_spec=pltpu.PrefetchScalarGridSpec(
                num_scalar_prefetch=1,
                grid=(2, per),
                in_specs=[
                    pl.BlockSpec((t, rows), lambda p, j, m: (0, 0)),
                    pl.BlockSpec((t, tile), lambda p, j, m: (0, p * per + j)),
                ],
                out_specs=[out, out],
                scratch_shapes=[pltpu.VMEM((rows, t), bf), pltpu.VMEM((rows, tile), f4)],
            ),
            out_shape=[shape, shape],
            compiler_params=pltpu.CompilerParams(vmem_limit_bytes=VMEM_LIMIT),
            cost_estimate=pl.CostEstimate(
                flops=4 * t * rows * half, bytes_accessed=2 * (t * rows + 2 * t * half + 2 * rows * half), transcendentals=0
            ),
            name="terms",
        )(self.me()[None], x, dy)

    def plus(self, a, b):
        return a.astype(f4) + b.astype(f4)

    def split_a(self, keep, got):
        h = self.n // 4
        sends = [self.plus(keep[p, h:], got[p, h:]).astype(bf) for p in range(2)]
        return sends, [self.plus(keep[p, :h], got[p, :h]).astype(bf) for p in range(2)]

    def send_a(self, sends):
        return [self.swap(sends[0], 4), self.swap(sends[1], 2)]

    def split_b(self, keeps, gots):
        h = self.n // 8
        sends = [self.plus(k[h:], g[h:]).astype(bf) for k, g in zip(keeps, gots)]
        return sends, [self.plus(k[:h], g[:h]) for k, g in zip(keeps, gots)]

    def send_b(self, sends):
        return [self.swap(sends[0], 2), self.swap(sends[1], 4)]

    def split_far(self, keeps, gots):
        both = lambda f: jnp.concatenate([self.plus(k[f], g[f]) for k, g in zip(keeps, gots)], -1)
        return [both(f).astype(bf) for f in range(1, self.far)], both(0)

    def send_far(self, sends):
        return [self.swap(x, 8 * (f + 1)) for f, x in enumerate(sends)]

    def total(self, own, gots):
        for g in gots:
            own = own + g.astype(f4)
        return own

    def all_sum(self, x):
        for b in range(self.bits):
            x = x + self.swap(x, 1 << b)
        return x


def rms_norm(values, gains):
    factor = lax.rsqrt(jnp.mean(values * values, axis=-1, keepdims=True) + epsilon)
    return values * factor * gains


def gate_math(gate, up, grad_inner):
    c = 0.7978845608028654
    square = gate * gate
    t = jnp.tanh(c * gate * (1.0 + 0.044715 * square))
    half = 0.5 * (1.0 + t)
    act = gate * half
    slope = half + 0.5 * gate * (1.0 - t * t) * (c * (1.0 + 3.0 * 0.044715 * square))
    return (act * up).astype(bf), (grad_inner * up * slope).astype(bf), (grad_inner * act).astype(bf)


def make_body(cube):
    def body(
        tokens, gain_one, query_weight, key_weight, value_weight, out_weight, gain_two, gate_weight,
        up_weight, down_weight, relative_bias_table, layout_bias_table, doc_lengths, box_x, box_y, cotangent,
    ):
        row_count, d = tokens.shape
        half_pairs = HEADS // 4
        own1 = jnp.concatenate([query_weight, key_weight, value_weight], 1)
        far1 = cube.far_swaps(own1)

        positions = jnp.arange(row_count, dtype=jnp.int32)
        slots = jnp.arange(doc_lengths.shape[1], dtype=jnp.int32)
        doc_ends = jnp.sum(jnp.where(slots[:, None] <= slots[None, :], doc_lengths[0][:, None], 0), axis=0)
        live_rows = positions < doc_ends[-1]
        doc_ids = jnp.sum((positions[:, None] >= doc_ends[None, :]).astype(jnp.int32), axis=1)
        seg_ids = jnp.where(live_rows, doc_ids, doc_lengths.shape[1] + positions)
        live_mask = live_rows.astype(f4)[:, None]
        mask = jnp.where(seg_ids[:, None] == seg_ids[None, :], 0.0, masked_score).astype(f4)
        levels = jnp.arange(GRID, dtype=jnp.int32)
        hots = jnp.concatenate([box_x[:, None] == levels, box_y[:, None] == levels], 1).astype(bf)
        down_hots = jnp.concatenate(
            [box_x[None] == levels[::-1, None], box_y[None] == levels[::-1, None]], 0
        ).astype(bf)
        bands, far, values = tables(relative_bias_table, layout_bias_table)
        inputs_wide = tokens.astype(f4)
        normed_wide, norm_one_back = jax.vjp(rms_norm, inputs_wide, gain_one)
        normed = normed_wide.astype(bf)
        grad_output = cotangent.astype(f4)
        grad_ffn = (live_mask * grad_output).astype(bf)

        far1, normed, mask, hots, down_hots, bands, far, values, grad_ffn = tie(
            (far1, normed, mask, hots, down_hots, bands, far, values, grad_ffn)
        )
        pair1 = cube.halves(far1)
        out_weight_, down_weight_, gate_weight_, up_weight_ = tie(
            (out_weight, down_weight, gate_weight, up_weight), pair1
        )
        got1 = cube.step_a(pair1)
        far_o = cube.far_swaps(out_weight_)
        got1, far_o, down_weight_, gate_weight_, up_weight_ = tie((got1, far_o, down_weight_, gate_weight_, up_weight_))
        pair1 = cube.joined(pair1, got1)
        down_weight_, gate_weight_, up_weight_ = tie((down_weight_, gate_weight_, up_weight_), pair1)
        got1 = cube.step_b(pair1)
        far_d = cube.far_swaps(down_weight_)
        got1, far_o, far_d, gate_weight_, up_weight_ = tie((got1, far_o, far_d, gate_weight_, up_weight_))
        core1 = cube.step_core(pair1, got1)
        pair2 = cube.halves([jnp.concatenate([o, x], 0) for o, x in zip(far_o, far_d)])
        gate_weight_, up_weight_ = tie((gate_weight_, up_weight_), pair2)
        got2 = cube.step_a(pair2)
        far_g = cube.far_swaps(gate_weight_)
        core1, got2, far_g, up_weight_ = tie((core1, got2, far_g, up_weight_))
        pair2 = cube.joined(pair2, got2)
        normed_, up_weight_ = tie((normed, up_weight_), pair2)
        got2 = cube.step_b(pair2)
        far_u = cube.far_swaps(up_weight_)
        qkv, qkv_full = cube.project(normed_, cube.pieces(pair1, got1, core1))
        attended_a, probs_a = fwd(qkv, hots, values, bands, far, mask, 0, half_pairs)
        got2, far_u, attended_a = tie((got2, far_u, attended_a))
        core2 = cube.step_core(pair2, got2)
        pair3 = [jnp.stack(far_g), jnp.stack(far_u)]
        qkv_ = tie(qkv, pair3, attended_a)
        got3 = cube.step_a(pair3)
        attended_b, probs_b = fwd(qkv_, hots, values, bands, far, mask, half_pairs, half_pairs)
        core2, got3, attended_b = tie((core2, got3, attended_b))
        pair3 = cube.joined(pair3, got3)
        attended_b = tie(attended_b, pair3)
        got3 = cube.step_b(pair3)
        out_rows = out_weight.shape[0]
        out_full, down_full = cube.assemble(
            cube.pieces(pair2, got2, core2), [(0, out_rows), (out_rows, down_weight.shape[0])]
        )
        attended = jnp.concatenate([attended_a, attended_b], 1)
        branch = jnp.dot(attended, out_full, preferred_element_type=f4)
        hidden = inputs_wide + live_mask * branch
        normed_two_wide, norm_two_back = jax.vjp(rms_norm, hidden, gain_two)
        normed_two = normed_two_wide.astype(bf)
        grad_inner = jnp.einsum("td,fd->tf", grad_ffn, down_full, preferred_element_type=f4)
        got3, normed_two, grad_inner = tie((got3, normed_two, grad_inner))
        core3 = cube.step_core(pair3, got3)
        inner_rows, grad_gate, grad_up, gu_full = cube.gated(normed_two, cube.pieces(pair3, got3, core3), grad_inner)
        ff = gate_weight.shape[1]

        send_d, keep_d = cube.terms(inner_rows, grad_ffn)
        got_d = cube.swap(send_d, 1)
        grad_gate_, normed_two_ = tie((grad_gate, normed_two), send_d)
        send_g, keep_g = cube.terms(normed_two_, grad_gate_)
        got_d, send_g, keep_g = tie((got_d, send_g, keep_g))
        got_g = cube.swap(send_g, 1)
        sends_d, keeps_d = cube.split_a(keep_d, got_d)
        got_d = cube.send_a(sends_d)
        grad_up_, normed_two_ = tie((grad_up, normed_two), sends_d, send_g)
        send_u, keep_u = cube.terms(normed_two_, grad_up_)
        grad_up_, gu_full_ = tie((grad_up, gu_full), send_u)
        grad_normed_two = jnp.einsum("tf,df->td", grad_gate, gu_full_[:, :ff], preferred_element_type=f4)
        got_d, got_g, send_u, keep_u, grad_normed_two = tie((got_d, got_g, send_u, keep_u, grad_normed_two))
        got_u = cube.swap(send_u, 1)
        sends_d, keeps_d = cube.split_b(keeps_d, got_d)
        got_d = cube.send_b(sends_d)
        sends_g, keeps_g = cube.split_a(keep_g, got_g)
        got_g = cube.send_a(sends_g)
        grad_up_, gu_full_, grad_normed_two = tie((grad_up_, gu_full_, grad_normed_two), sends_d, sends_g)
        grad_normed_two = grad_normed_two + jnp.einsum(
            "tf,df->td", grad_up_, gu_full_[:, ff:], preferred_element_type=f4
        )
        grad_hidden_part, grad_gain_two = norm_two_back(grad_normed_two)
        grad_hidden = grad_output + grad_hidden_part
        grad_branch = (live_mask * grad_hidden).astype(bf)
        grad_attended = jnp.einsum("td,ed->te", grad_branch, out_full, preferred_element_type=f4).astype(bf)
        got_d, got_g, got_u, grad_attended = tie((got_d, got_g, got_u, grad_attended))
        sends_d, own_d = cube.split_far(keeps_d, got_d)
        far_d = cube.send_far(sends_d)
        sends_g, keeps_g = cube.split_b(keeps_g, got_g)
        got_g = cube.send_b(sends_g)
        sends_u, keeps_u = cube.split_a(keep_u, got_u)
        got_u = cube.send_a(sends_u)
        grad_attended = tie(grad_attended, sends_d, sends_g, sends_u)
        grads_a, rel_a, lay_a = bwd(qkv, grad_attended, hots, down_hots, probs_a, 0, half_pairs)
        grads_b, rel_b, lay_b = bwd(qkv, grad_attended, hots, down_hots, probs_b, half_pairs, half_pairs)
        grad_qkv = jnp.concatenate([grads_a[0], grads_b[0], grads_a[1], grads_b[1], grads_a[2], grads_b[2]], 1)
        send_q, keep_q = cube.terms(normed, grad_qkv)
        far_d, got_g, got_u, send_q, keep_q = tie((far_d, got_g, got_u, send_q, keep_q))
        got_q = cube.swap(send_q, 1)
        share_down = cube.total(own_d, far_d)
        sends_g, own_g = cube.split_far(keeps_g, got_g)
        far_g = cube.send_far(sends_g)
        sends_u, keeps_u = cube.split_b(keeps_u, got_u)
        got_u = cube.send_b(sends_u)
        attended_, grad_branch_ = tie((attended, grad_branch), send_q, sends_u, sends_g)
        send_o, keep_o = cube.terms(attended_, grad_branch_)
        got_q, send_o, keep_o = tie((got_q, send_o, keep_o))
        got_o = cube.swap(send_o, 1)
        sends_q, keeps_q = cube.split_a(keep_q, got_q)
        got_q = cube.send_a(sends_q)
        grad_qkv = tie(grad_qkv, sends_q, send_o)
        grad_normed = jnp.einsum("te,de->td", grad_qkv, qkv_full, preferred_element_type=f4)
        grad_input_part, grad_gain_one = norm_one_back(grad_normed)
        grad_tokens = grad_hidden + grad_input_part
        far_g, got_u, got_q, got_o, grad_tokens, grad_gain_one = tie(
            (far_g, got_u, got_q, got_o, grad_tokens, grad_gain_one)
        )
        share_gate = cube.total(own_g, far_g)
        sends_u, own_u = cube.split_far(keeps_u, got_u)
        far_u = cube.send_far(sends_u)
        sends_q, keeps_q = cube.split_b(keeps_q, got_q)
        got_q = cube.send_b(sends_q)
        sends_o, keeps_o = cube.split_a(keep_o, got_o)
        got_o = cube.send_a(sends_o)
        inner_ = tie(inner_rows, sends_u, sends_q, sends_o)
        ffn_rows = jnp.dot(inner_, down_full, preferred_element_type=f4)
        block_out = (hidden + live_mask * ffn_rows).astype(bf)
        grad_rel_table, grad_layout_table = table_grads(
            jnp.concatenate([rel_a, rel_b], 0), jnp.concatenate([lay_a, lay_b], 0)
        )
        far_u, got_q, got_o, block_out = tie((far_u, got_q, got_o, block_out))
        share_up = cube.total(own_u, far_u)
        sends_q, own_q = cube.split_far(keeps_q, got_q)
        far_q = cube.send_far(sends_q)
        sends_o, keeps_o = cube.split_b(keeps_o, got_o)
        got_o = cube.send_b(sends_o)
        small = cube.all_sum(
            jnp.concatenate(
                [grad_gain_one, grad_gain_two, grad_rel_table.reshape(-1), grad_layout_table.reshape(-1)]
            ).reshape(-1, 128)
        ).reshape(-1)
        sends_o, own_o = cube.split_far(keeps_o, got_o)
        far_o = cube.send_far(sends_o)
        share_out = cube.total(own_o, far_o)
        share_qkv = cube.total(own_q, far_q)
        rel_n, lay_n = relative_bias_table.size, layout_bias_table.size
        return (
            block_out,
            grad_tokens,
            small[:d],
            share_qkv[:, :d],
            share_qkv[:, d : 2 * d],
            share_qkv[:, 2 * d :],
            share_out,
            small[d : 2 * d],
            share_gate,
            share_up,
            share_down,
            small[2 * d : 2 * d + rel_n].reshape(relative_bias_table.shape),
            small[2 * d + rel_n : 2 * d + rel_n + lay_n].reshape(layout_bias_table.shape),
        )

    return body


def solution(mesh):
    rows = P(AXES, None)
    line = P(AXES)
    whole = P()
    return jax.shard_map(
        make_body(Cube(mesh)),
        mesh=mesh,
        in_specs=(
            rows, whole, rows, rows, rows, rows, whole, rows, rows, rows, whole, whole, rows, line, line, rows,
        ),
        out_specs=(
            rows, rows, whole, rows, rows, rows, rows, whole, rows, rows, rows, whole, whole,
        ),
        check_vma=False,
    )
```

```python
import numpy as np
import jax
import jax.numpy as jnp
from jax import lax
from jax.experimental import pallas as pl
from jax.experimental.pallas import tpu as pltpu
from jax.sharding import PartitionSpec as P

bf = jnp.bfloat16
f4 = jnp.float32

HEADS,HEAD=16,64
bucket_edges=(1,2,3,4,5,6,7,8,12,16,23,32,46,64,91)
GRID=64
def np_bucket(n):
    n=np.asarray(n); m=np.abs(n)
    b=np.zeros(n.shape,np.int32)
    for e in bucket_edges: b+=(m>=e)
    return b+(n>0)*16
BLK=128
NT=(((1,),(1,)),((),()))
NN=(((1,),(0,)),((),()))
def dot(a,b,dims=NN): return lax.dot_general(a,b,dims,preferred_element_type=f4)

def fwd_kernel(q_ref,k_ref,v_ref,oh_ref,ff_ref,w_ref,far_ref,mask_ref,o_ref,p_ref):
    t=q_ref.shape[0]; nb=t//BLK
    lane=lax.broadcasted_iota(jnp.int32,(t,2*HEAD),1)
    q=q_ref[...]; oh=oh_ref[...]; v=v_ref[...]
    oht=oh.T; ka=jnp.concatenate([k_ref[...].T,oht,oht],axis=0)
    for j in range(2):
        mine=(lane<HEAD) if j==0 else (lane>=HEAD)
        band=pltpu.roll(jnp.broadcast_to(w_ref[0,j:j+1,:],(BLK,4*BLK)),0,1,stride=1,stride_axis=0)
        near=far_ref[0,j:j+1,0:BLK]; past=far_ref[0,j:j+1,BLK:2*BLK]
        rows=dot(oh,ff_ref[j]).astype(bf)
        qa=jnp.concatenate([jnp.where(mine,q,jnp.zeros_like(q)),rows],axis=1)
        whole=dot(qa,ka)
        for s in range(nb):
            sc=whole[s*BLK:(s+1)*BLK]
            rel=[]
            for c in range(nb):
                if c<s-1: rel.append(jnp.broadcast_to(past,(BLK,BLK)))
                elif c>s+1: rel.append(jnp.broadcast_to(near,(BLK,BLK)))
                else: rel.append(band[:,(c-s+1)*BLK:(c-s+2)*BLK])
            sc=(sc+jnp.concatenate(rel,axis=1))+mask_ref[s*BLK:(s+1)*BLK,:]
            top=jnp.max(sc,axis=1,keepdims=True)
            e=jnp.exp(sc-top)
            p=e*(1.0/jnp.sum(e,axis=1,keepdims=True))
            p_ref[j,s*BLK:(s+1)*BLK,:]=p
            o=dot(p.astype(bf),v).astype(bf)
            o_ref[s*BLK:(s+1)*BLK,j*HEAD:(j+1)*HEAD]=o[:,j*HEAD:(j+1)*HEAD]

def bwd_kernel(q_ref,k_ref,v_ref,g_ref,oh_ref,oht_ref,p_ref,d_ref,rel_ref,lay_ref,ds_s,pb_s):
    t=q_ref.shape[0]; nb=t//BLK
    lane=lax.broadcasted_iota(jnp.int32,(t,2*HEAD),1)
    q=q_ref[...]; k=k_ref[...]; v=v_ref[...]; g=g_ref[...]; oh=oh_ref[...]
    koh=jnp.concatenate([k,oh],axis=1)
    qt=q.T; gt=g.T; vt=v.T
    outs=[]
    for j in range(2):
        mine=(lane<HEAD) if j==0 else (lane>=HEAD)
        gm=jnp.where(mine,g,jnp.zeros_like(g))
        band=[jnp.zeros((BLK,BLK),f4) for _ in range(3)]
        past=jnp.zeros((BLK,BLK),f4); near=jnp.zeros((BLK,BLK),f4)
        whole=dot(gm,vt)
        for s in range(nb):
            rows=slice(s*BLK,(s+1)*BLK)
            dp=whole[rows]
            p=p_ref[j,rows,:]
            ds=p*(dp-jnp.sum(p*dp,axis=1,keepdims=True))
            for c in range(nb):
                tile=ds[:,c*BLK:(c+1)*BLK]
                if c<s-1: past=past+tile
                elif c>s+1: near=near+tile
                else: band[c-s+1]=band[c-s+1]+tile
            dsb=ds.astype(bf)
            ds_s[rows,:]=dsb; pb_s[rows,:]=p.astype(bf)
        dq=dot(ds_s[...],koh)
        dkt=dot(qt,ds_s[...]); dvt=dot(gt,pb_s[...])
        outs.append((dq[:,:2*HEAD],dkt,dvt))
        r=dq[:,2*HEAD:]
        hi=r.astype(bf); lo=(r-hi.astype(f4)).astype(bf)
        gl=dot(oht_ref[...],jnp.concatenate([hi,lo],axis=1))
        gl=gl[:,:2*GRID]+gl[:,2*GRID:]
        for i in range(2):
            part=gl[i*GRID:(i+1)*GRID,i*GRID:(i+1)*GRID]
            part=pltpu.roll(jnp.concatenate([part,jnp.zeros((GRID,GRID),f4)],axis=1),0,1,stride=1,stride_axis=0)
            lay_ref[0,2*j+i:2*j+i+1,:]=jnp.sum(part,axis=0,keepdims=True)
        wide=jnp.concatenate(band+[jnp.zeros((BLK,BLK),f4)],axis=1)
        acc=wide[0:8]
        for i in range(1,BLK//8):
            acc=acc+pltpu.roll(wide[8*i:8*i+8],4*BLK-8*i,1)
        line=acc[0:1]
        for i in range(1,8):
            line=line+pltpu.roll(acc[i:i+1],4*BLK-i,1)
        rel_ref[0,j:j+1,0:4*BLK]=line
        rel_ref[0,j:j+1,4*BLK:5*BLK]=jnp.sum(near,axis=0,keepdims=True)
        rel_ref[0,j:j+1,5*BLK:6*BLK]=jnp.sum(past,axis=0,keepdims=True)
    d_ref[0]=jnp.where(lane<HEAD,outs[0][0],outs[1][0]).astype(bf)
    sub=lax.broadcasted_iota(jnp.int32,(2*HEAD,t),0)
    d_ref[1]=jnp.where(sub<HEAD,outs[0][1],outs[1][1]).astype(bf).T
    d_ref[2]=jnp.where(sub<HEAD,outs[0][2],outs[1][2]).astype(bf).T

def fwd(qkv,oh,ff,w,far,mask,lo,n):
    t=qkv.shape[0]; pairs=HEADS//2
    col=lambda off: pl.BlockSpec((t,2*HEAD),lambda i,off=off:(0,off+lo+i))
    return pl.pallas_call(fwd_kernel,grid=(n,),
        in_specs=[col(0),col(pairs),col(2*pairs),pl.BlockSpec((t,2*GRID),lambda i:(0,0)),
          pl.BlockSpec((2,2*GRID,4*GRID),lambda i:(lo+i,0,0)),pl.BlockSpec((1,2,4*BLK),lambda i:(lo+i,0,0)),
          pl.BlockSpec((1,2,2*BLK),lambda i:(lo+i,0,0)),pl.BlockSpec((t,t),lambda i:(0,0))],
        out_specs=[pl.BlockSpec((t,2*HEAD),lambda i:(0,i)),pl.BlockSpec((2,t,t),lambda i:(i,0,0))],
        out_shape=[jax.ShapeDtypeStruct((t,2*HEAD*n),bf),jax.ShapeDtypeStruct((2*n,t,t),f4)],
        compiler_params=pltpu.CompilerParams(vmem_limit_bytes=48<<20),
        cost_estimate=pl.CostEstimate(flops=7_000_000_000*n//8,bytes_accessed=24_000_000*n//8,transcendentals=4_200_000*n//8),
        name="attend_forward")(qkv,qkv,qkv,oh,ff,w,far,mask)

def bwd(qkv,g,oh,oht,p,lo,n):
    t=qkv.shape[0]; pairs=HEADS//2
    col=lambda off: pl.BlockSpec((t,2*HEAD),lambda i,off=off:(0,off+lo+i))
    return pl.pallas_call(bwd_kernel,grid=(n,),
        in_specs=[col(0),col(pairs),col(2*pairs),col(0),pl.BlockSpec((t,2*GRID),lambda i:(0,0)),pl.BlockSpec((2*GRID,t),lambda i:(0,0)),
          pl.BlockSpec((2,t,t),lambda i:(i,0,0))],
        out_specs=[pl.BlockSpec((3,t,2*HEAD),lambda i:(0,0,i)),pl.BlockSpec((1,2,6*BLK),lambda i:(i,0,0)),pl.BlockSpec((1,4,2*GRID),lambda i:(i,0,0))],
        out_shape=[jax.ShapeDtypeStruct((3,t,2*HEAD*n),bf),jax.ShapeDtypeStruct((n,2,6*BLK),f4),jax.ShapeDtypeStruct((n,4,2*GRID),f4)],
        scratch_shapes=[pltpu.VMEM((t,t),bf),pltpu.VMEM((t,t),bf)],
        compiler_params=pltpu.CompilerParams(vmem_limit_bytes=48<<20),
        cost_estimate=pl.CostEstimate(flops=9_000_000_000*n//8,bytes_accessed=24_000_000*n//8,transcendentals=0),
        name="attend_backward")(qkv,qkv,qkv,g,oh,oht,p)

HI=lax.Precision.HIGHEST
def hot(n):
    return (np_bucket(n)[None,:]==np.arange(32)[:,None]).astype(np.float32)
N_GRID=(np.arange(GRID)[:,None]-np.arange(GRID)[None,:]).reshape(-1)
_m=np.arange(512); N_BAND=128-np.where(_m>=385,_m-512,_m)
def tables(rel,lay):
    w=jnp.einsum("bh,bn->hn",rel,jnp.asarray(hot(N_BAND)),precision=HI).reshape(8,2,512)
    far=jnp.concatenate([jnp.broadcast_to(rel[15][:,None],(16,128)),jnp.broadcast_to(rel[31][:,None],(16,128))],1).reshape(8,2,256)
    f=[jnp.einsum("bh,bn->hn",lay[32*i:32*i+32],jnp.asarray(hot(N_GRID)),precision=HI).reshape(16,64,64) for i in range(2)]
    z=jnp.zeros((16,64,64),f4)
    full=jnp.concatenate([jnp.concatenate([f[0],z],2),jnp.concatenate([z,f[1]],2)],1)
    hi=full.astype(bf)
    hi32=lax.reduce_precision(full,8,7)
    lo=(full-hi32).astype(bf)
    return w,far,jnp.concatenate([hi,lo],2)
def table_grads(relsum,laysum):
    rs=relsum.reshape(16,768); ls=laysum.reshape(16,2,128)
    oh=hot(N_BAND); oh[:,384]=0
    e15=np.zeros((32,128),np.float32); e15[15]=1
    e31=np.zeros((32,128),np.float32); e31[31]=1
    C=np.concatenate([oh,e15,e31],1)
    grel=jnp.einsum("bn,hn->bh",jnp.asarray(C),rs,precision=HI)
    m=np.arange(128); nn=63-m
    oh2=hot(nn); oh2[:,127]=0
    glay=jnp.einsum("bn,hxn->xbh",jnp.asarray(oh2),ls,precision=HI).reshape(64,16)
    return grel,glay

epsilon = 1e-06
masked_score = -1e30
AXES = ("wide", "narrow")
VMEM_LIMIT = 58 << 20
TILE = 256


def tie(values, *after):
    return lax.optimization_barrier((values, after))[0]


class Cube:
    def __init__(self, mesh):
        self.n = mesh.shape["wide"] * mesh.shape["narrow"]
        self.bits = self.n.bit_length() - 1
        self.per_wide = mesh.shape["narrow"]
        self.far = self.n // 8

    def me(self):
        return (lax.axis_index("wide") * self.per_wide + lax.axis_index("narrow")).astype(jnp.int32)

    def swap(self, x, mask):
        return lax.ppermute(x, AXES, [(i, i ^ mask) for i in range(self.n)])

    def far_first(self, own):
        return [own[None], self.swap(own[None], self.n // 2)]

    def far_rest(self, blocks):
        for b in range(self.bits - 2, 2, -1):
            cur = jnp.concatenate(blocks, 0)
            blocks = [cur, self.swap(cur, 1 << b)]
        return blocks

    def far_rel(self):
        rel = [0]
        for b in range(self.bits - 1, 2, -1):
            rel = rel + [d ^ (1 << b) for d in rel]
        return rel

    def step_a(self, pair):
        return [self.swap(pair[0], 2), self.swap(pair[1], 4)]

    def step_b(self, pair):
        return [self.swap(pair[0], 4), self.swap(pair[1], 2)]

    def joined(self, pair, got):
        return [jnp.concatenate([x, g], 0) for x, g in zip(pair, got)]

    def step_core(self, pair):
        return [self.swap(x, 1) for x in pair]

    def pieces(self, pair, cores):
        out = []
        for x, g, masks in zip(pair, cores, ((2, 4), (4, 2))):
            rel = self.far_rel()
            for m in masks:
                rel = rel + [d ^ m for d in rel]
            out.append([(x, rel), (g, [d ^ 1 for d in rel])])
        return out

    def plan(self, parts, bands):
        flat, steps, col = [], [], 0
        for pieces in parts:
            mine = []
            for arr, rel in pieces:
                for j, d in enumerate(rel):
                    for k, (r0, r) in enumerate(bands):
                        mine.append((len(flat), j, d, r0, r, k, col, arr.shape[2]))
                flat.append(arr)
            col += pieces[0][0].shape[2]
            steps.append(mine)
        return flat, steps, col

    def assemble(self, parts, bands):
        flat, steps, col = self.plan(parts, bands)
        count = sum(len(x) for x in steps)

        def kernel(me_ref, *refs):
            outs, sem = refs[len(flat) : len(flat) + len(bands)], refs[-1]
            copies = []
            for at, j, d, r0, r, k, c0, w in [x for mine in steps for x in mine]:
                copies.append(
                    pltpu.make_async_copy(
                        refs[at].at[j, pl.ds(r0, r)],
                        outs[k].at[me_ref[0] ^ d, :, pl.ds(c0, w)],
                        sem.at[len(copies)],
                    )
                )
            for c in copies:
                c.start()
            for c in copies:
                c.wait()

        outs = pl.pallas_call(
            kernel,
            grid_spec=pltpu.PrefetchScalarGridSpec(
                num_scalar_prefetch=1,
                grid=(1,),
                in_specs=[pl.BlockSpec(memory_space=pl.ANY)] * len(flat),
                out_specs=[pl.BlockSpec((self.n, r, col), lambda i, m: (0, 0, 0)) for _, r in bands],
                scratch_shapes=[pltpu.SemaphoreType.DMA((count,))],
            ),
            out_shape=[jax.ShapeDtypeStruct((self.n, r, col), bf) for _, r in bands],
            compiler_params=pltpu.CompilerParams(vmem_limit_bytes=VMEM_LIMIT),
            cost_estimate=pl.CostEstimate(
                flops=0, bytes_accessed=4 * self.n * col * sum(r for _, r in bands), transcendentals=0
            ),
            name="assemble",
        )(self.me()[None], *flat)
        return [o.reshape(-1, col) for o in outs]

    def project(self, x, parts):
        r = parts[0][0][0].shape[1]
        t, d = x.shape
        if r % 16:
            [whole] = self.assemble(parts, [(0, r)])
            return jnp.dot(x, whole, preferred_element_type=f4).astype(bf), whole
        flat, steps, col = self.plan(parts, [(0, r)])
        count = sum(len(m) for m in steps)
        tile = 512

        def kernel(me_ref, x_ref, *refs):
            y_ref, w_ref, held, sem, out_sem = refs[len(flat) :]
            todo, k = [], 0
            for mine in steps:
                copies = []
                for at, j, d_, _, _, _, c0, w in mine:
                    copies.append(
                        pltpu.make_async_copy(
                            refs[at].at[j], held.at[me_ref[0] ^ d_, :, pl.ds(c0, w)], sem.at[k]
                        )
                    )
                    k += 1
                for c in copies:
                    c.start()
                todo.append(copies)
            writes = []
            for mine, copies in zip(steps, todo):
                c0, w = mine[0][6], mine[0][7]
                for c in copies:
                    c.wait()
                write = pltpu.make_async_copy(
                    held.at[:, :, pl.ds(c0, w)], w_ref.at[:, :, pl.ds(c0, w)], out_sem.at[len(writes)]
                )
                write.start()
                writes.append(write)
                for c in range(c0, c0 + w, tile):
                    block = held[:, :, c : c + tile].reshape(d, tile)
                    y_ref[:, c : c + tile] = dot(x_ref[...], block).astype(bf)
            for write in writes:
                write.wait()

        y, whole = pl.pallas_call(
            kernel,
            grid_spec=pltpu.PrefetchScalarGridSpec(
                num_scalar_prefetch=1,
                grid=(1,),
                in_specs=[pl.BlockSpec((t, d), lambda i, m: (0, 0))]
                + [pl.BlockSpec(memory_space=pl.ANY)] * len(flat),
                out_specs=[pl.BlockSpec((t, col), lambda i, m: (0, 0)), pl.BlockSpec(memory_space=pl.ANY)],
                scratch_shapes=[
                    pltpu.VMEM((self.n, r, col), bf),
                    pltpu.SemaphoreType.DMA((count,)),
                    pltpu.SemaphoreType.DMA((len(steps),)),
                ],
            ),
            out_shape=[jax.ShapeDtypeStruct((t, col), bf), jax.ShapeDtypeStruct((self.n, r, col), bf)],
            compiler_params=pltpu.CompilerParams(vmem_limit_bytes=VMEM_LIMIT),
            cost_estimate=pl.CostEstimate(
                flops=2 * t * d * col, bytes_accessed=4 * d * col + 2 * t * (d + col), transcendentals=0
            ),
            name="project",
        )(self.me()[None], x, *flat)
        return y, whole.reshape(d, col)

    def gated(self, x, whole, grad_inner):
        t, d = x.shape
        ff = grad_inner.shape[1]

        def kernel(x_ref, w_ref, g_ref, inner_ref, grad_ref):
            both = dot(x_ref[...], w_ref[...])
            inner, gate, up = gate_math(both[:, :TILE], both[:, TILE:], g_ref[...])
            inner_ref[...] = inner
            grad_ref[:, :TILE] = gate
            grad_ref[:, TILE:] = up

        block = pl.BlockSpec((t, TILE), lambda i: (0, i))
        return pl.pallas_call(
            kernel,
            grid=(ff // TILE,),
            in_specs=[
                pl.BlockSpec((t, d), lambda i: (0, 0)),
                pl.BlockSpec((d, 2 * TILE), lambda i: (0, i)),
                block,
            ],
            out_specs=[block, pl.BlockSpec((t, 2 * TILE), lambda i: (0, i))],
            out_shape=[jax.ShapeDtypeStruct((t, ff), bf), jax.ShapeDtypeStruct((t, 2 * ff), bf)],
            compiler_params=pltpu.CompilerParams(vmem_limit_bytes=VMEM_LIMIT),
            cost_estimate=pl.CostEstimate(
                flops=4 * t * d * ff, bytes_accessed=4 * d * ff + 10 * t * ff, transcendentals=t * ff
            ),
            name="gated",
        )(x, whole, grad_inner)

    def places(self, p):
        out = [0]
        for m in [1 << b for b in range(self.bits - 1, 2, -1)] + [[2, 4], [4, 2]][p] + [1]:
            out = out + [d ^ m for d in out]
        return out

    def terms(self, x, dy, width=None, into=None):
        t, rows = x.shape
        if dy.ndim == 2:
            dy = dy[None]
        r, each = rows // self.n, dy.shape[2]
        half = dy.shape[0] * each // 2
        n = self.n
        if r % 8:
            g = jnp.concatenate([jnp.einsum("tf,td->fd", x, y, preferred_element_type=f4).astype(bf) for y in dy], 1)
            g = g.reshape((2,) * self.bits + (r, -1))
            for b in range(self.bits):
                g = jnp.where((self.me() >> b) & 1 == 1, jnp.flip(g, self.bits - 1 - b), g)
            last = self.bits - 1
            both = []
            for p, near in enumerate(((last - 2, last - 1), (last - 1, last - 2))):
                order = (last, *near, *range(last - 3, -1, -1), last + 1, last + 2)
                part = jnp.transpose(g[..., p * half : (p + 1) * half], order)
                both.append(part.reshape(n, r, half))
            both = jnp.stack(both)
            both = both[:, n // 2 :], both[:, : n // 2]
            if into is not None:
                return tuple(jnp.concatenate([a[..., : a.shape[-1] - half], b], -1) for a, b in zip(into, both))
            if width is not None:
                return tuple(jnp.pad(b, ((0, 0), (0, 0), (0, 0), (0, width - half))) for b in both)
            return both
        ordered = r % 16 == 0
        tile = max(c for c in range(128, half + 1, 128) if half % c == 0 and each % c == 0 and c * rows <= 1500000)
        chunk = 256
        per, across = half // tile, each // tile

        def kernel(me_ref, x_ref, y_ref, *refs):
            send_ref, keep_ref, turned, acc = refs[-4:]
            first = pl.program_id(0) == 0
            y_ = y_ref[0]

            def who(at):
                d0, d1 = self.places(0)[at], self.places(1)[at]
                return pl.multiple_of((me_ref[0] ^ jnp.where(first, d0, d1)) * r, r)

            if ordered:

                @pl.when((pl.program_id(0) == 0) & (pl.program_id(1) == 0))
                def _():
                    for c in range(0, rows, chunk):
                        acc[c : c + chunk, :] = x_ref[:, c : c + chunk].T

                @pl.when(pl.program_id(1) == 0)
                def _():
                    for at in range(n):
                        turned[at * r : (at + 1) * r, :] = acc[pl.ds(who(at), r), :]

                for c in range(0, rows, chunk):
                    out = dot(turned[c : c + chunk, :], y_).astype(bf)
                    for k in range(chunk // r):
                        at = c // r + k
                        ref = keep_ref if at < n // 2 else send_ref
                        ref[0, at % (n // 2)] = out[k * r : (k + 1) * r]
                return

            for c in range(0, rows, chunk):
                acc[c : c + chunk, :] = dot(x_ref[:, c : c + chunk], y_, (((0,), (0,)), ((), ())))
            for at in range(n):
                ref = keep_ref if at < n // 2 else send_ref
                ref[0, at % (n // 2)] = acc[pl.ds(who(at), r), :].astype(bf)

        if into is not None:
            width = into[0].shape[3]
        skip = 0 if into is None else (width - half) // tile
        out = pl.BlockSpec((1, n // 2, r, tile), lambda p, j, m: (p, 0, 0, skip + j))
        shape = jax.ShapeDtypeStruct((2, n // 2, r, width or half), bf)
        more = () if into is None else tuple(into)
        return pl.pallas_call(
            kernel,
            grid_spec=pltpu.PrefetchScalarGridSpec(
                num_scalar_prefetch=1,
                grid=(2, per),
                in_specs=[
                    pl.BlockSpec((t, rows), lambda p, j, m: (0, 0)),
                    pl.BlockSpec(
                        (1, t, tile), lambda p, j, m: ((p * per + j) // across, 0, (p * per + j) % across)
                    ),
                ]
                + [pl.BlockSpec(memory_space=pl.ANY)] * len(more),
                out_specs=[out, out],
                scratch_shapes=[
                    pltpu.VMEM((rows, t) if ordered else (8, 128), bf),
                    pltpu.VMEM((rows, t), bf) if ordered else pltpu.VMEM((rows, tile), f4),
                ],
            ),
            out_shape=[shape, shape],
            input_output_aliases={} if into is None else {3: 0, 4: 1},
            compiler_params=pltpu.CompilerParams(vmem_limit_bytes=VMEM_LIMIT),
            cost_estimate=pl.CostEstimate(
                flops=4 * t * rows * half, bytes_accessed=2 * (t * rows + 2 * t * half + 2 * rows * half), transcendentals=0
            ),
            name="terms",
        )(self.me()[None], x, dy, *more)

    def plus(self, a, b):
        return a.astype(f4) + b.astype(f4)

    def split_a(self, keep, got):
        h = self.n // 4

        def side(p, lo, hi):
            return self.plus(keep[p, lo:hi], got[p, lo:hi]).astype(bf)

        return [side(p, h, 2 * h) for p in range(2)], [side(p, 0, h) for p in range(2)]

    def send_a(self, sends):
        return [self.swap(sends[0], 4), self.swap(sends[1], 2)]

    def split_b(self, keeps, gots):
        h = self.n // 8
        sends = [self.plus(k[h:], g[h:]).astype(bf) for k, g in zip(keeps, gots)]
        return sends, [self.plus(k[:h], g[:h]) for k, g in zip(keeps, gots)]

    def send_b(self, sends):
        return [self.swap(sends[0], 2), self.swap(sends[1], 4)]

    def split_far(self, keeps, gots):
        h = self.far // 2

        def both(lo, hi):
            return jnp.concatenate([self.plus(k[lo:hi], g[lo:hi]) for k, g in zip(keeps, gots)], -1)

        return both(h, 2 * h).astype(bf), both(0, h)

    def far_step(self, keep, got):
        h = keep.shape[0] // 2
        return self.plus(keep[h:], got[h:]).astype(bf), self.plus(keep[:h], got[:h])

    def far_send(self, send):
        return self.swap(send, self.n // 2 // send.shape[0])

    def far_end(self, keep, got):
        while keep.shape[0] > 2:
            send, keep = self.far_step(keep, got)
            got = self.far_send(send)
        return self.far_step(keep, got)

    def total(self, own, got):
        return self.plus(own, got)[0]


def moved(name, moves, ins, outs):
    def kernel(*refs):
        for i, src, o, dst in moves:
            refs[len(ins) + o][dst] = refs[i][src]

    return pl.pallas_call(
        kernel,
        out_shape=[jax.ShapeDtypeStruct(x, bf) for x in outs],
        compiler_params=pltpu.CompilerParams(vmem_limit_bytes=VMEM_LIMIT),
        cost_estimate=pl.CostEstimate(
            flops=0, bytes_accessed=sum(2 * x.size for x in ins) + sum(2 * int(np.prod(x)) for x in outs), transcendentals=0
        ),
        name=name,
    )(*ins)


def packed(query, key, value, out, down, gate, up):
    every = slice(None)
    moves = []
    at = 0
    for i, x in enumerate((query, key, value)):
        moves.append((i, (every, every), 0, (every, slice(at, at + x.shape[1]))))
        at += x.shape[1]
    rows = out.shape[0]
    moves.append((3, (every, every), 1, (slice(0, rows), every)))
    moves.append((4, (every, every), 1, (slice(rows, rows + down.shape[0]), every)))
    for c in range(0, gate.shape[1], TILE):
        moves.append((5, (every, slice(c, c + TILE)), 2, (every, slice(2 * c, 2 * c + TILE))))
        moves.append((6, (every, slice(c, c + TILE)), 2, (every, slice(2 * c + TILE, 2 * c + 2 * TILE))))
    shapes = [(query.shape[0], at), (rows + down.shape[0], out.shape[1]), (gate.shape[0], 2 * gate.shape[1])]
    return moved("pack", moves, (query, key, value, out, down, gate, up), shapes)


def stacked(blocks):
    ins, moves, at = [], [], 0
    half = blocks[0].shape[2] // 2
    for x in blocks:
        for p in range(2):
            cols = slice(p * half, (p + 1) * half)
            moves.append(
                (len(ins), (slice(None), slice(None), cols), p, (slice(at, at + x.shape[0]), slice(None), slice(None)))
            )
        ins.append(x)
        at += x.shape[0]
    return moved("stack", moves, tuple(ins), [(at, blocks[0].shape[1], half)] * 2)


def rms_norm(values, gains):
    factor = lax.rsqrt(jnp.mean(values * values, axis=-1, keepdims=True) + epsilon)
    return values * factor * gains


def gate_math(gate, up, grad_inner):
    c = 0.7978845608028654
    square = gate * gate
    t = jnp.tanh(c * gate * (1.0 + 0.044715 * square))
    half = 0.5 * (1.0 + t)
    act = gate * half
    slope = half + 0.5 * gate * (1.0 - t * t) * (c * (1.0 + 3.0 * 0.044715 * square))
    return (act * up).astype(bf), (grad_inner * up * slope).astype(bf), (grad_inner * act).astype(bf)


def make_body(cube):
    def body(
        tokens, gain_one, query_weight, key_weight, value_weight, out_weight, gain_two, gate_weight,
        up_weight, down_weight, relative_bias_table, layout_bias_table, doc_lengths, box_x, box_y, cotangent,
    ):
        row_count, d = tokens.shape
        pairs = HEADS // 2
        own1, own2, own3 = packed(
            query_weight, key_weight, value_weight, out_weight, down_weight, gate_weight, up_weight
        )
        gu_full = lax.all_gather(own3, AXES, axis=0, tiled=True)
        far1 = cube.far_first(own1)

        positions = jnp.arange(row_count, dtype=jnp.int32)
        slots = jnp.arange(doc_lengths.shape[1], dtype=jnp.int32)
        doc_ends = jnp.sum(jnp.where(slots[:, None] <= slots[None, :], doc_lengths[0][:, None], 0), axis=0)
        live_rows = positions < doc_ends[-1]
        doc_ids = jnp.sum((positions[:, None] >= doc_ends[None, :]).astype(jnp.int32), axis=1)
        seg_ids = jnp.where(live_rows, doc_ids, doc_lengths.shape[1] + positions)
        live_mask = live_rows.astype(f4)[:, None]
        mask = jnp.where(seg_ids[:, None] == seg_ids[None, :], 0.0, masked_score).astype(f4)
        levels = jnp.arange(GRID, dtype=jnp.int32)
        hots = jnp.concatenate([box_x[:, None] == levels, box_y[:, None] == levels], 1).astype(bf)
        down_hots = jnp.concatenate(
            [box_x[None] == levels[::-1, None], box_y[None] == levels[::-1, None]], 0
        ).astype(bf)
        bands, far, values = tables(relative_bias_table, layout_bias_table)
        inputs_wide = tokens.astype(f4)
        normed_wide, norm_one_back = jax.vjp(rms_norm, inputs_wide, gain_one)
        normed = normed_wide.astype(bf)
        grad_output = cotangent.astype(f4)
        grad_ffn = (live_mask * grad_output).astype(bf)

        far1, own2, normed, mask, hots, down_hots, bands, far, values, grad_ffn = tie(
            (far1, own2, normed, mask, hots, down_hots, bands, far, values, grad_ffn)
        )
        far1 = cube.far_rest(far1)
        far1, own2 = tie((far1, own2))
        pair1 = stacked(far1)
        own2 = tie(own2, pair1)
        got1 = cube.step_a(pair1)
        far2 = cube.far_first(own2)
        got1, far2 = tie((got1, far2))
        pair1 = cube.joined(pair1, got1)
        got1 = cube.step_b(pair1)
        far2 = cube.far_rest(far2)
        got1, far2 = tie((got1, far2))
        pair1 = cube.joined(pair1, got1)
        core1 = cube.step_core(pair1)
        pair2 = stacked(far2)
        got2 = cube.step_a(pair2)
        normed_ = tie(normed, pair2)
        qkv, qkv_full = cube.project(normed_, cube.pieces(pair1, core1))
        got2, qkv = tie((got2, qkv))
        pair2 = cube.joined(pair2, got2)
        got2 = cube.step_b(pair2)
        qkv_ = tie(qkv, pair2)
        attended, probs = fwd(qkv_, hots, values, bands, far, mask, 0, pairs)
        got2, attended = tie((got2, attended))
        pair2 = cube.joined(pair2, got2)
        core2 = cube.step_core(pair2)
        out_rows = out_weight.shape[0]
        out_full, down_full = cube.assemble(
            cube.pieces(pair2, core2), [(0, out_rows), (out_rows, down_weight.shape[0])]
        )
        branch = jnp.dot(attended, out_full, preferred_element_type=f4)
        hidden = inputs_wide + live_mask * branch
        normed_two_wide, norm_two_back = jax.vjp(rms_norm, hidden, gain_two)
        normed_two = normed_two_wide.astype(bf)
        grad_inner = jnp.einsum("td,fd->tf", grad_ffn, down_full, preferred_element_type=f4)
        gu_full, normed_two, grad_inner = tie((gu_full, normed_two, grad_inner))
        inner_rows, grad_gu = cube.gated(normed_two, gu_full, grad_inner)

        send_d, keep_d = cube.terms(inner_rows, grad_ffn)
        got_d = cube.swap(send_d, 1)
        grad_gu_ = tie(grad_gu, send_d)
        send_g, keep_g = cube.terms(normed_two, grad_gu_)
        got_d, send_g, keep_g = tie((got_d, send_g, keep_g))
        got_g = cube.swap(send_g, 1)
        sends_d, keeps_d = cube.split_a(keep_d, got_d)
        got_d = cube.send_a(sends_d)
        gu_full_, grad_gu_ = tie((gu_full, grad_gu_), send_g, sends_d)
        grad_normed_two = jnp.einsum("tf,df->td", grad_gu_, gu_full_, preferred_element_type=f4)
        got_d, got_g, grad_normed_two = tie((got_d, got_g, grad_normed_two))
        sends_d, keeps_d = cube.split_b(keeps_d, got_d)
        got_d = cube.send_b(sends_d)
        got_g, grad_normed_two = tie((got_g, grad_normed_two), sends_d)
        sends_g, keeps_g = cube.split_a(keep_g, got_g)
        grad_hidden_part, grad_gain_two = norm_two_back(grad_normed_two)
        grad_hidden = grad_output + grad_hidden_part
        grad_branch = (live_mask * grad_hidden).astype(bf)
        got_d, sends_g, grad_branch = tie((got_d, sends_g, grad_branch))
        got_g = cube.send_a(sends_g)
        keeps_d, got_d = tie((keeps_d, got_d), sends_g)
        send_d, own_d = cube.split_far(keeps_d, got_d)
        far_d = cube.far_send(send_d)
        grad_branch_ = tie(grad_branch, send_d)
        grad_attended = jnp.einsum("td,ed->te", grad_branch_, out_full, preferred_element_type=f4).astype(bf)
        grad_qkv, rel_sums, lay_sums = bwd(qkv, grad_attended, hots, down_hots, probs, 0, pairs)
        send_q, keep_q = cube.terms(normed, grad_qkv, 2 * d)
        send_q, keep_q = cube.terms(attended, grad_branch, into=(send_q, keep_q))
        got_g, far_d, send_q, keep_q = tie((got_g, far_d, send_q, keep_q))
        sends_g, keeps_g = cube.split_b(keeps_g, got_g)
        got_g = cube.send_b(sends_g)
        got_q = cube.swap(send_q, 1)
        send_d, own_d = cube.far_end(own_d, far_d)
        far_d = cube.far_send(send_d)
        grad_qkv = tie(grad_qkv, sends_g, send_d)
        grad_normed = jnp.zeros((), f4)
        for i in range(3):
            grad_normed = grad_normed + jnp.einsum(
                "te,de->td", grad_qkv[i], qkv_full[:, i * d : (i + 1) * d], preferred_element_type=f4
            )
        grad_input_part, grad_gain_one = norm_one_back(grad_normed)
        grad_tokens = grad_hidden + grad_input_part
        grad_rel_table, grad_layout_table = table_grads(rel_sums, lay_sums)
        small = jnp.concatenate(
            [grad_gain_one, grad_gain_two, grad_rel_table.reshape(-1), grad_layout_table.reshape(-1)]
        ).reshape(-1, 128)
        got_g, got_q, far_d, grad_tokens, small = tie((got_g, got_q, far_d, grad_tokens, small))
        sends_q, keeps_q = cube.split_a(keep_q, got_q)
        got_q = cube.send_a(sends_q)
        keeps_g, got_g, small = tie((keeps_g, got_g, small), sends_q)
        send_g, own_g = cube.split_far(keeps_g, got_g)
        far_g = cube.far_send(send_g)
        got_s = cube.swap(small, 1)
        inner_, far_d = tie((inner_rows, far_d), send_g)
        share_down = cube.total(own_d, far_d)
        ffn_rows = jnp.dot(inner_, down_full, preferred_element_type=f4)
        block_out = (hidden + live_mask * ffn_rows).astype(bf)
        far_g, small, got_s, block_out = tie((far_g, small, got_s, block_out))
        send_g, own_g = cube.far_end(own_g, far_g)
        far_g = cube.far_send(send_g)
        small = small + got_s
        got_s = cube.swap(small, 2)
        got_q, small, got_s = tie((got_q, small, got_s), send_g)
        sends_q, keeps_q = cube.split_b(keeps_q, got_q)
        got_q = cube.send_b(sends_q)
        small = small + got_s
        got_s = cube.swap(small, 4)
        got_q, small, got_s = tie((got_q, small, got_s))
        send_q, own_q = cube.split_far(keeps_q, got_q)
        far_q = cube.far_send(send_q)
        small = small + got_s
        for b in range(3, cube.bits - 1):
            small = small + cube.swap(small, 1 << b)
        own_g, far_g = tie((own_g, far_g), send_q)
        share_gu = cube.total(own_g, far_g)
        far_q, small = tie((far_q, small))
        send_q, own_q = cube.far_end(own_q, far_q)
        far_q = cube.far_send(send_q)
        small = (small + cube.swap(small, cube.n // 2)).reshape(-1)
        share_q = cube.total(own_q, far_q)
        c = gate_weight.shape[1]
        share_gate = jnp.concatenate([share_gu[:, 2 * i : 2 * i + TILE] for i in range(0, c, TILE)], 1)
        share_up = jnp.concatenate([share_gu[:, 2 * i + TILE : 2 * i + 2 * TILE] for i in range(0, c, TILE)], 1)
        wide = 3 * d // 2
        left, right = share_q[:, : wide + d // 2], share_q[:, wide + d // 2 :]
        share_qkv = jnp.concatenate([left[:, :wide], right[:, :wide]], 1)
        share_out = jnp.concatenate([left[:, wide:], right[:, wide:]], 1)
        rel_n, lay_n = relative_bias_table.size, layout_bias_table.size
        return (
            block_out,
            grad_tokens,
            small[:d],
            share_qkv[:, :d],
            share_qkv[:, d : 2 * d],
            share_qkv[:, 2 * d :],
            share_out,
            small[d : 2 * d],
            share_gate,
            share_up,
            share_down,
            small[2 * d : 2 * d + rel_n].reshape(relative_bias_table.shape),
            small[2 * d + rel_n : 2 * d + rel_n + lay_n].reshape(layout_bias_table.shape),
        )

    return body


def solution(mesh):
    rows = P(AXES, None)
    line = P(AXES)
    whole = P()
    return jax.shard_map(
        make_body(Cube(mesh)),
        mesh=mesh,
        in_specs=(
            rows, whole, rows, rows, rows, rows, whole, rows, rows, rows, whole, whole, rows, line, line, rows,
        ),
        out_specs=(
            rows, rows, whole, rows, rows, rows, rows, whole, rows, rows, rows, whole, whole,
        ),
        check_vma=False,
    )
```

```python
import numpy as np
import jax
import jax.numpy as jnp
from jax import lax
from jax.experimental import pallas as pl
from jax.experimental.pallas import tpu as pltpu
from jax.sharding import PartitionSpec as P

bf = jnp.bfloat16
f4 = jnp.float32

HEADS,HEAD=16,64
bucket_edges=(1,2,3,4,5,6,7,8,12,16,23,32,46,64,91)
GRID=64
def np_bucket(n):
    n=np.asarray(n); m=np.abs(n)
    b=np.zeros(n.shape,np.int32)
    for e in bucket_edges: b+=(m>=e)
    return b+(n>0)*16
BLK=128
NT=(((1,),(1,)),((),()))
NN=(((1,),(0,)),((),()))
def dot(a,b,dims=NN): return lax.dot_general(a,b,dims,preferred_element_type=f4)

def fwd_kernel(q_ref,k_ref,v_ref,oh_ref,ff_ref,w_ref,far_ref,mask_ref,o_ref,p_ref):
    t=q_ref.shape[0]; nb=t//BLK
    lane=lax.broadcasted_iota(jnp.int32,(t,2*HEAD),1)
    q=q_ref[...]; oh=oh_ref[...]; v=v_ref[...]
    oht=oh.T; ka=jnp.concatenate([k_ref[...].T,oht,oht],axis=0)
    for j in range(2):
        mine=(lane<HEAD) if j==0 else (lane>=HEAD)
        band=pltpu.roll(jnp.broadcast_to(w_ref[0,j:j+1,:],(BLK,4*BLK)),0,1,stride=1,stride_axis=0)
        near=far_ref[0,j:j+1,0:BLK]; past=far_ref[0,j:j+1,BLK:2*BLK]
        rows=dot(oh,ff_ref[j]).astype(bf)
        qa=jnp.concatenate([jnp.where(mine,q,jnp.zeros_like(q)),rows],axis=1)
        whole=dot(qa,ka)
        for s in range(nb):
            sc=whole[s*BLK:(s+1)*BLK]
            rel=[]
            for c in range(nb):
                if c<s-1: rel.append(jnp.broadcast_to(past,(BLK,BLK)))
                elif c>s+1: rel.append(jnp.broadcast_to(near,(BLK,BLK)))
                else: rel.append(band[:,(c-s+1)*BLK:(c-s+2)*BLK])
            sc=(sc+jnp.concatenate(rel,axis=1))+mask_ref[s*BLK:(s+1)*BLK,:]
            top=jnp.max(sc,axis=1,keepdims=True)
            e=jnp.exp(sc-top)
            p=e*(1.0/jnp.sum(e,axis=1,keepdims=True))
            p_ref[j,s*BLK:(s+1)*BLK,:]=p
            o=dot(p.astype(bf),v).astype(bf)
            o_ref[s*BLK:(s+1)*BLK,j*HEAD:(j+1)*HEAD]=o[:,j*HEAD:(j+1)*HEAD]

def bwd_kernel(q_ref,k_ref,v_ref,g_ref,oh_ref,oht_ref,p_ref,d_ref,rel_ref,lay_ref,ds_s,pb_s):
    t=q_ref.shape[0]; nb=t//BLK
    lane=lax.broadcasted_iota(jnp.int32,(t,2*HEAD),1)
    q=q_ref[...]; k=k_ref[...]; v=v_ref[...]; g=g_ref[...]; oh=oh_ref[...]
    koh=jnp.concatenate([k,oh],axis=1)
    qt=q.T; gt=g.T; vt=v.T
    outs=[]
    for j in range(2):
        mine=(lane<HEAD) if j==0 else (lane>=HEAD)
        gm=jnp.where(mine,g,jnp.zeros_like(g))
        band=[jnp.zeros((BLK,BLK),f4) for _ in range(3)]
        past=jnp.zeros((BLK,BLK),f4); near=jnp.zeros((BLK,BLK),f4)
        whole=dot(gm,vt)
        for s in range(nb):
            rows=slice(s*BLK,(s+1)*BLK)
            dp=whole[rows]
            p=p_ref[j,rows,:]
            ds=p*(dp-jnp.sum(p*dp,axis=1,keepdims=True))
            for c in range(nb):
                tile=ds[:,c*BLK:(c+1)*BLK]
                if c<s-1: past=past+tile
                elif c>s+1: near=near+tile
                else: band[c-s+1]=band[c-s+1]+tile
            dsb=ds.astype(bf)
            ds_s[rows,:]=dsb; pb_s[rows,:]=p.astype(bf)
        dq=dot(ds_s[...],koh)
        dkt=dot(qt,ds_s[...]); dvt=dot(gt,pb_s[...])
        outs.append((dq[:,:2*HEAD],dkt,dvt))
        r=dq[:,2*HEAD:]
        hi=r.astype(bf); lo=(r-hi.astype(f4)).astype(bf)
        gl=dot(oht_ref[...],jnp.concatenate([hi,lo],axis=1))
        gl=gl[:,:2*GRID]+gl[:,2*GRID:]
        for i in range(2):
            part=gl[i*GRID:(i+1)*GRID,i*GRID:(i+1)*GRID]
            part=pltpu.roll(jnp.concatenate([part,jnp.zeros((GRID,GRID),f4)],axis=1),0,1,stride=1,stride_axis=0)
            lay_ref[0,2*j+i:2*j+i+1,:]=jnp.sum(part,axis=0,keepdims=True)
        wide=jnp.concatenate(band+[jnp.zeros((BLK,BLK),f4)],axis=1)
        acc=wide[0:8]
        for i in range(1,BLK//8):
            acc=acc+pltpu.roll(wide[8*i:8*i+8],4*BLK-8*i,1)
        line=acc[0:1]
        for i in range(1,8):
            line=line+pltpu.roll(acc[i:i+1],4*BLK-i,1)
        rel_ref[0,j:j+1,0:4*BLK]=line
        rel_ref[0,j:j+1,4*BLK:5*BLK]=jnp.sum(near,axis=0,keepdims=True)
        rel_ref[0,j:j+1,5*BLK:6*BLK]=jnp.sum(past,axis=0,keepdims=True)
    d_ref[0]=jnp.where(lane<HEAD,outs[0][0],outs[1][0]).astype(bf)
    sub=lax.broadcasted_iota(jnp.int32,(2*HEAD,t),0)
    d_ref[1]=jnp.where(sub<HEAD,outs[0][1],outs[1][1]).astype(bf).T
    d_ref[2]=jnp.where(sub<HEAD,outs[0][2],outs[1][2]).astype(bf).T

def fwd(qkv,oh,ff,w,far,mask,lo,n):
    t=qkv.shape[0]; pairs=HEADS//2
    col=lambda off: pl.BlockSpec((t,2*HEAD),lambda i,off=off:(0,off+lo+i))
    return pl.pallas_call(fwd_kernel,grid=(n,),
        in_specs=[col(0),col(pairs),col(2*pairs),pl.BlockSpec((t,2*GRID),lambda i:(0,0)),
          pl.BlockSpec((2,2*GRID,4*GRID),lambda i:(lo+i,0,0)),pl.BlockSpec((1,2,4*BLK),lambda i:(lo+i,0,0)),
          pl.BlockSpec((1,2,2*BLK),lambda i:(lo+i,0,0)),pl.BlockSpec((t,t),lambda i:(0,0))],
        out_specs=[pl.BlockSpec((t,2*HEAD),lambda i:(0,i)),pl.BlockSpec((2,t,t),lambda i:(i,0,0))],
        out_shape=[jax.ShapeDtypeStruct((t,2*HEAD*n),bf),jax.ShapeDtypeStruct((2*n,t,t),f4)],
        compiler_params=pltpu.CompilerParams(vmem_limit_bytes=48<<20),
        cost_estimate=pl.CostEstimate(flops=7_000_000_000*n//8,bytes_accessed=24_000_000*n//8,transcendentals=4_200_000*n//8),
        name="attend_forward")(qkv,qkv,qkv,oh,ff,w,far,mask)

def bwd(qkv,g,oh,oht,p,lo,n):
    t=qkv.shape[0]; pairs=HEADS//2
    col=lambda off: pl.BlockSpec((t,2*HEAD),lambda i,off=off:(0,off+lo+i))
    return pl.pallas_call(bwd_kernel,grid=(n,),
        in_specs=[col(0),col(pairs),col(2*pairs),col(0),pl.BlockSpec((t,2*GRID),lambda i:(0,0)),pl.BlockSpec((2*GRID,t),lambda i:(0,0)),
          pl.BlockSpec((2,t,t),lambda i:(i,0,0))],
        out_specs=[pl.BlockSpec((3,t,2*HEAD),lambda i:(0,0,i)),pl.BlockSpec((1,2,6*BLK),lambda i:(i,0,0)),pl.BlockSpec((1,4,2*GRID),lambda i:(i,0,0))],
        out_shape=[jax.ShapeDtypeStruct((3,t,2*HEAD*n),bf),jax.ShapeDtypeStruct((n,2,6*BLK),f4),jax.ShapeDtypeStruct((n,4,2*GRID),f4)],
        scratch_shapes=[pltpu.VMEM((t,t),bf),pltpu.VMEM((t,t),bf)],
        compiler_params=pltpu.CompilerParams(vmem_limit_bytes=48<<20),
        cost_estimate=pl.CostEstimate(flops=9_000_000_000*n//8,bytes_accessed=24_000_000*n//8,transcendentals=0),
        name="attend_backward")(qkv,qkv,qkv,g,oh,oht,p)

HI=lax.Precision.HIGHEST
def hot(n):
    return (np_bucket(n)[None,:]==np.arange(32)[:,None]).astype(np.float32)
N_GRID=(np.arange(GRID)[:,None]-np.arange(GRID)[None,:]).reshape(-1)
_m=np.arange(512); N_BAND=128-np.where(_m>=385,_m-512,_m)
def tables(rel,lay):
    w=jnp.einsum("bh,bn->hn",rel,jnp.asarray(hot(N_BAND)),precision=HI).reshape(8,2,512)
    far=jnp.concatenate([jnp.broadcast_to(rel[15][:,None],(16,128)),jnp.broadcast_to(rel[31][:,None],(16,128))],1).reshape(8,2,256)
    f=[jnp.einsum("bh,bn->hn",lay[32*i:32*i+32],jnp.asarray(hot(N_GRID)),precision=HI).reshape(16,64,64) for i in range(2)]
    z=jnp.zeros((16,64,64),f4)
    full=jnp.concatenate([jnp.concatenate([f[0],z],2),jnp.concatenate([z,f[1]],2)],1)
    hi=full.astype(bf)
    hi32=lax.reduce_precision(full,8,7)
    lo=(full-hi32).astype(bf)
    return w,far,jnp.concatenate([hi,lo],2)
def table_grads(relsum,laysum):
    rs=relsum.reshape(16,768); ls=laysum.reshape(16,2,128)
    oh=hot(N_BAND); oh[:,384]=0
    e15=np.zeros((32,128),np.float32); e15[15]=1
    e31=np.zeros((32,128),np.float32); e31[31]=1
    C=np.concatenate([oh,e15,e31],1)
    grel=jnp.einsum("bn,hn->bh",jnp.asarray(C),rs,precision=HI)
    m=np.arange(128); nn=63-m
    oh2=hot(nn); oh2[:,127]=0
    glay=jnp.einsum("bn,hxn->xbh",jnp.asarray(oh2),ls,precision=HI).reshape(64,16)
    return grel,glay

epsilon = 1e-06
masked_score = -1e30
AXES = ("wide", "narrow")
VMEM_LIMIT = 58 << 20
TILE = 256


def tie(values, *after):
    return lax.optimization_barrier((values, after))[0]


class Cube:
    def __init__(self, mesh):
        self.n = mesh.shape["wide"] * mesh.shape["narrow"]
        self.bits = self.n.bit_length() - 1
        self.per_wide = mesh.shape["narrow"]
        self.far = self.n // 8

    def me(self):
        return (lax.axis_index("wide") * self.per_wide + lax.axis_index("narrow")).astype(jnp.int32)

    def swap(self, x, mask):
        return lax.ppermute(x, AXES, [(i, i ^ mask) for i in range(self.n)])

    def far_first(self, own):
        return [own[None], self.swap(own[None], self.n // 2)]

    def far_rest(self, blocks):
        for b in range(self.bits - 2, 2, -1):
            cur = jnp.concatenate(blocks, 0)
            blocks = [cur, self.swap(cur, 1 << b)]
        return blocks

    def far_rel(self):
        rel = [0]
        for b in range(self.bits - 1, 2, -1):
            rel = rel + [d ^ (1 << b) for d in rel]
        return rel

    def step_a(self, pair):
        return [self.swap(pair[0], 2), self.swap(pair[1], 4)]

    def step_b(self, pair):
        return [self.swap(pair[0], 4), self.swap(pair[1], 2)]

    def joined(self, pair, got):
        return [jnp.concatenate([x, g], 0) for x, g in zip(pair, got)]

    def step_core(self, pair):
        return [self.swap(x, 1) for x in pair]

    def pieces(self, pair, cores):
        out = []
        for x, g, masks in zip(pair, cores, ((2, 4), (4, 2))):
            rel = self.far_rel()
            for m in masks:
                rel = rel + [d ^ m for d in rel]
            out.append([(x, rel), (g, [d ^ 1 for d in rel])])
        return out

    def plan(self, parts, bands):
        flat, steps, col = [], [], 0
        for pieces in parts:
            mine = []
            for arr, rel in pieces:
                for j, d in enumerate(rel):
                    for k, (r0, r) in enumerate(bands):
                        mine.append((len(flat), j, d, r0, r, k, col, arr.shape[2]))
                flat.append(arr)
            col += pieces[0][0].shape[2]
            steps.append(mine)
        return flat, steps, col

    def assemble(self, parts, bands):
        flat, steps, col = self.plan(parts, bands)
        count = sum(len(x) for x in steps)

        def kernel(me_ref, *refs):
            outs, sem = refs[len(flat) : len(flat) + len(bands)], refs[-1]
            copies = []
            for at, j, d, r0, r, k, c0, w in [x for mine in steps for x in mine]:
                copies.append(
                    pltpu.make_async_copy(
                        refs[at].at[j, pl.ds(r0, r)],
                        outs[k].at[me_ref[0] ^ d, :, pl.ds(c0, w)],
                        sem.at[len(copies)],
                    )
                )
            for c in copies:
                c.start()
            for c in copies:
                c.wait()

        outs = pl.pallas_call(
            kernel,
            grid_spec=pltpu.PrefetchScalarGridSpec(
                num_scalar_prefetch=1,
                grid=(1,),
                in_specs=[pl.BlockSpec(memory_space=pl.ANY)] * len(flat),
                out_specs=[pl.BlockSpec((self.n, r, col), lambda i, m: (0, 0, 0)) for _, r in bands],
                scratch_shapes=[pltpu.SemaphoreType.DMA((count,))],
            ),
            out_shape=[jax.ShapeDtypeStruct((self.n, r, col), bf) for _, r in bands],
            compiler_params=pltpu.CompilerParams(vmem_limit_bytes=VMEM_LIMIT),
            cost_estimate=pl.CostEstimate(
                flops=0, bytes_accessed=4 * self.n * col * sum(r for _, r in bands), transcendentals=0
            ),
            name="assemble",
        )(self.me()[None], *flat)
        return [o.reshape(-1, col) for o in outs]

    def project(self, x, parts):
        r = parts[0][0][0].shape[1]
        t, d = x.shape
        if r % 16:
            [whole] = self.assemble(parts, [(0, r)])
            return jnp.dot(x, whole, preferred_element_type=f4).astype(bf), whole
        flat, steps, col = self.plan(parts, [(0, r)])
        count = sum(len(m) for m in steps)
        tile = 512

        def kernel(me_ref, x_ref, *refs):
            y_ref, w_ref, held, sem, out_sem = refs[len(flat) :]
            todo, k = [], 0
            for mine in steps:
                copies = []
                for at, j, d_, _, _, _, c0, w in mine:
                    copies.append(
                        pltpu.make_async_copy(
                            refs[at].at[j], held.at[me_ref[0] ^ d_, :, pl.ds(c0, w)], sem.at[k]
                        )
                    )
                    k += 1
                for c in copies:
                    c.start()
                todo.append(copies)
            writes = []
            for mine, copies in zip(steps, todo):
                c0, w = mine[0][6], mine[0][7]
                for c in copies:
                    c.wait()
                write = pltpu.make_async_copy(
                    held.at[:, :, pl.ds(c0, w)], w_ref.at[:, :, pl.ds(c0, w)], out_sem.at[len(writes)]
                )
                write.start()
                writes.append(write)
                for c in range(c0, c0 + w, tile):
                    block = held[:, :, c : c + tile].reshape(d, tile)
                    y_ref[:, c : c + tile] = dot(x_ref[...], block).astype(bf)
            for write in writes:
                write.wait()

        y, whole = pl.pallas_call(
            kernel,
            grid_spec=pltpu.PrefetchScalarGridSpec(
                num_scalar_prefetch=1,
                grid=(1,),
                in_specs=[pl.BlockSpec((t, d), lambda i, m: (0, 0))]
                + [pl.BlockSpec(memory_space=pl.ANY)] * len(flat),
                out_specs=[pl.BlockSpec((t, col), lambda i, m: (0, 0)), pl.BlockSpec(memory_space=pl.ANY)],
                scratch_shapes=[
                    pltpu.VMEM((self.n, r, col), bf),
                    pltpu.SemaphoreType.DMA((count,)),
                    pltpu.SemaphoreType.DMA((len(steps),)),
                ],
            ),
            out_shape=[jax.ShapeDtypeStruct((t, col), bf), jax.ShapeDtypeStruct((self.n, r, col), bf)],
            compiler_params=pltpu.CompilerParams(vmem_limit_bytes=VMEM_LIMIT),
            cost_estimate=pl.CostEstimate(
                flops=2 * t * d * col, bytes_accessed=4 * d * col + 2 * t * (d + col), transcendentals=0
            ),
            name="project",
        )(self.me()[None], x, *flat)
        return y, whole.reshape(d, col)

    def gated(self, x, whole, grad_ffn, down):
        t, d = x.shape
        ff = down.shape[0]

        def kernel(x_ref, w_ref, g_ref, down_ref, inner_ref, grad_ref):
            both = dot(x_ref[...], w_ref[...])
            grad_inner = dot(g_ref[...], down_ref[...], NT)
            inner, gate, up = gate_math(both[:, :TILE], both[:, TILE:], grad_inner)
            inner_ref[...] = inner
            grad_ref[:, :TILE] = gate
            grad_ref[:, TILE:] = up

        rows = pl.BlockSpec((t, d), lambda i: (0, 0))
        return pl.pallas_call(
            kernel,
            grid=(ff // TILE,),
            in_specs=[
                rows,
                pl.BlockSpec((d, 2 * TILE), lambda i: (0, i)),
                rows,
                pl.BlockSpec((TILE, d), lambda i: (i, 0)),
            ],
            out_specs=[
                pl.BlockSpec((t, TILE), lambda i: (0, i)),
                pl.BlockSpec((t, 2 * TILE), lambda i: (0, i)),
            ],
            out_shape=[jax.ShapeDtypeStruct((t, ff), bf), jax.ShapeDtypeStruct((t, 2 * ff), bf)],
            compiler_params=pltpu.CompilerParams(vmem_limit_bytes=VMEM_LIMIT),
            cost_estimate=pl.CostEstimate(
                flops=6 * t * d * ff, bytes_accessed=6 * d * ff + 6 * t * ff, transcendentals=t * ff
            ),
            name="gated",
        )(x, whole, grad_ffn, down)

    def places(self, p):
        out = [0]
        for m in [1 << b for b in range(self.bits - 1, 2, -1)] + [[2, 4], [4, 2]][p] + [1]:
            out = out + [d ^ m for d in out]
        return out

    def terms(self, x, dy, width=None, into=None):
        t, rows = x.shape
        if dy.ndim == 2:
            dy = dy[None]
        r, each = rows // self.n, dy.shape[2]
        half = dy.shape[0] * each // 2
        n = self.n
        if r % 8:
            g = jnp.concatenate([jnp.einsum("tf,td->fd", x, y, preferred_element_type=f4).astype(bf) for y in dy], 1)
            g = g.reshape((2,) * self.bits + (r, -1))
            for b in range(self.bits):
                g = jnp.where((self.me() >> b) & 1 == 1, jnp.flip(g, self.bits - 1 - b), g)
            last = self.bits - 1
            both = []
            for p, near in enumerate(((last - 2, last - 1), (last - 1, last - 2))):
                order = (last, *near, *range(last - 3, -1, -1), last + 1, last + 2)
                part = jnp.transpose(g[..., p * half : (p + 1) * half], order)
                both.append(part.reshape(n, r, half))
            both = jnp.stack(both)
            both = both[:, n // 2 :], both[:, : n // 2]
            if into is not None:
                return tuple(jnp.concatenate([a[..., : a.shape[-1] - half], b], -1) for a, b in zip(into, both))
            if width is not None:
                return tuple(jnp.pad(b, ((0, 0), (0, 0), (0, 0), (0, width - half))) for b in both)
            return both
        ordered = r % 16 == 0
        tile = max(c for c in range(128, half + 1, 128) if half % c == 0 and each % c == 0 and c * rows <= 1500000)
        chunk = 256
        per, across = half // tile, each // tile

        def kernel(me_ref, x_ref, y_ref, *refs):
            send_ref, keep_ref, turned, acc = refs[-4:]
            first = pl.program_id(0) == 0
            y_ = y_ref[0]

            def who(at):
                d0, d1 = self.places(0)[at], self.places(1)[at]
                return pl.multiple_of((me_ref[0] ^ jnp.where(first, d0, d1)) * r, r)

            if ordered:

                @pl.when((pl.program_id(0) == 0) & (pl.program_id(1) == 0))
                def _():
                    for c in range(0, rows, chunk):
                        acc[c : c + chunk, :] = x_ref[:, c : c + chunk].T

                @pl.when(pl.program_id(1) == 0)
                def _():
                    for at in range(n):
                        turned[at * r : (at + 1) * r, :] = acc[pl.ds(who(at), r), :]

                for c in range(0, rows, chunk):
                    out = dot(turned[c : c + chunk, :], y_).astype(bf)
                    for k in range(chunk // r):
                        at = c // r + k
                        ref = keep_ref if at < n // 2 else send_ref
                        ref[0, at % (n // 2)] = out[k * r : (k + 1) * r]
                return

            for c in range(0, rows, chunk):
                acc[c : c + chunk, :] = dot(x_ref[:, c : c + chunk], y_, (((0,), (0,)), ((), ())))
            for at in range(n):
                ref = keep_ref if at < n // 2 else send_ref
                ref[0, at % (n // 2)] = acc[pl.ds(who(at), r), :].astype(bf)

        if into is not None:
            width = into[0].shape[3]
        skip = 0 if into is None else (width - half) // tile
        out = pl.BlockSpec((1, n // 2, r, tile), lambda p, j, m: (p, 0, 0, skip + j))
        shape = jax.ShapeDtypeStruct((2, n // 2, r, width or half), bf)
        more = () if into is None else tuple(into)
        return pl.pallas_call(
            kernel,
            grid_spec=pltpu.PrefetchScalarGridSpec(
                num_scalar_prefetch=1,
                grid=(2, per),
                in_specs=[
                    pl.BlockSpec((t, rows), lambda p, j, m: (0, 0)),
                    pl.BlockSpec(
                        (1, t, tile), lambda p, j, m: ((p * per + j) // across, 0, (p * per + j) % across)
                    ),
                ]
                + [pl.BlockSpec(memory_space=pl.ANY)] * len(more),
                out_specs=[out, out],
                scratch_shapes=[
                    pltpu.VMEM((rows, t) if ordered else (8, 128), bf),
                    pltpu.VMEM((rows, t), bf) if ordered else pltpu.VMEM((rows, tile), f4),
                ],
            ),
            out_shape=[shape, shape],
            input_output_aliases={} if into is None else {3: 0, 4: 1},
            compiler_params=pltpu.CompilerParams(vmem_limit_bytes=VMEM_LIMIT),
            cost_estimate=pl.CostEstimate(
                flops=4 * t * rows * half, bytes_accessed=2 * (t * rows + 2 * t * half + 2 * rows * half), transcendentals=0
            ),
            name="terms",
        )(self.me()[None], x, dy, *more)

    def plus(self, a, b):
        return a.astype(f4) + b.astype(f4)

    def split_a(self, keep, got):
        h = self.n // 4

        def side(p, lo, hi):
            return self.plus(keep[p, lo:hi], got[p, lo:hi]).astype(bf)

        return [side(p, h, 2 * h) for p in range(2)], [side(p, 0, h) for p in range(2)]

    def send_a(self, sends):
        return [self.swap(sends[0], 4), self.swap(sends[1], 2)]

    def split_b(self, keeps, gots):
        h = self.n // 8
        sends = [self.plus(k[h:], g[h:]).astype(bf) for k, g in zip(keeps, gots)]
        return sends, [self.plus(k[:h], g[:h]) for k, g in zip(keeps, gots)]

    def send_b(self, sends):
        return [self.swap(sends[0], 2), self.swap(sends[1], 4)]

    def split_far(self, keeps, gots):
        h = self.far // 2

        def both(lo, hi):
            return jnp.concatenate([self.plus(k[lo:hi], g[lo:hi]) for k, g in zip(keeps, gots)], -1)

        return both(h, 2 * h).astype(bf), both(0, h)

    def far_step(self, keep, got):
        h = keep.shape[0] // 2
        return self.plus(keep[h:], got[h:]).astype(bf), self.plus(keep[:h], got[:h])

    def far_send(self, send):
        return self.swap(send, self.n // 2 // send.shape[0])

    def far_end(self, keep, got):
        while keep.shape[0] > 2:
            send, keep = self.far_step(keep, got)
            got = self.far_send(send)
        return self.far_step(keep, got)

    def total(self, own, got):
        return self.plus(own, got)[0]


def moved(name, moves, ins, outs):
    def kernel(*refs):
        for i, src, o, dst in moves:
            refs[len(ins) + o][dst] = refs[i][src]

    return pl.pallas_call(
        kernel,
        out_shape=[jax.ShapeDtypeStruct(x, bf) for x in outs],
        compiler_params=pltpu.CompilerParams(vmem_limit_bytes=VMEM_LIMIT),
        cost_estimate=pl.CostEstimate(
            flops=0, bytes_accessed=sum(2 * x.size for x in ins) + sum(2 * int(np.prod(x)) for x in outs), transcendentals=0
        ),
        name=name,
    )(*ins)


def packed(query, key, value, out, gate, up):
    every = slice(None)
    moves = []
    at = 0
    for i, x in enumerate((query, key, value)):
        moves.append((i, (every, every), 0, (every, slice(at, at + x.shape[1]))))
        at += x.shape[1]
    ff = gate.shape[1]
    for c in range(0, ff, TILE):
        moves.append((3, (every, slice(c, c + TILE)), 1, (every, slice(2 * c, 2 * c + TILE))))
        moves.append((4, (every, slice(c, c + TILE)), 1, (every, slice(2 * c + TILE, 2 * c + 2 * TILE))))
    moves.append((5, (every, every), 1, (every, slice(2 * ff, 2 * ff + out.shape[1]))))
    shapes = [(query.shape[0], at), (gate.shape[0], 2 * ff + out.shape[1])]
    return moved("pack", moves, (query, key, value, gate, up, out), shapes)


def stacked(blocks):
    ins, moves, at = [], [], 0
    half = blocks[0].shape[2] // 2
    for x in blocks:
        for p in range(2):
            cols = slice(p * half, (p + 1) * half)
            moves.append(
                (len(ins), (slice(None), slice(None), cols), p, (slice(at, at + x.shape[0]), slice(None), slice(None)))
            )
        ins.append(x)
        at += x.shape[0]
    return moved("stack", moves, tuple(ins), [(at, blocks[0].shape[1], half)] * 2)


def rms_norm(values, gains):
    factor = lax.rsqrt(jnp.mean(values * values, axis=-1, keepdims=True) + epsilon)
    return values * factor * gains


def gate_math(gate, up, grad_inner):
    c = 0.7978845608028654
    square = gate * gate
    t = jnp.tanh(c * gate * (1.0 + 0.044715 * square))
    half = 0.5 * (1.0 + t)
    act = gate * half
    slope = half + 0.5 * gate * (1.0 - t * t) * (c * (1.0 + 3.0 * 0.044715 * square))
    return (act * up).astype(bf), (grad_inner * up * slope).astype(bf), (grad_inner * act).astype(bf)


def make_body(cube):
    def body(
        tokens, gain_one, query_weight, key_weight, value_weight, out_weight, gain_two, gate_weight,
        up_weight, down_weight, relative_bias_table, layout_bias_table, doc_lengths, box_x, box_y, cotangent,
    ):
        row_count, d = tokens.shape
        pairs = HEADS // 2
        own1, own3 = packed(query_weight, key_weight, value_weight, out_weight, gate_weight, up_weight)
        own2 = down_weight
        guo_full = lax.all_gather(own3, AXES, axis=0, tiled=True)
        far1 = cube.far_first(own1)

        positions = jnp.arange(row_count, dtype=jnp.int32)
        slots = jnp.arange(doc_lengths.shape[1], dtype=jnp.int32)
        doc_ends = jnp.sum(jnp.where(slots[:, None] <= slots[None, :], doc_lengths[0][:, None], 0), axis=0)
        live_rows = positions < doc_ends[-1]
        doc_ids = jnp.sum((positions[:, None] >= doc_ends[None, :]).astype(jnp.int32), axis=1)
        seg_ids = jnp.where(live_rows, doc_ids, doc_lengths.shape[1] + positions)
        live_mask = live_rows.astype(f4)[:, None]
        mask = jnp.where(seg_ids[:, None] == seg_ids[None, :], 0.0, masked_score).astype(f4)
        levels = jnp.arange(GRID, dtype=jnp.int32)
        hots = jnp.concatenate([box_x[:, None] == levels, box_y[:, None] == levels], 1).astype(bf)
        down_hots = jnp.concatenate(
            [box_x[None] == levels[::-1, None], box_y[None] == levels[::-1, None]], 0
        ).astype(bf)
        bands, far, values = tables(relative_bias_table, layout_bias_table)
        inputs_wide = tokens.astype(f4)
        normed_wide, norm_one_back = jax.vjp(rms_norm, inputs_wide, gain_one)
        normed = normed_wide.astype(bf)
        grad_output = cotangent.astype(f4)
        grad_ffn = (live_mask * grad_output).astype(bf)

        far1, own2, normed, mask, hots, down_hots, bands, far, values, grad_ffn = tie(
            (far1, own2, normed, mask, hots, down_hots, bands, far, values, grad_ffn)
        )
        far1 = cube.far_rest(far1)
        far1, own2 = tie((far1, own2))
        pair1 = stacked(far1)
        own2 = tie(own2, pair1)
        got1 = cube.step_a(pair1)
        far2 = cube.far_first(own2)
        got1, far2 = tie((got1, far2))
        pair1 = cube.joined(pair1, got1)
        got1 = cube.step_b(pair1)
        far2 = cube.far_rest(tie(far2, pair1))
        got1, far2 = tie((got1, far2))
        pair1 = cube.joined(pair1, got1)
        core1 = cube.step_core(pair1)
        pair2 = stacked(far2)
        got2 = cube.step_a(pair2)
        normed_ = tie(normed, pair2)
        qkv, qkv_full = cube.project(normed_, cube.pieces(pair1, core1))
        got2, qkv = tie((got2, qkv))
        pair2 = cube.joined(pair2, got2)
        got2 = cube.step_b(pair2)
        qkv_ = tie(qkv, pair2)
        attended, probs = fwd(qkv_, hots, values, bands, far, mask, 0, pairs)
        got2, attended = tie((got2, attended))
        pair2 = cube.joined(pair2, got2)
        core2 = cube.step_core(pair2)
        guo_full, attended = tie((guo_full, attended), pair2)
        ff2 = 2 * gate_weight.shape[1]
        gu_full, out_full = guo_full[:, :ff2], guo_full[:, ff2:]
        branch = jnp.dot(attended, out_full, preferred_element_type=f4)
        hidden = inputs_wide + live_mask * branch
        normed_two_wide, norm_two_back = jax.vjp(rms_norm, hidden, gain_two)
        normed_two = normed_two_wide.astype(bf)
        [down_full] = cube.assemble(cube.pieces(pair2, core2), [(0, down_weight.shape[0])])
        inner_rows, grad_gu = cube.gated(normed_two, guo_full, grad_ffn, down_full)

        send_d, keep_d = cube.terms(inner_rows, grad_ffn)
        got_d = cube.swap(send_d, 1)
        grad_gu_ = tie(grad_gu, send_d)
        send_g, keep_g = cube.terms(normed_two, grad_gu_)
        got_d, send_g, keep_g = tie((got_d, send_g, keep_g))
        got_g = cube.swap(send_g, 1)
        sends_d, keeps_d = cube.split_a(keep_d, got_d)
        got_d = cube.send_a(sends_d)
        gu_full_, grad_gu_ = tie((gu_full, grad_gu_), send_g, sends_d)
        grad_normed_two = jnp.einsum("tf,df->td", grad_gu_, gu_full_, preferred_element_type=f4)
        got_g, grad_normed_two = tie((got_g, grad_normed_two))
        sends_g, keeps_g = cube.split_a(keep_g, got_g)
        got_d, sends_g, grad_normed_two = tie((got_d, sends_g, grad_normed_two))
        sends_d, keeps_d = cube.split_b(keeps_d, got_d)
        got_d = cube.send_b(sends_d)
        got_g = cube.send_a(sends_g)
        grad_normed_two = tie(grad_normed_two, sends_d)
        grad_hidden_part, grad_gain_two = norm_two_back(grad_normed_two)
        grad_hidden = grad_output + grad_hidden_part
        grad_branch = (live_mask * grad_hidden).astype(bf)
        grad_attended = jnp.einsum("td,ed->te", grad_branch, out_full, preferred_element_type=f4).astype(bf)
        grad_qkv, rel_sums, lay_sums = bwd(qkv, grad_attended, hots, down_hots, probs, 0, pairs)
        send_q, keep_q = cube.terms(normed, grad_qkv, 2 * d)
        send_q, keep_q = cube.terms(attended, grad_branch, into=(send_q, keep_q))
        got_g, got_d, send_q, keep_q = tie((got_g, got_d, send_q, keep_q))
        sends_g, keeps_g = cube.split_b(keeps_g, got_g)
        got_g = cube.send_b(sends_g)
        got_q = cube.swap(send_q, 1)
        keeps_d, got_d = tie((keeps_d, got_d), sends_g)
        send_d, own_d = cube.split_far(keeps_d, got_d)
        far_d = cube.far_send(send_d)
        grad_qkv = tie(grad_qkv, sends_g)
        grad_normed = jnp.zeros((), f4)
        for i in range(3):
            grad_normed = grad_normed + jnp.einsum(
                "te,de->td", grad_qkv[i], qkv_full[:, i * d : (i + 1) * d], preferred_element_type=f4
            )
        grad_input_part, grad_gain_one = norm_one_back(grad_normed)
        grad_tokens = grad_hidden + grad_input_part
        grad_rel_table, grad_layout_table = table_grads(rel_sums, lay_sums)
        small = jnp.concatenate(
            [grad_gain_one, grad_gain_two, grad_rel_table.reshape(-1), grad_layout_table.reshape(-1)]
        ).reshape(-1, 128)
        own_d, far_d, got_q, grad_tokens, small = tie((own_d, far_d, got_q, grad_tokens, small))
        send_d, own_d = cube.far_end(own_d, far_d)
        far_d = cube.far_send(send_d)
        got_s = cube.swap(small, 1)
        sends_q, keeps_q = cube.split_a(keep_q, got_q)
        got_g, sends_q, grad_tokens, small, got_s = tie((got_g, sends_q, grad_tokens, small, got_s))
        small = small + got_s
        got_q = cube.send_a(sends_q)
        keeps_g, got_g, small = tie((keeps_g, got_g, small), sends_q)
        send_g, own_g = cube.split_far(keeps_g, got_g)
        far_g = cube.far_send(send_g)
        got_s = cube.swap(small, 2)
        inner_ = tie(inner_rows, send_g)
        ffn_rows = jnp.dot(inner_, down_full, preferred_element_type=f4)
        block_out = (hidden + live_mask * ffn_rows).astype(bf)
        far_g, far_d, block_out = tie((far_g, far_d, block_out))
        send_g, own_g = cube.far_end(own_g, far_g)
        far_g = cube.far_send(send_g)
        got_q, small, got_s = tie((got_q, small, got_s), send_g)
        sends_q, keeps_q = cube.split_b(keeps_q, got_q)
        got_q = cube.send_b(sends_q)
        small = small + got_s
        got_s = cube.swap(small, 4)
        share_down = cube.total(*tie((own_d, far_d), sends_q))
        got_q, small, got_s = tie((got_q, small, got_s))
        send_q, own_q = cube.split_far(keeps_q, got_q)
        far_q = cube.far_send(send_q)
        small = small + got_s
        for b in range(3, cube.bits - 1):
            small = small + cube.swap(small, 1 << b)
        own_g, far_g = tie((own_g, far_g), send_q)
        share_gu = cube.total(own_g, far_g)
        far_q, small = tie((far_q, small))
        send_q, own_q = cube.far_end(own_q, far_q)
        far_q = cube.far_send(send_q)
        small = (small + cube.swap(small, cube.n // 2)).reshape(-1)
        share_q = cube.total(own_q, far_q)
        c = gate_weight.shape[1]
        share_gate = jnp.concatenate([share_gu[:, 2 * i : 2 * i + TILE] for i in range(0, c, TILE)], 1)
        share_up = jnp.concatenate([share_gu[:, 2 * i + TILE : 2 * i + 2 * TILE] for i in range(0, c, TILE)], 1)
        wide = 3 * d // 2
        left, right = share_q[:, : wide + d // 2], share_q[:, wide + d // 2 :]
        share_qkv = jnp.concatenate([left[:, :wide], right[:, :wide]], 1)
        share_out = jnp.concatenate([left[:, wide:], right[:, wide:]], 1)
        rel_n, lay_n = relative_bias_table.size, layout_bias_table.size
        return (
            block_out,
            grad_tokens,
            small[:d],
            share_qkv[:, :d],
            share_qkv[:, d : 2 * d],
            share_qkv[:, 2 * d :],
            share_out,
            small[d : 2 * d],
            share_gate,
            share_up,
            share_down,
            small[2 * d : 2 * d + rel_n].reshape(relative_bias_table.shape),
            small[2 * d + rel_n : 2 * d + rel_n + lay_n].reshape(layout_bias_table.shape),
        )

    return body


def solution(mesh):
    rows = P(AXES, None)
    line = P(AXES)
    whole = P()
    return jax.shard_map(
        make_body(Cube(mesh)),
        mesh=mesh,
        in_specs=(
            rows, whole, rows, rows, rows, rows, whole, rows, rows, rows, whole, whole, rows, line, line, rows,
        ),
        out_specs=(
            rows, rows, whole, rows, rows, rows, rows, whole, rows, rows, rows, whole, whole,
        ),
        check_vma=False,
    )
```

```python
import numpy as np
import jax
import jax.numpy as jnp
from jax import lax
from jax.experimental import pallas as pl
from jax.experimental.pallas import tpu as pltpu
from jax.sharding import PartitionSpec as P

bf = jnp.bfloat16
f4 = jnp.float32

HEADS,HEAD=16,64
bucket_edges=(1,2,3,4,5,6,7,8,12,16,23,32,46,64,91)
GRID=64
def np_bucket(n):
    n=np.asarray(n); m=np.abs(n)
    b=np.zeros(n.shape,np.int32)
    for e in bucket_edges: b+=(m>=e)
    return b+(n>0)*16
BLK=128
NT=(((1,),(1,)),((),()))
NN=(((1,),(0,)),((),()))
def dot(a,b,dims=NN): return lax.dot_general(a,b,dims,preferred_element_type=f4)

def fwd_kernel(q_ref,k_ref,v_ref,oh_ref,ff_ref,w_ref,far_ref,mask_ref,o_ref,p_ref):
    t=q_ref.shape[0]; nb=t//BLK
    lane=lax.broadcasted_iota(jnp.int32,(t,2*HEAD),1)
    q=q_ref[...]; oh=oh_ref[...]; v=v_ref[...]
    oht=oh.T; ka=jnp.concatenate([k_ref[...].T,oht,oht],axis=0)
    for j in range(2):
        mine=(lane<HEAD) if j==0 else (lane>=HEAD)
        band=pltpu.roll(jnp.broadcast_to(w_ref[0,j:j+1,:],(BLK,4*BLK)),0,1,stride=1,stride_axis=0)
        near=far_ref[0,j:j+1,0:BLK]; past=far_ref[0,j:j+1,BLK:2*BLK]
        rows=dot(oh,ff_ref[j]).astype(bf)
        qa=jnp.concatenate([jnp.where(mine,q,jnp.zeros_like(q)),rows],axis=1)
        whole=dot(qa,ka)
        for s in range(nb):
            sc=whole[s*BLK:(s+1)*BLK]
            rel=[]
            for c in range(nb):
                if c<s-1: rel.append(jnp.broadcast_to(past,(BLK,BLK)))
                elif c>s+1: rel.append(jnp.broadcast_to(near,(BLK,BLK)))
                else: rel.append(band[:,(c-s+1)*BLK:(c-s+2)*BLK])
            sc=(sc+jnp.concatenate(rel,axis=1))+mask_ref[s*BLK:(s+1)*BLK,:]
            top=jnp.max(sc,axis=1,keepdims=True)
            e=jnp.exp(sc-top)
            p=e*(1.0/jnp.sum(e,axis=1,keepdims=True))
            p_ref[j,s*BLK:(s+1)*BLK,:]=p
            o=dot(p.astype(bf),v).astype(bf)
            o_ref[s*BLK:(s+1)*BLK,j*HEAD:(j+1)*HEAD]=o[:,j*HEAD:(j+1)*HEAD]

def bwd_kernel(q_ref,k_ref,v_ref,g_ref,oh_ref,oht_ref,p_ref,d_ref,rel_ref,lay_ref,ds_s,pb_s):
    t=q_ref.shape[0]; nb=t//BLK
    lane=lax.broadcasted_iota(jnp.int32,(t,2*HEAD),1)
    q=q_ref[...]; k=k_ref[...]; v=v_ref[...]; g=g_ref[...]; oh=oh_ref[...]
    koh=jnp.concatenate([k,oh],axis=1)
    qt=q.T; gt=g.T; vt=v.T
    outs=[]
    for j in range(2):
        mine=(lane<HEAD) if j==0 else (lane>=HEAD)
        gm=jnp.where(mine,g,jnp.zeros_like(g))
        band=[jnp.zeros((BLK,BLK),f4) for _ in range(3)]
        past=jnp.zeros((BLK,BLK),f4); near=jnp.zeros((BLK,BLK),f4)
        whole=dot(gm,vt)
        for s in range(nb):
            rows=slice(s*BLK,(s+1)*BLK)
            dp=whole[rows]
            p=p_ref[j,rows,:]
            ds=p*(dp-jnp.sum(p*dp,axis=1,keepdims=True))
            for c in range(nb):
                tile=ds[:,c*BLK:(c+1)*BLK]
                if c<s-1: past=past+tile
                elif c>s+1: near=near+tile
                else: band[c-s+1]=band[c-s+1]+tile
            dsb=ds.astype(bf)
            ds_s[rows,:]=dsb; pb_s[rows,:]=p.astype(bf)
        dq=dot(ds_s[...],koh)
        dkt=dot(qt,ds_s[...]); dvt=dot(gt,pb_s[...])
        outs.append((dq[:,:2*HEAD],dkt,dvt))
        r=dq[:,2*HEAD:]
        hi=r.astype(bf); lo=(r-hi.astype(f4)).astype(bf)
        gl=dot(oht_ref[...],jnp.concatenate([hi,lo],axis=1))
        gl=gl[:,:2*GRID]+gl[:,2*GRID:]
        for i in range(2):
            part=gl[i*GRID:(i+1)*GRID,i*GRID:(i+1)*GRID]
            part=pltpu.roll(jnp.concatenate([part,jnp.zeros((GRID,GRID),f4)],axis=1),0,1,stride=1,stride_axis=0)
            lay_ref[0,2*j+i:2*j+i+1,:]=jnp.sum(part,axis=0,keepdims=True)
        wide=jnp.concatenate(band+[jnp.zeros((BLK,BLK),f4)],axis=1)
        acc=wide[0:8]
        for i in range(1,BLK//8):
            acc=acc+pltpu.roll(wide[8*i:8*i+8],4*BLK-8*i,1)
        line=acc[0:1]
        for i in range(1,8):
            line=line+pltpu.roll(acc[i:i+1],4*BLK-i,1)
        rel_ref[0,j:j+1,0:4*BLK]=line
        rel_ref[0,j:j+1,4*BLK:5*BLK]=jnp.sum(near,axis=0,keepdims=True)
        rel_ref[0,j:j+1,5*BLK:6*BLK]=jnp.sum(past,axis=0,keepdims=True)
    d_ref[0]=jnp.where(lane<HEAD,outs[0][0],outs[1][0]).astype(bf)
    sub=lax.broadcasted_iota(jnp.int32,(2*HEAD,t),0)
    d_ref[1]=jnp.where(sub<HEAD,outs[0][1],outs[1][1]).astype(bf).T
    d_ref[2]=jnp.where(sub<HEAD,outs[0][2],outs[1][2]).astype(bf).T

def fwd(qkv,oh,ff,w,far,mask,lo,n):
    t=qkv.shape[0]; pairs=HEADS//2
    col=lambda off: pl.BlockSpec((t,2*HEAD),lambda i,off=off:(0,off+lo+i))
    return pl.pallas_call(fwd_kernel,grid=(n,),
        in_specs=[col(0),col(pairs),col(2*pairs),pl.BlockSpec((t,2*GRID),lambda i:(0,0)),
          pl.BlockSpec((2,2*GRID,4*GRID),lambda i:(lo+i,0,0)),pl.BlockSpec((1,2,4*BLK),lambda i:(lo+i,0,0)),
          pl.BlockSpec((1,2,2*BLK),lambda i:(lo+i,0,0)),pl.BlockSpec((t,t),lambda i:(0,0))],
        out_specs=[pl.BlockSpec((t,2*HEAD),lambda i:(0,i)),pl.BlockSpec((2,t,t),lambda i:(i,0,0))],
        out_shape=[jax.ShapeDtypeStruct((t,2*HEAD*n),bf),jax.ShapeDtypeStruct((2*n,t,t),f4)],
        compiler_params=pltpu.CompilerParams(vmem_limit_bytes=48<<20),
        cost_estimate=pl.CostEstimate(flops=7_000_000_000*n//8,bytes_accessed=24_000_000*n//8,transcendentals=4_200_000*n//8),
        name="attend_forward")(qkv,qkv,qkv,oh,ff,w,far,mask)

def bwd(qkv,g,oh,oht,p,lo,n):
    t=qkv.shape[0]; pairs=HEADS//2
    col=lambda off: pl.BlockSpec((t,2*HEAD),lambda i,off=off:(0,off+lo+i))
    return pl.pallas_call(bwd_kernel,grid=(n,),
        in_specs=[col(0),col(pairs),col(2*pairs),col(0),pl.BlockSpec((t,2*GRID),lambda i:(0,0)),pl.BlockSpec((2*GRID,t),lambda i:(0,0)),
          pl.BlockSpec((2,t,t),lambda i:(i,0,0))],
        out_specs=[pl.BlockSpec((3,t,2*HEAD),lambda i:(0,0,i)),pl.BlockSpec((1,2,6*BLK),lambda i:(i,0,0)),pl.BlockSpec((1,4,2*GRID),lambda i:(i,0,0))],
        out_shape=[jax.ShapeDtypeStruct((3,t,2*HEAD*n),bf),jax.ShapeDtypeStruct((n,2,6*BLK),f4),jax.ShapeDtypeStruct((n,4,2*GRID),f4)],
        scratch_shapes=[pltpu.VMEM((t,t),bf),pltpu.VMEM((t,t),bf)],
        compiler_params=pltpu.CompilerParams(vmem_limit_bytes=48<<20),
        cost_estimate=pl.CostEstimate(flops=9_000_000_000*n//8,bytes_accessed=24_000_000*n//8,transcendentals=0),
        name="attend_backward")(qkv,qkv,qkv,g,oh,oht,p)

HI=lax.Precision.HIGHEST
def hot(n):
    return (np_bucket(n)[None,:]==np.arange(32)[:,None]).astype(np.float32)
N_GRID=(np.arange(GRID)[:,None]-np.arange(GRID)[None,:]).reshape(-1)
_m=np.arange(512); N_BAND=128-np.where(_m>=385,_m-512,_m)
def tables(rel,lay):
    w=jnp.einsum("bh,bn->hn",rel,jnp.asarray(hot(N_BAND)),precision=HI).reshape(8,2,512)
    far=jnp.concatenate([jnp.broadcast_to(rel[15][:,None],(16,128)),jnp.broadcast_to(rel[31][:,None],(16,128))],1).reshape(8,2,256)
    f=[jnp.einsum("bh,bn->hn",lay[32*i:32*i+32],jnp.asarray(hot(N_GRID)),precision=HI).reshape(16,64,64) for i in range(2)]
    z=jnp.zeros((16,64,64),f4)
    full=jnp.concatenate([jnp.concatenate([f[0],z],2),jnp.concatenate([z,f[1]],2)],1)
    hi=full.astype(bf)
    hi32=lax.reduce_precision(full,8,7)
    lo=(full-hi32).astype(bf)
    return w,far,jnp.concatenate([hi,lo],2)
def table_grads(relsum,laysum):
    rs=relsum.reshape(16,768); ls=laysum.reshape(16,2,128)
    oh=hot(N_BAND); oh[:,384]=0
    e15=np.zeros((32,128),np.float32); e15[15]=1
    e31=np.zeros((32,128),np.float32); e31[31]=1
    C=np.concatenate([oh,e15,e31],1)
    grel=jnp.einsum("bn,hn->bh",jnp.asarray(C),rs,precision=HI)
    m=np.arange(128); nn=63-m
    oh2=hot(nn); oh2[:,127]=0
    glay=jnp.einsum("bn,hxn->xbh",jnp.asarray(oh2),ls,precision=HI).reshape(64,16)
    return grel,glay

epsilon = 1e-06
masked_score = -1e30
AXES = ("wide", "narrow")
VMEM_LIMIT = 58 << 20
TILE = 256


def tie(values, *after):
    return lax.optimization_barrier((values, after))[0]


class Cube:
    def __init__(self, mesh):
        self.n = mesh.shape["wide"] * mesh.shape["narrow"]
        self.bits = self.n.bit_length() - 1
        self.per_wide = mesh.shape["narrow"]
        self.far = self.n // 8

    def me(self):
        return (lax.axis_index("wide") * self.per_wide + lax.axis_index("narrow")).astype(jnp.int32)

    def swap(self, x, mask):
        return lax.ppermute(x, AXES, [(i, i ^ mask) for i in range(self.n)])

    def far_first(self, own):
        return [own[None], self.swap(own[None], self.n // 2)]

    def far_rest(self, blocks):
        for b in range(self.bits - 2, 2, -1):
            cur = jnp.concatenate(blocks, 0)
            blocks = [cur, self.swap(cur, 1 << b)]
        return blocks

    def far_rel(self):
        rel = [0]
        for b in range(self.bits - 1, 2, -1):
            rel = rel + [d ^ (1 << b) for d in rel]
        return rel

    def step_a(self, pair):
        return [self.swap(pair[0], 2), self.swap(pair[1], 4)]

    def step_b(self, pair):
        return [self.swap(pair[0], 4), self.swap(pair[1], 2)]

    def joined(self, pair, got):
        return [jnp.concatenate([x, g], 0) for x, g in zip(pair, got)]

    def step_core(self, pair):
        return [self.swap(x, 1) for x in pair]

    def pieces(self, pair, cores):
        out = []
        for x, g, masks in zip(pair, cores, ((2, 4), (4, 2))):
            rel = self.far_rel()
            for m in masks:
                rel = rel + [d ^ m for d in rel]
            out.append([(x, rel), (g, [d ^ 1 for d in rel])])
        return out

    def plan(self, parts, bands):
        flat, steps, col = [], [], 0
        for pieces in parts:
            mine = []
            for arr, rel in pieces:
                for j, d in enumerate(rel):
                    for k, (r0, r) in enumerate(bands):
                        mine.append((len(flat), j, d, r0, r, k, col, arr.shape[2]))
                flat.append(arr)
            col += pieces[0][0].shape[2]
            steps.append(mine)
        return flat, steps, col

    def assemble(self, parts, bands):
        flat, steps, col = self.plan(parts, bands)
        count = sum(len(x) for x in steps)

        def kernel(me_ref, *refs):
            outs, sem = refs[len(flat) : len(flat) + len(bands)], refs[-1]
            copies = []
            for at, j, d, r0, r, k, c0, w in [x for mine in steps for x in mine]:
                copies.append(
                    pltpu.make_async_copy(
                        refs[at].at[j, pl.ds(r0, r)],
                        outs[k].at[me_ref[0] ^ d, :, pl.ds(c0, w)],
                        sem.at[len(copies)],
                    )
                )
            for c in copies:
                c.start()
            for c in copies:
                c.wait()

        outs = pl.pallas_call(
            kernel,
            grid_spec=pltpu.PrefetchScalarGridSpec(
                num_scalar_prefetch=1,
                grid=(1,),
                in_specs=[pl.BlockSpec(memory_space=pl.ANY)] * len(flat),
                out_specs=[pl.BlockSpec((self.n, r, col), lambda i, m: (0, 0, 0)) for _, r in bands],
                scratch_shapes=[pltpu.SemaphoreType.DMA((count,))],
            ),
            out_shape=[jax.ShapeDtypeStruct((self.n, r, col), bf) for _, r in bands],
            compiler_params=pltpu.CompilerParams(vmem_limit_bytes=VMEM_LIMIT),
            cost_estimate=pl.CostEstimate(
                flops=0, bytes_accessed=4 * self.n * col * sum(r for _, r in bands), transcendentals=0
            ),
            name="assemble",
        )(self.me()[None], *flat)
        return [o.reshape(-1, col) for o in outs]

    def project(self, x, parts):
        r = parts[0][0][0].shape[1]
        t, d = x.shape
        if r % 16:
            [whole] = self.assemble(parts, [(0, r)])
            return jnp.dot(x, whole, preferred_element_type=f4).astype(bf), whole
        flat, steps, col = self.plan(parts, [(0, r)])
        count = sum(len(m) for m in steps)
        tile = 512

        def kernel(me_ref, x_ref, *refs):
            y_ref, w_ref, held, sem, out_sem = refs[len(flat) :]
            todo, k = [], 0
            for mine in steps:
                copies = []
                for at, j, d_, _, _, _, c0, w in mine:
                    copies.append(
                        pltpu.make_async_copy(
                            refs[at].at[j], held.at[me_ref[0] ^ d_, :, pl.ds(c0, w)], sem.at[k]
                        )
                    )
                    k += 1
                for c in copies:
                    c.start()
                todo.append(copies)
            writes = []
            for mine, copies in zip(steps, todo):
                c0, w = mine[0][6], mine[0][7]
                for c in copies:
                    c.wait()
                write = pltpu.make_async_copy(
                    held.at[:, :, pl.ds(c0, w)], w_ref.at[:, :, pl.ds(c0, w)], out_sem.at[len(writes)]
                )
                write.start()
                writes.append(write)
                for c in range(c0, c0 + w, tile):
                    block = held[:, :, c : c + tile].reshape(d, tile)
                    y_ref[:, c : c + tile] = dot(x_ref[...], block).astype(bf)
            for write in writes:
                write.wait()

        y, whole = pl.pallas_call(
            kernel,
            grid_spec=pltpu.PrefetchScalarGridSpec(
                num_scalar_prefetch=1,
                grid=(1,),
                in_specs=[pl.BlockSpec((t, d), lambda i, m: (0, 0))]
                + [pl.BlockSpec(memory_space=pl.ANY)] * len(flat),
                out_specs=[pl.BlockSpec((t, col), lambda i, m: (0, 0)), pl.BlockSpec(memory_space=pl.ANY)],
                scratch_shapes=[
                    pltpu.VMEM((self.n, r, col), bf),
                    pltpu.SemaphoreType.DMA((count,)),
                    pltpu.SemaphoreType.DMA((len(steps),)),
                ],
            ),
            out_shape=[jax.ShapeDtypeStruct((t, col), bf), jax.ShapeDtypeStruct((self.n, r, col), bf)],
            compiler_params=pltpu.CompilerParams(vmem_limit_bytes=VMEM_LIMIT),
            cost_estimate=pl.CostEstimate(
                flops=2 * t * d * col, bytes_accessed=4 * d * col + 2 * t * (d + col), transcendentals=0
            ),
            name="project",
        )(self.me()[None], x, *flat)
        return y, whole.reshape(d, col)

    def gated(self, x, whole, grad_ffn, down):
        t, d = x.shape
        ff = down.shape[0]

        def kernel(x_ref, w_ref, g_ref, down_ref, inner_ref, grad_ref):
            both = dot(x_ref[...], w_ref[...])
            grad_inner = dot(g_ref[...], down_ref[...], NT)
            inner, gate, up = gate_math(both[:, :TILE], both[:, TILE:], grad_inner)
            inner_ref[...] = inner
            grad_ref[:, :TILE] = gate
            grad_ref[:, TILE:] = up

        rows = pl.BlockSpec((t, d), lambda i: (0, 0))
        return pl.pallas_call(
            kernel,
            grid=(ff // TILE,),
            in_specs=[
                rows,
                pl.BlockSpec((d, 2 * TILE), lambda i: (0, i)),
                rows,
                pl.BlockSpec((TILE, d), lambda i: (i, 0)),
            ],
            out_specs=[
                pl.BlockSpec((t, TILE), lambda i: (0, i)),
                pl.BlockSpec((t, 2 * TILE), lambda i: (0, i)),
            ],
            out_shape=[jax.ShapeDtypeStruct((t, ff), bf), jax.ShapeDtypeStruct((t, 2 * ff), bf)],
            compiler_params=pltpu.CompilerParams(vmem_limit_bytes=VMEM_LIMIT),
            cost_estimate=pl.CostEstimate(
                flops=6 * t * d * ff, bytes_accessed=6 * d * ff + 6 * t * ff, transcendentals=t * ff
            ),
            name="gated",
        )(x, whole, grad_ffn, down)

    def places(self, p, far_first=False):
        out, far = [0], [1 << b for b in range(self.bits - 1, 2, -1)]
        for m in ([2, 4] + far if far_first else far + [[2, 4], [4, 2]][p]) + [1]:
            out = out + [d ^ m for d in out]
        return out

    def terms(self, x, dy, width=None, into=None, far_first=False):
        t, rows = x.shape
        if dy.ndim == 2:
            dy = dy[None]
        r, each = rows // self.n, dy.shape[2]
        half = dy.shape[0] * each // 2
        n = self.n
        if r % 8:
            g = jnp.concatenate([jnp.einsum("tf,td->fd", x, y, preferred_element_type=f4).astype(bf) for y in dy], 1)
            g = g.reshape((2,) * self.bits + (r, -1))
            for b in range(self.bits):
                g = jnp.where((self.me() >> b) & 1 == 1, jnp.flip(g, self.bits - 1 - b), g)
            last = self.bits - 1
            both = []
            for p, near in enumerate(((last - 2, last - 1), (last - 1, last - 2))):
                far = range(last - 3, -1, -1)
                order = (last, *far, last - 2, last - 1) if far_first else (last, *near, *far)
                order = (*order, last + 1, last + 2)
                part = jnp.transpose(g[..., p * half : (p + 1) * half], order)
                both.append(part.reshape(n, r, half))
            both = jnp.stack(both)
            both = both[:, n // 2 :], both[:, : n // 2]
            if into is not None:
                return tuple(jnp.concatenate([a[..., : a.shape[-1] - half], b], -1) for a, b in zip(into, both))
            if width is not None:
                return tuple(jnp.pad(b, ((0, 0), (0, 0), (0, 0), (0, width - half))) for b in both)
            return both
        ordered = r % 16 == 0
        tile = max(c for c in range(128, half + 1, 128) if half % c == 0 and each % c == 0 and c * rows <= 1500000)
        chunk = 256
        per, across = half // tile, each // tile

        def kernel(me_ref, x_ref, y_ref, *refs):
            send_ref, keep_ref, turned, acc = refs[-4:]
            first = pl.program_id(0) == 0
            y_ = y_ref[0]

            def who(at):
                d0, d1 = self.places(0, far_first)[at], self.places(1, far_first)[at]
                return pl.multiple_of((me_ref[0] ^ jnp.where(first, d0, d1)) * r, r)

            if ordered:

                @pl.when((pl.program_id(0) == 0) & (pl.program_id(1) == 0))
                def _():
                    for c in range(0, rows, chunk):
                        acc[c : c + chunk, :] = x_ref[:, c : c + chunk].T

                @pl.when(pl.program_id(1) == 0)
                def _():
                    for at in range(n):
                        turned[at * r : (at + 1) * r, :] = acc[pl.ds(who(at), r), :]

                for c in range(0, rows, chunk):
                    out = dot(turned[c : c + chunk, :], y_).astype(bf)
                    for k in range(chunk // r):
                        at = c // r + k
                        ref = keep_ref if at < n // 2 else send_ref
                        ref[0, at % (n // 2)] = out[k * r : (k + 1) * r]
                return

            for c in range(0, rows, chunk):
                acc[c : c + chunk, :] = dot(x_ref[:, c : c + chunk], y_, (((0,), (0,)), ((), ())))
            for at in range(n):
                ref = keep_ref if at < n // 2 else send_ref
                ref[0, at % (n // 2)] = acc[pl.ds(who(at), r), :].astype(bf)

        if into is not None:
            width = into[0].shape[3]
        skip = 0 if into is None else (width - half) // tile
        out = pl.BlockSpec((1, n // 2, r, tile), lambda p, j, m: (p, 0, 0, skip + j))
        shape = jax.ShapeDtypeStruct((2, n // 2, r, width or half), bf)
        more = () if into is None else tuple(into)
        return pl.pallas_call(
            kernel,
            grid_spec=pltpu.PrefetchScalarGridSpec(
                num_scalar_prefetch=1,
                grid=(2, per),
                in_specs=[
                    pl.BlockSpec((t, rows), lambda p, j, m: (0, 0)),
                    pl.BlockSpec(
                        (1, t, tile), lambda p, j, m: ((p * per + j) // across, 0, (p * per + j) % across)
                    ),
                ]
                + [pl.BlockSpec(memory_space=pl.ANY)] * len(more),
                out_specs=[out, out],
                scratch_shapes=[
                    pltpu.VMEM((rows, t) if ordered else (8, 128), bf),
                    pltpu.VMEM((rows, t), bf) if ordered else pltpu.VMEM((rows, tile), f4),
                ],
            ),
            out_shape=[shape, shape],
            input_output_aliases={} if into is None else {3: 0, 4: 1},
            compiler_params=pltpu.CompilerParams(vmem_limit_bytes=VMEM_LIMIT),
            cost_estimate=pl.CostEstimate(
                flops=4 * t * rows * half, bytes_accessed=2 * (t * rows + 2 * t * half + 2 * rows * half), transcendentals=0
            ),
            name="terms",
        )(self.me()[None], x, dy, *more)

    def plus(self, a, b):
        return a.astype(f4) + b.astype(f4)

    def split_a(self, keep, got):
        h = self.n // 4

        def side(p, lo, hi):
            return self.plus(keep[p, lo:hi], got[p, lo:hi]).astype(bf)

        return [side(p, h, 2 * h) for p in range(2)], [side(p, 0, h) for p in range(2)]

    def halve(self, keep, got, kind):
        h = keep.shape[1] // 2
        return self.plus(keep[:, h:], got[:, h:]).astype(bf), self.plus(keep[:, :h], got[:, :h]).astype(kind)

    def send_a(self, sends):
        return [self.swap(sends[0], 4), self.swap(sends[1], 2)]

    def split_b(self, keeps, gots):
        h = self.n // 8
        sends = [self.plus(k[h:], g[h:]).astype(bf) for k, g in zip(keeps, gots)]
        return sends, [self.plus(k[:h], g[:h]) for k, g in zip(keeps, gots)]

    def send_b(self, sends):
        return [self.swap(sends[0], 2), self.swap(sends[1], 4)]

    def split_far(self, keeps, gots):
        h = self.far // 2

        def both(lo, hi):
            return jnp.concatenate([self.plus(k[lo:hi], g[lo:hi]) for k, g in zip(keeps, gots)], -1)

        return both(h, 2 * h).astype(bf), both(0, h)

    def far_step(self, keep, got):
        h = keep.shape[0] // 2
        return self.plus(keep[h:], got[h:]).astype(bf), self.plus(keep[:h], got[:h])

    def far_send(self, send):
        return self.swap(send, self.n // 2 // send.shape[0])

    def far_end(self, keep, got):
        while keep.shape[0] > 2:
            send, keep = self.far_step(keep, got)
            got = self.far_send(send)
        return self.far_step(keep, got)

    def total(self, own, got):
        return self.plus(own, got)[0]


def moved(name, moves, ins, outs):
    def kernel(*refs):
        for i, src, o, dst in moves:
            refs[len(ins) + o][dst] = refs[i][src]

    return pl.pallas_call(
        kernel,
        out_shape=[jax.ShapeDtypeStruct(x, bf) for x in outs],
        compiler_params=pltpu.CompilerParams(vmem_limit_bytes=VMEM_LIMIT),
        cost_estimate=pl.CostEstimate(
            flops=0, bytes_accessed=sum(2 * x.size for x in ins) + sum(2 * int(np.prod(x)) for x in outs), transcendentals=0
        ),
        name=name,
    )(*ins)


def packed(query, key, value, out, gate, up):
    every = slice(None)
    moves = []
    at = 0
    for i, x in enumerate((query, key, value)):
        moves.append((i, (every, every), 0, (every, slice(at, at + x.shape[1]))))
        at += x.shape[1]
    ff = gate.shape[1]
    for c in range(0, ff, TILE):
        moves.append((3, (every, slice(c, c + TILE)), 1, (every, slice(2 * c, 2 * c + TILE))))
        moves.append((4, (every, slice(c, c + TILE)), 1, (every, slice(2 * c + TILE, 2 * c + 2 * TILE))))
    moves.append((5, (every, every), 1, (every, slice(2 * ff, 2 * ff + out.shape[1]))))
    shapes = [(query.shape[0], at), (gate.shape[0], 2 * ff + out.shape[1])]
    return moved("pack", moves, (query, key, value, gate, up, out), shapes)


def stacked(blocks):
    ins, moves, at = [], [], 0
    half = blocks[0].shape[2] // 2
    for x in blocks:
        for p in range(2):
            cols = slice(p * half, (p + 1) * half)
            moves.append(
                (len(ins), (slice(None), slice(None), cols), p, (slice(at, at + x.shape[0]), slice(None), slice(None)))
            )
        ins.append(x)
        at += x.shape[0]
    return moved("stack", moves, tuple(ins), [(at, blocks[0].shape[1], half)] * 2)


def rms_norm(values, gains):
    factor = lax.rsqrt(jnp.mean(values * values, axis=-1, keepdims=True) + epsilon)
    return values * factor * gains


def gate_math(gate, up, grad_inner):
    c = 0.7978845608028654
    square = gate * gate
    t = jnp.tanh(c * gate * (1.0 + 0.044715 * square))
    half = 0.5 * (1.0 + t)
    act = gate * half
    slope = half + 0.5 * gate * (1.0 - t * t) * (c * (1.0 + 3.0 * 0.044715 * square))
    return (act * up).astype(bf), (grad_inner * up * slope).astype(bf), (grad_inner * act).astype(bf)


def make_body(cube):
    def body(
        tokens, gain_one, query_weight, key_weight, value_weight, out_weight, gain_two, gate_weight,
        up_weight, down_weight, relative_bias_table, layout_bias_table, doc_lengths, box_x, box_y, cotangent,
    ):
        row_count, d = tokens.shape
        pairs = HEADS // 2
        own1, own3 = packed(query_weight, key_weight, value_weight, out_weight, gate_weight, up_weight)
        own2 = down_weight
        guo_full = lax.all_gather(own3, AXES, axis=0, tiled=True)
        far1 = cube.far_first(own1)

        positions = jnp.arange(row_count, dtype=jnp.int32)
        slots = jnp.arange(doc_lengths.shape[1], dtype=jnp.int32)
        doc_ends = jnp.sum(jnp.where(slots[:, None] <= slots[None, :], doc_lengths[0][:, None], 0), axis=0)
        live_rows = positions < doc_ends[-1]
        doc_ids = jnp.sum((positions[:, None] >= doc_ends[None, :]).astype(jnp.int32), axis=1)
        seg_ids = jnp.where(live_rows, doc_ids, doc_lengths.shape[1] + positions)
        live_mask = live_rows.astype(f4)[:, None]
        mask = jnp.where(seg_ids[:, None] == seg_ids[None, :], 0.0, masked_score).astype(f4)
        levels = jnp.arange(GRID, dtype=jnp.int32)
        hots = jnp.concatenate([box_x[:, None] == levels, box_y[:, None] == levels], 1).astype(bf)
        down_hots = jnp.concatenate(
            [box_x[None] == levels[::-1, None], box_y[None] == levels[::-1, None]], 0
        ).astype(bf)
        bands, far, values = tables(relative_bias_table, layout_bias_table)
        inputs_wide = tokens.astype(f4)
        normed_wide, norm_one_back = jax.vjp(rms_norm, inputs_wide, gain_one)
        normed = normed_wide.astype(bf)
        grad_output = cotangent.astype(f4)
        grad_ffn = (live_mask * grad_output).astype(bf)

        far1, own2, normed, mask, hots, down_hots, bands, far, values, grad_ffn = tie(
            (far1, own2, normed, mask, hots, down_hots, bands, far, values, grad_ffn)
        )
        far1 = cube.far_rest(far1)
        far1, own2 = tie((far1, own2))
        pair1 = stacked(far1)
        own2 = tie(own2, pair1)
        got1 = cube.step_a(pair1)
        far2 = cube.far_first(own2)
        got1, far2 = tie((got1, far2))
        pair1 = cube.joined(pair1, got1)
        got1 = cube.step_b(pair1)
        far2 = cube.far_rest(tie(far2, pair1))
        got1, far2 = tie((got1, far2))
        pair1 = cube.joined(pair1, got1)
        core1 = cube.step_core(pair1)
        pair2 = stacked(far2)
        got2 = cube.step_a(pair2)
        normed_ = tie(normed, pair2)
        qkv, qkv_full = cube.project(normed_, cube.pieces(pair1, core1))
        got2, qkv = tie((got2, qkv))
        pair2 = cube.joined(pair2, got2)
        got2 = cube.step_b(pair2)
        qkv_ = tie(qkv, pair2)
        attended, probs = fwd(qkv_, hots, values, bands, far, mask, 0, pairs)
        got2, attended = tie((got2, attended))
        pair2 = cube.joined(pair2, got2)
        core2 = cube.step_core(pair2)
        guo_full, attended = tie((guo_full, attended), pair2)
        ff2 = 2 * gate_weight.shape[1]
        gu_full, out_full = guo_full[:, :ff2], guo_full[:, ff2:]
        branch = jnp.dot(attended, out_full, preferred_element_type=f4)
        hidden = inputs_wide + live_mask * branch
        normed_two_wide, norm_two_back = jax.vjp(rms_norm, hidden, gain_two)
        normed_two = normed_two_wide.astype(bf)
        [down_full] = cube.assemble(cube.pieces(pair2, core2), [(0, down_weight.shape[0])])
        inner_rows, grad_gu = cube.gated(normed_two, guo_full, grad_ffn, down_full)

        send_d, keep_d = cube.terms(inner_rows, grad_ffn, far_first=True)
        got_d = cube.swap(send_d, 1)
        grad_gu_ = tie(grad_gu, send_d)
        send_g, keep_g = cube.terms(normed_two, grad_gu_)
        got_d, send_g, keep_g = tie((got_d, send_g, keep_g))
        got_g = cube.swap(send_g, 1)
        send_d, keep_d = cube.halve(keep_d, got_d, bf)
        got_d = cube.swap(send_d, 8)
        gu_full_, grad_gu_ = tie((gu_full, grad_gu_), send_g, send_d)
        grad_normed_two = jnp.einsum("tf,df->td", grad_gu_, gu_full_, preferred_element_type=f4)
        got_g, grad_normed_two = tie((got_g, grad_normed_two))
        sends_g, keeps_g = cube.split_a(keep_g, got_g)
        sends_g, grad_normed_two = tie((sends_g, grad_normed_two))
        got_g = cube.send_a(sends_g)
        grad_hidden_part, grad_gain_two = norm_two_back(grad_normed_two)
        grad_hidden = grad_output + grad_hidden_part
        grad_branch = (live_mask * grad_hidden).astype(bf)
        grad_attended = jnp.einsum("td,ed->te", grad_branch, out_full, preferred_element_type=f4).astype(bf)
        grad_qkv, rel_sums, lay_sums = bwd(qkv, grad_attended, hots, down_hots, probs, 0, pairs)
        got_d, grad_qkv = tie((got_d, grad_qkv))
        for b in range(4, cube.bits):
            send_d, keep_d = cube.halve(keep_d, got_d, f4)
            got_d = cube.swap(send_d, 1 << b)
        grad_qkv = tie(grad_qkv, send_d)
        send_q, keep_q = cube.terms(normed, grad_qkv, 2 * d)
        send_q, keep_q = cube.terms(attended, grad_branch, into=(send_q, keep_q))
        got_g, send_q, keep_q = tie((got_g, send_q, keep_q))
        sends_g, keeps_g = cube.split_b(keeps_g, got_g)
        got_g = cube.send_b(sends_g)
        got_q = cube.swap(send_q, 1)
        grad_qkv = tie(grad_qkv, sends_g)
        grad_normed = jnp.zeros((), f4)
        for i in range(3):
            grad_normed = grad_normed + jnp.einsum(
                "te,de->td", grad_qkv[i], qkv_full[:, i * d : (i + 1) * d], preferred_element_type=f4
            )
        grad_input_part, grad_gain_one = norm_one_back(grad_normed)
        grad_tokens = grad_hidden + grad_input_part
        grad_rel_table, grad_layout_table = table_grads(rel_sums, lay_sums)
        small = jnp.concatenate(
            [grad_gain_one, grad_gain_two, grad_rel_table.reshape(-1), grad_layout_table.reshape(-1)]
        ).reshape(-1, 128)
        got_q, grad_tokens, small = tie((got_q, grad_tokens, small))
        got_s = cube.swap(small, 1)
        sends_q, keeps_q = cube.split_a(keep_q, got_q)
        got_g, sends_q, grad_tokens, small, got_s = tie((got_g, sends_q, grad_tokens, small, got_s))
        small = small + got_s
        got_q = cube.send_a(sends_q)
        keeps_g, got_g, small = tie((keeps_g, got_g, small), sends_q)
        send_g, own_g = cube.split_far(keeps_g, got_g)
        far_g = cube.far_send(send_g)
        got_s = cube.swap(small, 2)
        inner_ = tie(inner_rows, send_g)
        ffn_rows = jnp.dot(inner_, down_full, preferred_element_type=f4)
        block_out = (hidden + live_mask * ffn_rows).astype(bf)
        far_g, block_out = tie((far_g, block_out))
        send_g, own_g = cube.far_end(own_g, far_g)
        far_g = cube.far_send(send_g)
        got_q, small, got_s = tie((got_q, small, got_s), send_g)
        sends_q, keeps_q = cube.split_b(keeps_q, got_q)
        got_q = cube.send_b(sends_q)
        small = small + got_s
        got_s = cube.swap(small, 4)
        got_q, got_d, small, got_s = tie((got_q, got_d, small, got_s))
        send_q, own_q = cube.split_far(keeps_q, got_q)
        far_q = cube.far_send(send_q)
        keep_d, got_d = tie((keep_d, got_d), send_q)
        send_d, keep_d = cube.halve(keep_d, got_d, f4)
        got_d = cube.swap(send_d, 4)
        small = small + got_s
        for b in range(3, cube.bits - 1):
            small = small + cube.swap(small, 1 << b)
        own_g, far_g = tie((own_g, far_g), send_q)
        share_gu = cube.total(own_g, far_g)
        far_q, got_d, small = tie((far_q, got_d, small))
        send_q, own_q = cube.far_end(own_q, far_q)
        far_q = cube.far_send(send_q)
        keep_d, got_d = tie((keep_d, got_d), send_q)
        send_d, keep_d = cube.halve(keep_d, got_d, f4)
        got_d = cube.swap(send_d, 2)
        share_down = jnp.concatenate([cube.plus(keep_d[p, 0], got_d[p, 0]) for p in range(2)], 1)
        small = (small + cube.swap(small, cube.n // 2)).reshape(-1)
        share_q = cube.total(own_q, far_q)
        c = gate_weight.shape[1]
        share_gate = jnp.concatenate([share_gu[:, 2 * i : 2 * i + TILE] for i in range(0, c, TILE)], 1)
        share_up = jnp.concatenate([share_gu[:, 2 * i + TILE : 2 * i + 2 * TILE] for i in range(0, c, TILE)], 1)
        wide = 3 * d // 2
        left, right = share_q[:, : wide + d // 2], share_q[:, wide + d // 2 :]
        share_qkv = jnp.concatenate([left[:, :wide], right[:, :wide]], 1)
        share_out = jnp.concatenate([left[:, wide:], right[:, wide:]], 1)
        rel_n, lay_n = relative_bias_table.size, layout_bias_table.size
        return (
            block_out,
            grad_tokens,
            small[:d],
            share_qkv[:, :d],
            share_qkv[:, d : 2 * d],
            share_qkv[:, 2 * d :],
            share_out,
            small[d : 2 * d],
            share_gate,
            share_up,
            share_down,
            small[2 * d : 2 * d + rel_n].reshape(relative_bias_table.shape),
            small[2 * d + rel_n : 2 * d + rel_n + lay_n].reshape(layout_bias_table.shape),
        )

    return body


def solution(mesh):
    rows = P(AXES, None)
    line = P(AXES)
    whole = P()
    return jax.shard_map(
        make_body(Cube(mesh)),
        mesh=mesh,
        in_specs=(
            rows, whole, rows, rows, rows, rows, whole, rows, rows, rows, whole, whole, rows, line, line, rows,
        ),
        out_specs=(
            rows, rows, whole, rows, rows, rows, rows, whole, rows, rows, rows, whole, whole,
        ),
        check_vma=False,
    )
```

```python
import numpy as np
import jax
import jax.numpy as jnp
from jax import lax
from jax.experimental import pallas as pl
from jax.experimental.pallas import tpu as pltpu
from jax.sharding import PartitionSpec as P

bf = jnp.bfloat16
f4 = jnp.float32

HEADS,HEAD=16,64
bucket_edges=(1,2,3,4,5,6,7,8,12,16,23,32,46,64,91)
GRID=64
def np_bucket(n):
    n=np.asarray(n); m=np.abs(n)
    b=np.zeros(n.shape,np.int32)
    for e in bucket_edges: b+=(m>=e)
    return b+(n>0)*16
BLK=128
NT=(((1,),(1,)),((),()))
NN=(((1,),(0,)),((),()))
def dot(a,b,dims=NN): return lax.dot_general(a,b,dims,preferred_element_type=f4)

def fwd_kernel(q_ref,k_ref,v_ref,oh_ref,ff_ref,w_ref,far_ref,mask_ref,o_ref,p_ref):
    t=q_ref.shape[0]; nb=t//BLK
    lane=lax.broadcasted_iota(jnp.int32,(t,2*HEAD),1)
    q=q_ref[...]; oh=oh_ref[...]; v=v_ref[...]
    oht=oh.T; ka=jnp.concatenate([k_ref[...].T,oht,oht],axis=0)
    for j in range(2):
        mine=(lane<HEAD) if j==0 else (lane>=HEAD)
        band=pltpu.roll(jnp.broadcast_to(w_ref[0,j:j+1,:],(BLK,4*BLK)),0,1,stride=1,stride_axis=0)
        near=far_ref[0,j:j+1,0:BLK]; past=far_ref[0,j:j+1,BLK:2*BLK]
        rows=dot(oh,ff_ref[j]).astype(bf)
        qa=jnp.concatenate([jnp.where(mine,q,jnp.zeros_like(q)),rows],axis=1)
        whole=dot(qa,ka)
        for s in range(nb):
            sc=whole[s*BLK:(s+1)*BLK]
            rel=[]
            for c in range(nb):
                if c<s-1: rel.append(jnp.broadcast_to(past,(BLK,BLK)))
                elif c>s+1: rel.append(jnp.broadcast_to(near,(BLK,BLK)))
                else: rel.append(band[:,(c-s+1)*BLK:(c-s+2)*BLK])
            sc=(sc+jnp.concatenate(rel,axis=1))+mask_ref[s*BLK:(s+1)*BLK,:]
            top=jnp.max(sc,axis=1,keepdims=True)
            e=jnp.exp(sc-top)
            p=e*(1.0/jnp.sum(e,axis=1,keepdims=True))
            p_ref[j,s*BLK:(s+1)*BLK,:]=p
            o=dot(p.astype(bf),v).astype(bf)
            o_ref[s*BLK:(s+1)*BLK,j*HEAD:(j+1)*HEAD]=o[:,j*HEAD:(j+1)*HEAD]

def bwd_kernel(q_ref,k_ref,v_ref,g_ref,oh_ref,oht_ref,p_ref,d_ref,rel_ref,lay_ref,ds_s,pb_s):
    t=q_ref.shape[0]; nb=t//BLK
    lane=lax.broadcasted_iota(jnp.int32,(t,2*HEAD),1)
    q=q_ref[...]; k=k_ref[...]; v=v_ref[...]; g=g_ref[...]; oh=oh_ref[...]
    koh=jnp.concatenate([k,oh],axis=1)
    qt=q.T; gt=g.T; vt=v.T
    outs=[]
    for j in range(2):
        mine=(lane<HEAD) if j==0 else (lane>=HEAD)
        gm=jnp.where(mine,g,jnp.zeros_like(g))
        band=[jnp.zeros((BLK,BLK),f4) for _ in range(3)]
        past=jnp.zeros((BLK,BLK),f4); near=jnp.zeros((BLK,BLK),f4)
        whole=dot(gm,vt)
        for s in range(nb):
            rows=slice(s*BLK,(s+1)*BLK)
            dp=whole[rows]
            p=p_ref[j,rows,:]
            ds=p*(dp-jnp.sum(p*dp,axis=1,keepdims=True))
            for c in range(nb):
                tile=ds[:,c*BLK:(c+1)*BLK]
                if c<s-1: past=past+tile
                elif c>s+1: near=near+tile
                else: band[c-s+1]=band[c-s+1]+tile
            dsb=ds.astype(bf)
            ds_s[rows,:]=dsb; pb_s[rows,:]=p.astype(bf)
        dq=dot(ds_s[...],koh)
        dkt=dot(qt,ds_s[...]); dvt=dot(gt,pb_s[...])
        outs.append((dq[:,:2*HEAD],dkt,dvt))
        r=dq[:,2*HEAD:]
        hi=r.astype(bf); lo=(r-hi.astype(f4)).astype(bf)
        gl=dot(oht_ref[...],jnp.concatenate([hi,lo],axis=1))
        gl=gl[:,:2*GRID]+gl[:,2*GRID:]
        for i in range(2):
            part=gl[i*GRID:(i+1)*GRID,i*GRID:(i+1)*GRID]
            part=pltpu.roll(jnp.concatenate([part,jnp.zeros((GRID,GRID),f4)],axis=1),0,1,stride=1,stride_axis=0)
            lay_ref[0,2*j+i:2*j+i+1,:]=jnp.sum(part,axis=0,keepdims=True)
        wide=jnp.concatenate(band+[jnp.zeros((BLK,BLK),f4)],axis=1)
        acc=wide[0:8]
        for i in range(1,BLK//8):
            acc=acc+pltpu.roll(wide[8*i:8*i+8],4*BLK-8*i,1)
        line=acc[0:1]
        for i in range(1,8):
            line=line+pltpu.roll(acc[i:i+1],4*BLK-i,1)
        rel_ref[0,j:j+1,0:4*BLK]=line
        rel_ref[0,j:j+1,4*BLK:5*BLK]=jnp.sum(near,axis=0,keepdims=True)
        rel_ref[0,j:j+1,5*BLK:6*BLK]=jnp.sum(past,axis=0,keepdims=True)
    d_ref[0]=jnp.where(lane<HEAD,outs[0][0],outs[1][0]).astype(bf)
    sub=lax.broadcasted_iota(jnp.int32,(2*HEAD,t),0)
    d_ref[1]=jnp.where(sub<HEAD,outs[0][1],outs[1][1]).astype(bf).T
    d_ref[2]=jnp.where(sub<HEAD,outs[0][2],outs[1][2]).astype(bf).T

def fwd(qkv,oh,ff,w,far,mask,lo,n):
    t=qkv.shape[0]; pairs=HEADS//2
    col=lambda off: pl.BlockSpec((t,2*HEAD),lambda i,off=off:(0,off+lo+i))
    return pl.pallas_call(fwd_kernel,grid=(n,),
        in_specs=[col(0),col(pairs),col(2*pairs),pl.BlockSpec((t,2*GRID),lambda i:(0,0)),
          pl.BlockSpec((2,2*GRID,4*GRID),lambda i:(lo+i,0,0)),pl.BlockSpec((1,2,4*BLK),lambda i:(lo+i,0,0)),
          pl.BlockSpec((1,2,2*BLK),lambda i:(lo+i,0,0)),pl.BlockSpec((t,t),lambda i:(0,0))],
        out_specs=[pl.BlockSpec((t,2*HEAD),lambda i:(0,i)),pl.BlockSpec((2,t,t),lambda i:(i,0,0))],
        out_shape=[jax.ShapeDtypeStruct((t,2*HEAD*n),bf),jax.ShapeDtypeStruct((2*n,t,t),f4)],
        compiler_params=pltpu.CompilerParams(vmem_limit_bytes=48<<20),
        cost_estimate=pl.CostEstimate(flops=7_000_000_000*n//8,bytes_accessed=24_000_000*n//8,transcendentals=4_200_000*n//8),
        name="attend_forward")(qkv,qkv,qkv,oh,ff,w,far,mask)

def bwd(qkv,g,oh,oht,p,lo,n):
    t=qkv.shape[0]; pairs=HEADS//2
    col=lambda off: pl.BlockSpec((t,2*HEAD),lambda i,off=off:(0,off+lo+i))
    return pl.pallas_call(bwd_kernel,grid=(n,),
        in_specs=[col(0),col(pairs),col(2*pairs),col(0),pl.BlockSpec((t,2*GRID),lambda i:(0,0)),pl.BlockSpec((2*GRID,t),lambda i:(0,0)),
          pl.BlockSpec((2,t,t),lambda i:(i,0,0))],
        out_specs=[pl.BlockSpec((3,t,2*HEAD),lambda i:(0,0,i)),pl.BlockSpec((1,2,6*BLK),lambda i:(i,0,0)),pl.BlockSpec((1,4,2*GRID),lambda i:(i,0,0))],
        out_shape=[jax.ShapeDtypeStruct((3,t,2*HEAD*n),bf),jax.ShapeDtypeStruct((n,2,6*BLK),f4),jax.ShapeDtypeStruct((n,4,2*GRID),f4)],
        scratch_shapes=[pltpu.VMEM((t,t),bf),pltpu.VMEM((t,t),bf)],
        compiler_params=pltpu.CompilerParams(vmem_limit_bytes=48<<20),
        cost_estimate=pl.CostEstimate(flops=9_000_000_000*n//8,bytes_accessed=24_000_000*n//8,transcendentals=0),
        name="attend_backward")(qkv,qkv,qkv,g,oh,oht,p)

HI=lax.Precision.HIGHEST
def hot(n):
    return (np_bucket(n)[None,:]==np.arange(32)[:,None]).astype(np.float32)
N_GRID=(np.arange(GRID)[:,None]-np.arange(GRID)[None,:]).reshape(-1)
_m=np.arange(512); N_BAND=128-np.where(_m>=385,_m-512,_m)
def tables(rel,lay):
    w=jnp.einsum("bh,bn->hn",rel,jnp.asarray(hot(N_BAND)),precision=HI).reshape(8,2,512)
    far=jnp.concatenate([jnp.broadcast_to(rel[15][:,None],(16,128)),jnp.broadcast_to(rel[31][:,None],(16,128))],1).reshape(8,2,256)
    f=[jnp.einsum("bh,bn->hn",lay[32*i:32*i+32],jnp.asarray(hot(N_GRID)),precision=HI).reshape(16,64,64) for i in range(2)]
    z=jnp.zeros((16,64,64),f4)
    full=jnp.concatenate([jnp.concatenate([f[0],z],2),jnp.concatenate([z,f[1]],2)],1)
    hi=full.astype(bf)
    hi32=lax.reduce_precision(full,8,7)
    lo=(full-hi32).astype(bf)
    return w,far,jnp.concatenate([hi,lo],2)
def table_grads(relsum,laysum):
    rs=relsum.reshape(16,768); ls=laysum.reshape(16,2,128)
    oh=hot(N_BAND); oh[:,384]=0
    e15=np.zeros((32,128),np.float32); e15[15]=1
    e31=np.zeros((32,128),np.float32); e31[31]=1
    C=np.concatenate([oh,e15,e31],1)
    grel=jnp.einsum("bn,hn->bh",jnp.asarray(C),rs,precision=HI)
    m=np.arange(128); nn=63-m
    oh2=hot(nn); oh2[:,127]=0
    glay=jnp.einsum("bn,hxn->xbh",jnp.asarray(oh2),ls,precision=HI).reshape(64,16)
    return grel,glay

epsilon = 1e-06
masked_score = -1e30
AXES = ("wide", "narrow")
VMEM_LIMIT = 58 << 20
TILE = 256


def tie(values, *after):
    return lax.optimization_barrier((values, after))[0]


class Cube:
    def __init__(self, mesh):
        self.n = mesh.shape["wide"] * mesh.shape["narrow"]
        self.bits = self.n.bit_length() - 1
        self.per_wide = mesh.shape["narrow"]
        self.far = self.n // 8

    def me(self):
        return (lax.axis_index("wide") * self.per_wide + lax.axis_index("narrow")).astype(jnp.int32)

    def swap(self, x, mask):
        return lax.ppermute(x, AXES, [(i, i ^ mask) for i in range(self.n)])

    def far_first(self, own):
        return [own[None], self.swap(own[None], self.n // 2)]

    def far_rest(self, blocks):
        for b in range(self.bits - 2, 2, -1):
            cur = jnp.concatenate(blocks, 0)
            blocks = [cur, self.swap(cur, 1 << b)]
        return blocks

    def far_rel(self):
        rel = [0]
        for b in range(self.bits - 1, 2, -1):
            rel = rel + [d ^ (1 << b) for d in rel]
        return rel

    def step_a(self, pair):
        return [self.swap(pair[0], 2), self.swap(pair[1], 4)]

    def step_b(self, pair):
        return [self.swap(pair[0], 4), self.swap(pair[1], 2)]

    def joined(self, pair, got):
        return [jnp.concatenate([x, g], 0) for x, g in zip(pair, got)]

    def step_core(self, pair):
        return [self.swap(x, 1) for x in pair]

    def pieces(self, pair, cores):
        out = []
        for x, g, masks in zip(pair, cores, ((2, 4), (4, 2))):
            rel = self.far_rel()
            for m in masks:
                rel = rel + [d ^ m for d in rel]
            out.append([(x, rel), (g, [d ^ 1 for d in rel])])
        return out

    def plan(self, parts, bands):
        flat, steps, col = [], [], 0
        for pieces in parts:
            mine = []
            for arr, rel in pieces:
                for j, d in enumerate(rel):
                    for k, (r0, r) in enumerate(bands):
                        mine.append((len(flat), j, d, r0, r, k, col, arr.shape[2]))
                flat.append(arr)
            col += pieces[0][0].shape[2]
            steps.append(mine)
        return flat, steps, col

    def assemble(self, parts, bands):
        flat, steps, col = self.plan(parts, bands)
        count = sum(len(x) for x in steps)

        def kernel(me_ref, *refs):
            outs, sem = refs[len(flat) : len(flat) + len(bands)], refs[-1]
            copies = []
            for at, j, d, r0, r, k, c0, w in [x for mine in steps for x in mine]:
                copies.append(
                    pltpu.make_async_copy(
                        refs[at].at[j, pl.ds(r0, r)],
                        outs[k].at[me_ref[0] ^ d, :, pl.ds(c0, w)],
                        sem.at[len(copies)],
                    )
                )
            for c in copies:
                c.start()
            for c in copies:
                c.wait()

        outs = pl.pallas_call(
            kernel,
            grid_spec=pltpu.PrefetchScalarGridSpec(
                num_scalar_prefetch=1,
                grid=(1,),
                in_specs=[pl.BlockSpec(memory_space=pl.ANY)] * len(flat),
                out_specs=[pl.BlockSpec((self.n, r, col), lambda i, m: (0, 0, 0)) for _, r in bands],
                scratch_shapes=[pltpu.SemaphoreType.DMA((count,))],
            ),
            out_shape=[jax.ShapeDtypeStruct((self.n, r, col), bf) for _, r in bands],
            compiler_params=pltpu.CompilerParams(vmem_limit_bytes=VMEM_LIMIT),
            cost_estimate=pl.CostEstimate(
                flops=0, bytes_accessed=4 * self.n * col * sum(r for _, r in bands), transcendentals=0
            ),
            name="assemble",
        )(self.me()[None], *flat)
        return [o.reshape(-1, col) for o in outs]

    def place(self, parts, into=None):
        k, r, c = parts[0][0].shape
        rel = sorted(parts[0][1])
        arrays = [x for x, _ in parts] + ([] if into is None else [into])

        def kernel(me_ref, *refs):
            out, held, sem, out_sem = refs[len(arrays) :]
            copies = []
            for p, (_, mine) in enumerate(parts):
                for j, d in enumerate(mine):
                    copies.append(
                        pltpu.make_async_copy(
                            refs[p].at[j], held.at[rel.index(d), :, pl.ds(p * c, c)], sem.at[p * k + j]
                        )
                    )
            for copy in copies:
                copy.start()
            for copy in copies:
                copy.wait()
            writes = [
                pltpu.make_async_copy(held.at[i], out.at[me_ref[0] ^ d], out_sem.at[i]) for i, d in enumerate(rel)
            ]
            for copy in writes:
                copy.start()
            for copy in writes:
                copy.wait()

        return pl.pallas_call(
            kernel,
            grid_spec=pltpu.PrefetchScalarGridSpec(
                num_scalar_prefetch=1,
                grid=(1,),
                in_specs=[pl.BlockSpec(memory_space=pl.ANY)] * len(arrays),
                out_specs=pl.BlockSpec(memory_space=pl.ANY),
                scratch_shapes=[
                    pltpu.VMEM((k, r, 2 * c), bf),
                    pltpu.SemaphoreType.DMA((2 * k,)),
                    pltpu.SemaphoreType.DMA((k,)),
                ],
            ),
            out_shape=jax.ShapeDtypeStruct((self.n, r, 2 * c), bf),
            input_output_aliases={} if into is None else {len(arrays): 0},
            compiler_params=pltpu.CompilerParams(vmem_limit_bytes=VMEM_LIMIT),
            cost_estimate=pl.CostEstimate(flops=0, bytes_accessed=8 * k * r * c, transcendentals=0),
            name="place",
        )(self.me()[None], *arrays)

    def project(self, x, parts):
        r = parts[0][0][0].shape[1]
        t, d = x.shape
        if r % 16:
            [whole] = self.assemble(parts, [(0, r)])
            return jnp.dot(x, whole, preferred_element_type=f4).astype(bf), whole
        flat, steps, col = self.plan(parts, [(0, r)])
        count = sum(len(m) for m in steps)
        tile = 512

        def kernel(me_ref, x_ref, *refs):
            y_ref, w_ref, held, sem, out_sem = refs[len(flat) :]
            todo, k = [], 0
            for mine in steps:
                copies = []
                for at, j, d_, _, _, _, c0, w in mine:
                    copies.append(
                        pltpu.make_async_copy(
                            refs[at].at[j], held.at[me_ref[0] ^ d_, :, pl.ds(c0, w)], sem.at[k]
                        )
                    )
                    k += 1
                for c in copies:
                    c.start()
                todo.append(copies)
            writes = []
            for mine, copies in zip(steps, todo):
                c0, w = mine[0][6], mine[0][7]
                for c in copies:
                    c.wait()
                write = pltpu.make_async_copy(
                    held.at[:, :, pl.ds(c0, w)], w_ref.at[:, :, pl.ds(c0, w)], out_sem.at[len(writes)]
                )
                write.start()
                writes.append(write)
                for c in range(c0, c0 + w, tile):
                    block = held[:, :, c : c + tile].reshape(d, tile)
                    y_ref[:, c : c + tile] = dot(x_ref[...], block).astype(bf)
            for write in writes:
                write.wait()

        y, whole = pl.pallas_call(
            kernel,
            grid_spec=pltpu.PrefetchScalarGridSpec(
                num_scalar_prefetch=1,
                grid=(1,),
                in_specs=[pl.BlockSpec((t, d), lambda i, m: (0, 0))]
                + [pl.BlockSpec(memory_space=pl.ANY)] * len(flat),
                out_specs=[pl.BlockSpec((t, col), lambda i, m: (0, 0)), pl.BlockSpec(memory_space=pl.ANY)],
                scratch_shapes=[
                    pltpu.VMEM((self.n, r, col), bf),
                    pltpu.SemaphoreType.DMA((count,)),
                    pltpu.SemaphoreType.DMA((len(steps),)),
                ],
            ),
            out_shape=[jax.ShapeDtypeStruct((t, col), bf), jax.ShapeDtypeStruct((self.n, r, col), bf)],
            compiler_params=pltpu.CompilerParams(vmem_limit_bytes=VMEM_LIMIT),
            cost_estimate=pl.CostEstimate(
                flops=2 * t * d * col, bytes_accessed=4 * d * col + 2 * t * (d + col), transcendentals=0
            ),
            name="project",
        )(self.me()[None], x, *flat)
        return y, whole.reshape(d, col)

    def gated(self, x, whole, grad_ffn, down):
        t, d = x.shape
        ff = down.shape[0]

        def kernel(x_ref, w_ref, g_ref, down_ref, inner_ref, grad_ref):
            both = dot(x_ref[...], w_ref[...])
            grad_inner = dot(g_ref[...], down_ref[...], NT)
            inner, gate, up = gate_math(both[:, :TILE], both[:, TILE:], grad_inner)
            inner_ref[...] = inner
            grad_ref[:, :TILE] = gate
            grad_ref[:, TILE:] = up

        rows = pl.BlockSpec((t, d), lambda i: (0, 0))
        return pl.pallas_call(
            kernel,
            grid=(ff // TILE,),
            in_specs=[
                rows,
                pl.BlockSpec((d, 2 * TILE), lambda i: (0, i)),
                rows,
                pl.BlockSpec((TILE, d), lambda i: (i, 0)),
            ],
            out_specs=[
                pl.BlockSpec((t, TILE), lambda i: (0, i)),
                pl.BlockSpec((t, 2 * TILE), lambda i: (0, i)),
            ],
            out_shape=[jax.ShapeDtypeStruct((t, ff), bf), jax.ShapeDtypeStruct((t, 2 * ff), bf)],
            compiler_params=pltpu.CompilerParams(vmem_limit_bytes=VMEM_LIMIT),
            cost_estimate=pl.CostEstimate(
                flops=6 * t * d * ff, bytes_accessed=6 * d * ff + 6 * t * ff, transcendentals=t * ff
            ),
            name="gated",
        )(x, whole, grad_ffn, down)

    def places(self, p, far_first=False):
        out, far = [0], [1 << b for b in range(self.bits - 1, 2, -1)]
        for m in ([2, 4] + far if far_first else far + [[2, 4], [4, 2]][p]) + [1]:
            out = out + [d ^ m for d in out]
        return out

    def terms(self, x, dy, width=None, into=None, far_first=False):
        t, rows = x.shape
        if dy.ndim == 2:
            dy = dy[None]
        r, each = rows // self.n, dy.shape[2]
        half = dy.shape[0] * each // 2
        n = self.n
        if r % 8:
            g = jnp.concatenate([jnp.einsum("tf,td->fd", x, y, preferred_element_type=f4).astype(bf) for y in dy], 1)
            g = g.reshape((2,) * self.bits + (r, -1))
            for b in range(self.bits):
                g = jnp.where((self.me() >> b) & 1 == 1, jnp.flip(g, self.bits - 1 - b), g)
            last = self.bits - 1
            both = []
            for p, near in enumerate(((last - 2, last - 1), (last - 1, last - 2))):
                far = range(last - 3, -1, -1)
                order = (last, *far, last - 2, last - 1) if far_first else (last, *near, *far)
                order = (*order, last + 1, last + 2)
                part = jnp.transpose(g[..., p * half : (p + 1) * half], order)
                both.append(part.reshape(n, r, half))
            both = jnp.stack(both)
            both = both[:, n // 2 :], both[:, : n // 2]
            if into is not None:
                return tuple(jnp.concatenate([a[..., : a.shape[-1] - half], b], -1) for a, b in zip(into, both))
            if width is not None:
                return tuple(jnp.pad(b, ((0, 0), (0, 0), (0, 0), (0, width - half))) for b in both)
            return both
        ordered = r % 16 == 0
        tile = max(c for c in range(128, half + 1, 128) if half % c == 0 and each % c == 0 and c * rows <= 1500000)
        chunk = 256
        per, across = half // tile, each // tile

        def kernel(me_ref, x_ref, y_ref, *refs):
            send_ref, keep_ref, turned, acc = refs[-4:]
            first = pl.program_id(0) == 0
            y_ = y_ref[0]

            def who(at):
                d0, d1 = self.places(0, far_first)[at], self.places(1, far_first)[at]
                return pl.multiple_of((me_ref[0] ^ jnp.where(first, d0, d1)) * r, r)

            if ordered:

                @pl.when((pl.program_id(0) == 0) & (pl.program_id(1) == 0))
                def _():
                    for c in range(0, rows, chunk):
                        acc[c : c + chunk, :] = x_ref[:, c : c + chunk].T

                @pl.when(pl.program_id(1) == 0)
                def _():
                    for at in range(n):
                        turned[at * r : (at + 1) * r, :] = acc[pl.ds(who(at), r), :]

                for c in range(0, rows, chunk):
                    out = dot(turned[c : c + chunk, :], y_).astype(bf)
                    for k in range(chunk // r):
                        at = c // r + k
                        ref = keep_ref if at < n // 2 else send_ref
                        ref[0, at % (n // 2)] = out[k * r : (k + 1) * r]
                return

            for c in range(0, rows, chunk):
                acc[c : c + chunk, :] = dot(x_ref[:, c : c + chunk], y_, (((0,), (0,)), ((), ())))
            for at in range(n):
                ref = keep_ref if at < n // 2 else send_ref
                ref[0, at % (n // 2)] = acc[pl.ds(who(at), r), :].astype(bf)

        if into is not None:
            width = into[0].shape[3]
        skip = 0 if into is None else (width - half) // tile
        out = pl.BlockSpec((1, n // 2, r, tile), lambda p, j, m: (p, 0, 0, skip + j))
        shape = jax.ShapeDtypeStruct((2, n // 2, r, width or half), bf)
        more = () if into is None else tuple(into)
        return pl.pallas_call(
            kernel,
            grid_spec=pltpu.PrefetchScalarGridSpec(
                num_scalar_prefetch=1,
                grid=(2, per),
                in_specs=[
                    pl.BlockSpec((t, rows), lambda p, j, m: (0, 0)),
                    pl.BlockSpec(
                        (1, t, tile), lambda p, j, m: ((p * per + j) // across, 0, (p * per + j) % across)
                    ),
                ]
                + [pl.BlockSpec(memory_space=pl.ANY)] * len(more),
                out_specs=[out, out],
                scratch_shapes=[
                    pltpu.VMEM((rows, t) if ordered else (8, 128), bf),
                    pltpu.VMEM((rows, t), bf) if ordered else pltpu.VMEM((rows, tile), f4),
                ],
            ),
            out_shape=[shape, shape],
            input_output_aliases={} if into is None else {3: 0, 4: 1},
            compiler_params=pltpu.CompilerParams(vmem_limit_bytes=VMEM_LIMIT),
            cost_estimate=pl.CostEstimate(
                flops=4 * t * rows * half, bytes_accessed=2 * (t * rows + 2 * t * half + 2 * rows * half), transcendentals=0
            ),
            name="terms",
        )(self.me()[None], x, dy, *more)

    def plus(self, a, b):
        return a.astype(f4) + b.astype(f4)

    def split_a(self, keep, got):
        h = self.n // 4

        def side(p, lo, hi):
            return self.plus(keep[p, lo:hi], got[p, lo:hi]).astype(bf)

        return [side(p, h, 2 * h) for p in range(2)], [side(p, 0, h) for p in range(2)]

    def halve(self, keep, got, kind):
        h = keep.shape[1] // 2
        return self.plus(keep[:, h:], got[:, h:]).astype(bf), self.plus(keep[:, :h], got[:, :h]).astype(kind)

    def send_a(self, sends):
        return [self.swap(sends[0], 4), self.swap(sends[1], 2)]

    def split_b(self, keeps, gots):
        h = self.n // 8
        sends = [self.plus(k[h:], g[h:]).astype(bf) for k, g in zip(keeps, gots)]
        return sends, [self.plus(k[:h], g[:h]) for k, g in zip(keeps, gots)]

    def send_b(self, sends):
        return [self.swap(sends[0], 2), self.swap(sends[1], 4)]

    def split_far(self, keeps, gots):
        h = self.far // 2

        def both(lo, hi):
            return jnp.concatenate([self.plus(k[lo:hi], g[lo:hi]) for k, g in zip(keeps, gots)], -1)

        return both(h, 2 * h).astype(bf), both(0, h)

    def far_step(self, keep, got):
        h = keep.shape[0] // 2
        return self.plus(keep[h:], got[h:]).astype(bf), self.plus(keep[:h], got[:h])

    def far_send(self, send):
        return self.swap(send, self.n // 2 // send.shape[0])

    def far_end(self, keep, got):
        while keep.shape[0] > 2:
            send, keep = self.far_step(keep, got)
            got = self.far_send(send)
        return self.far_step(keep, got)

    def total(self, own, got):
        return self.plus(own, got)[0]


def moved(name, moves, ins, outs):
    def kernel(*refs):
        for i, src, o, dst in moves:
            refs[len(ins) + o][dst] = refs[i][src]

    return pl.pallas_call(
        kernel,
        out_shape=[jax.ShapeDtypeStruct(x, bf) for x in outs],
        compiler_params=pltpu.CompilerParams(vmem_limit_bytes=VMEM_LIMIT),
        cost_estimate=pl.CostEstimate(
            flops=0, bytes_accessed=sum(2 * x.size for x in ins) + sum(2 * int(np.prod(x)) for x in outs), transcendentals=0
        ),
        name=name,
    )(*ins)


def packed(query, key, value, out, gate, up):
    every = slice(None)
    moves = []
    at = 0
    for i, x in enumerate((query, key, value)):
        moves.append((i, (every, every), 0, (every, slice(at, at + x.shape[1]))))
        at += x.shape[1]
    ff = gate.shape[1]
    for c in range(0, ff, TILE):
        moves.append((3, (every, slice(c, c + TILE)), 1, (every, slice(2 * c, 2 * c + TILE))))
        moves.append((4, (every, slice(c, c + TILE)), 1, (every, slice(2 * c + TILE, 2 * c + 2 * TILE))))
    moves.append((5, (every, every), 1, (every, slice(2 * ff, 2 * ff + out.shape[1]))))
    shapes = [(query.shape[0], at), (gate.shape[0], 2 * ff + out.shape[1])]
    return moved("pack", moves, (query, key, value, gate, up, out), shapes)


def stacked(blocks):
    ins, moves, at = [], [], 0
    half = blocks[0].shape[2] // 2
    for x in blocks:
        for p in range(2):
            cols = slice(p * half, (p + 1) * half)
            moves.append(
                (len(ins), (slice(None), slice(None), cols), p, (slice(at, at + x.shape[0]), slice(None), slice(None)))
            )
        ins.append(x)
        at += x.shape[0]
    return moved("stack", moves, tuple(ins), [(at, blocks[0].shape[1], half)] * 2)


def attention_shares(own, got, d):
    rows = own.shape[0]
    part, wide = 2 * d, 3 * d // 2

    def kernel(own_ref, got_ref, *outs):
        at = lambda x: part * (x // wide) + x % wide
        step = d // 2
        for k in range(4):
            for h in range(2):
                x = at(k * d + h * step) if k < 3 else part * h + wide
                cols = slice(x, x + step)
                outs[k][:, h * step : (h + 1) * step] = own_ref[:, cols] + got_ref[:, cols].astype(f4)

    return pl.pallas_call(
        kernel,
        out_shape=[jax.ShapeDtypeStruct((rows, d), f4)] * 4,
        compiler_params=pltpu.CompilerParams(vmem_limit_bytes=VMEM_LIMIT),
        cost_estimate=pl.CostEstimate(flops=4 * rows * d, bytes_accessed=40 * rows * d, transcendentals=0),
        name="shares",
    )(own, got)


def rms_norm(values, gains):
    factor = lax.rsqrt(jnp.mean(values * values, axis=-1, keepdims=True) + epsilon)
    return values * factor * gains


def gate_math(gate, up, grad_inner):
    c = 0.7978845608028654
    square = gate * gate
    t = jnp.tanh(c * gate * (1.0 + 0.044715 * square))
    half = 0.5 * (1.0 + t)
    act = gate * half
    slope = half + 0.5 * gate * (1.0 - t * t) * (c * (1.0 + 3.0 * 0.044715 * square))
    return (act * up).astype(bf), (grad_inner * up * slope).astype(bf), (grad_inner * act).astype(bf)


def make_body(cube):
    def body(
        tokens, gain_one, query_weight, key_weight, value_weight, out_weight, gain_two, gate_weight,
        up_weight, down_weight, relative_bias_table, layout_bias_table, doc_lengths, box_x, box_y, cotangent,
    ):
        row_count, d = tokens.shape
        pairs = HEADS // 2
        own1, own3 = packed(query_weight, key_weight, value_weight, out_weight, gate_weight, up_weight)
        own2 = down_weight
        guo_full = lax.all_gather(own3, AXES, axis=0, tiled=True)
        far1 = cube.far_first(own1)

        positions = jnp.arange(row_count, dtype=jnp.int32)
        slots = jnp.arange(doc_lengths.shape[1], dtype=jnp.int32)
        doc_ends = jnp.sum(jnp.where(slots[:, None] <= slots[None, :], doc_lengths[0][:, None], 0), axis=0)
        live_rows = positions < doc_ends[-1]
        doc_ids = jnp.sum((positions[:, None] >= doc_ends[None, :]).astype(jnp.int32), axis=1)
        seg_ids = jnp.where(live_rows, doc_ids, doc_lengths.shape[1] + positions)
        live_mask = live_rows.astype(f4)[:, None]
        mask = jnp.where(seg_ids[:, None] == seg_ids[None, :], 0.0, masked_score).astype(f4)
        levels = jnp.arange(GRID, dtype=jnp.int32)
        hots = jnp.concatenate([box_x[:, None] == levels, box_y[:, None] == levels], 1).astype(bf)
        down_hots = jnp.concatenate(
            [box_x[None] == levels[::-1, None], box_y[None] == levels[::-1, None]], 0
        ).astype(bf)
        bands, far, values = tables(relative_bias_table, layout_bias_table)
        inputs_wide = tokens.astype(f4)
        normed_wide, norm_one_back = jax.vjp(rms_norm, inputs_wide, gain_one)
        normed = normed_wide.astype(bf)
        grad_output = cotangent.astype(f4)
        grad_ffn = (live_mask * grad_output).astype(bf)

        far1, own2, normed, mask, hots, down_hots, bands, far, values, grad_ffn = tie(
            (far1, own2, normed, mask, hots, down_hots, bands, far, values, grad_ffn)
        )
        far1 = cube.far_rest(far1)
        far1, own2 = tie((far1, own2))
        pair1 = stacked(far1)
        own2 = tie(own2, pair1)
        got1 = cube.step_a(pair1)
        far2 = cube.far_first(own2)
        got1, far2 = tie((got1, far2))
        pair1 = cube.joined(pair1, got1)
        got1 = cube.step_b(pair1)
        far2 = cube.far_rest(tie(far2, pair1))
        got1, far2 = tie((got1, far2))
        pair1 = cube.joined(pair1, got1)
        core1 = cube.step_core(pair1)
        pair2 = stacked(far2)
        got2 = cube.step_a(pair2)
        normed_ = tie(normed, pair2)
        qkv, qkv_full = cube.project(normed_, cube.pieces(pair1, core1))
        got2, qkv = tie((got2, qkv))
        pair2 = cube.joined(pair2, got2)
        got2 = cube.step_b(pair2)
        qkv_ = tie(qkv, pair2)
        attended, probs = fwd(qkv_, hots, values, bands, far, mask, 0, pairs)
        got2, attended = tie((got2, attended))
        pair2 = cube.joined(pair2, got2)
        core2 = cube.step_core(pair2)
        parts2 = cube.pieces(pair2, core2)
        down_full = cube.place([p[0] for p in parts2])
        guo_full, attended = tie((guo_full, attended), pair2)
        ff2 = 2 * gate_weight.shape[1]
        gu_full, out_full = guo_full[:, :ff2], guo_full[:, ff2:]
        branch = jnp.dot(attended, out_full, preferred_element_type=f4)
        hidden = inputs_wide + live_mask * branch
        normed_two_wide, norm_two_back = jax.vjp(rms_norm, hidden, gain_two)
        normed_two = normed_two_wide.astype(bf)
        down_full = cube.place([p[1] for p in parts2], down_full).reshape(-1, d)
        inner_rows, grad_gu = cube.gated(normed_two, guo_full, grad_ffn, down_full)

        send_d, keep_d = cube.terms(inner_rows, grad_ffn, far_first=True)
        got_d = cube.swap(send_d, 1)
        grad_gu_ = tie(grad_gu, send_d)
        send_g, keep_g = cube.terms(normed_two, grad_gu_)
        got_d, send_g, keep_g = tie((got_d, send_g, keep_g))
        got_g = cube.swap(send_g, 1)
        send_d, keep_d = cube.halve(keep_d, got_d, bf)
        got_d = cube.swap(send_d, 8)
        gu_full_, grad_gu_ = tie((gu_full, grad_gu_), send_g, send_d)
        grad_normed_two = jnp.einsum("tf,df->td", grad_gu_, gu_full_, preferred_element_type=f4)
        got_g, grad_normed_two = tie((got_g, grad_normed_two))
        sends_g, keeps_g = cube.split_a(keep_g, got_g)
        sends_g, grad_normed_two = tie((sends_g, grad_normed_two))
        got_g = cube.send_a(sends_g)
        grad_hidden_part, grad_gain_two = norm_two_back(grad_normed_two)
        grad_hidden = grad_output + grad_hidden_part
        grad_branch = (live_mask * grad_hidden).astype(bf)
        grad_attended = jnp.einsum("td,ed->te", grad_branch, out_full, preferred_element_type=f4).astype(bf)
        grad_qkv, rel_sums, lay_sums = bwd(qkv, grad_attended, hots, down_hots, probs, 0, pairs)
        got_d, grad_qkv = tie((got_d, grad_qkv))
        for b in range(4, cube.bits):
            send_d, keep_d = cube.halve(keep_d, got_d, f4)
            got_d = cube.swap(send_d, 1 << b)
        grad_qkv = tie(grad_qkv, send_d)
        send_q, keep_q = cube.terms(normed, grad_qkv, 2 * d)
        send_q, keep_q = cube.terms(attended, grad_branch, into=(send_q, keep_q))
        got_g, send_q, keep_q = tie((got_g, send_q, keep_q))
        sends_g, keeps_g = cube.split_b(keeps_g, got_g)
        got_g = cube.send_b(sends_g)
        got_q = cube.swap(send_q, 1)
        grad_qkv = tie(grad_qkv, sends_g)
        grad_normed = jnp.zeros((), f4)
        for i in range(3):
            grad_normed = grad_normed + jnp.einsum(
                "te,de->td", grad_qkv[i], qkv_full[:, i * d : (i + 1) * d], preferred_element_type=f4
            )
        grad_input_part, grad_gain_one = norm_one_back(grad_normed)
        grad_tokens = grad_hidden + grad_input_part
        grad_rel_table, grad_layout_table = table_grads(rel_sums, lay_sums)
        small = jnp.concatenate(
            [grad_gain_one, grad_gain_two, grad_rel_table.T.reshape(-1), grad_layout_table.T.reshape(-1)]
        ).reshape(-1, 128)
        got_q, grad_tokens, small = tie((got_q, grad_tokens, small))
        got_s = cube.swap(small, 1)
        sends_q, keeps_q = cube.split_a(keep_q, got_q)
        got_g, sends_q, grad_tokens, small, got_s = tie((got_g, sends_q, grad_tokens, small, got_s))
        small = small + got_s
        got_q = cube.send_a(sends_q)
        keeps_g, got_g, small = tie((keeps_g, got_g, small), sends_q)
        send_g, own_g = cube.split_far(keeps_g, got_g)
        far_g = cube.far_send(send_g)
        got_s = cube.swap(small, 8)
        inner_ = tie(inner_rows, send_g)
        ffn_rows = jnp.dot(inner_, down_full, preferred_element_type=f4)
        block_out = (hidden + live_mask * ffn_rows).astype(bf)
        far_g, block_out, small, got_s = tie((far_g, block_out, small, got_s))
        small = small + got_s
        send_g, own_g = cube.far_end(own_g, far_g)
        far_g = cube.far_send(send_g)
        got_q, small = tie((got_q, small), send_g)
        sends_q, keeps_q = cube.split_b(keeps_q, got_q)
        got_q = cube.send_b(sends_q)
        got_s = cube.swap(small, 2)
        got_q, got_d, small, got_s = tie((got_q, got_d, small, got_s))
        send_q, own_q = cube.split_far(keeps_q, got_q)
        far_q = cube.far_send(send_q)
        keep_d, got_d = tie((keep_d, got_d), send_q)
        send_d, keep_d = cube.halve(keep_d, got_d, f4)
        got_d = cube.swap(send_d, 4)
        small = small + got_s
        for b in range(4, cube.bits):
            got_s = cube.swap(small, 1 << b)
            if b < cube.bits - 1:
                small = small + got_s
        own_g, far_g = tie((own_g, far_g), send_q)
        share_gu = cube.total(own_g, far_g)
        far_q, got_d, small, got_s = tie((far_q, got_d, small, got_s))
        small = small + got_s
        send_q, own_q = cube.far_end(own_q, far_q)
        far_q = cube.far_send(send_q)
        keep_d, got_d = tie((keep_d, got_d), send_q)
        send_d, keep_d = cube.halve(keep_d, got_d, f4)
        got_d = cube.swap(send_d, 2)
        share_down = jnp.concatenate([cube.plus(keep_d[p, 0], got_d[p, 0]) for p in range(2)], 1)
        small = (small + cube.swap(small, 4)).reshape(-1)
        c = gate_weight.shape[1]
        share_gate = jnp.concatenate([share_gu[:, 2 * i : 2 * i + TILE] for i in range(0, c, TILE)], 1)
        share_up = jnp.concatenate([share_gu[:, 2 * i + TILE : 2 * i + 2 * TILE] for i in range(0, c, TILE)], 1)
        rel_n, lay_n = relative_bias_table.size, layout_bias_table.size
        grad_rel = small[2 * d : 2 * d + rel_n].reshape(relative_bias_table.shape[::-1]).T
        grad_lay = small[2 * d + rel_n : 2 * d + rel_n + lay_n].reshape(layout_bias_table.shape[::-1]).T
        gains_one, gains_two = small[:d], small[d : 2 * d]
        gains_one, gains_two, grad_rel, grad_lay, share_down, far_q = tie(
            (gains_one, gains_two, grad_rel, grad_lay, share_down, far_q)
        )
        share_query, share_key, share_value, share_out = attention_shares(own_q[0], far_q[0], d)
        return (
            block_out,
            grad_tokens,
            gains_one,
            share_query,
            share_key,
            share_value,
            share_out,
            gains_two,
            share_gate,
            share_up,
            share_down,
            grad_rel,
            grad_lay,
        )

    return body


def solution(mesh):
    rows = P(AXES, None)
    line = P(AXES)
    whole = P()
    return jax.shard_map(
        make_body(Cube(mesh)),
        mesh=mesh,
        in_specs=(
            rows, whole, rows, rows, rows, rows, whole, rows, rows, rows, whole, whole, rows, line, line, rows,
        ),
        out_specs=(
            rows, rows, whole, rows, rows, rows, rows, whole, rows, rows, rows, whole, whole,
        ),
        check_vma=False,
    )
```

```python
import numpy as np
import jax
import jax.numpy as jnp
from jax import lax
from jax.experimental import pallas as pl
from jax.experimental.pallas import tpu as pltpu
from jax.sharding import PartitionSpec as P

bf = jnp.bfloat16
f4 = jnp.float32

HEADS,HEAD=16,64
bucket_edges=(1,2,3,4,5,6,7,8,12,16,23,32,46,64,91)
GRID=64
def np_bucket(n):
    n=np.asarray(n); m=np.abs(n)
    b=np.zeros(n.shape,np.int32)
    for e in bucket_edges: b+=(m>=e)
    return b+(n>0)*16
BLK=128
NT=(((1,),(1,)),((),()))
NN=(((1,),(0,)),((),()))
def dot(a,b,dims=NN): return lax.dot_general(a,b,dims,preferred_element_type=f4)

def fwd_kernel(q_ref,k_ref,v_ref,oh_ref,ff_ref,w_ref,far_ref,mask_ref,o_ref,p_ref):
    t=q_ref.shape[0]; nb=t//BLK
    lane=lax.broadcasted_iota(jnp.int32,(t,2*HEAD),1)
    q=q_ref[...]; oh=oh_ref[...]; v=v_ref[...]
    oht=oh.T; ka=jnp.concatenate([k_ref[...].T,oht,oht],axis=0)
    for j in range(2):
        mine=(lane<HEAD) if j==0 else (lane>=HEAD)
        band=pltpu.roll(jnp.broadcast_to(w_ref[0,j:j+1,:],(BLK,4*BLK)),0,1,stride=1,stride_axis=0)
        near=far_ref[0,j:j+1,0:BLK]; past=far_ref[0,j:j+1,BLK:2*BLK]
        rows=dot(oh,ff_ref[j]).astype(bf)
        qa=jnp.concatenate([jnp.where(mine,q,jnp.zeros_like(q)),rows],axis=1)
        whole=dot(qa,ka)
        for s in range(nb):
            sc=whole[s*BLK:(s+1)*BLK]
            rel=[]
            for c in range(nb):
                if c<s-1: rel.append(jnp.broadcast_to(past,(BLK,BLK)))
                elif c>s+1: rel.append(jnp.broadcast_to(near,(BLK,BLK)))
                else: rel.append(band[:,(c-s+1)*BLK:(c-s+2)*BLK])
            sc=(sc+jnp.concatenate(rel,axis=1))+mask_ref[s*BLK:(s+1)*BLK,:]
            top=jnp.max(sc,axis=1,keepdims=True)
            e=jnp.exp(sc-top)
            p=e*(1.0/jnp.sum(e,axis=1,keepdims=True))
            p_ref[j,s*BLK:(s+1)*BLK,:]=p
            o=dot(p.astype(bf),v).astype(bf)
            o_ref[s*BLK:(s+1)*BLK,j*HEAD:(j+1)*HEAD]=o[:,j*HEAD:(j+1)*HEAD]

def bwd_kernel(q_ref,k_ref,v_ref,g_ref,oh_ref,oht_ref,p_ref,d_ref,rel_ref,lay_ref,ds_s,pb_s):
    t=q_ref.shape[0]; nb=t//BLK
    lane=lax.broadcasted_iota(jnp.int32,(t,2*HEAD),1)
    q=q_ref[...]; k=k_ref[...]; v=v_ref[...]; g=g_ref[...]; oh=oh_ref[...]
    koh=jnp.concatenate([k,oh],axis=1)
    qt=q.T; gt=g.T; vt=v.T
    outs=[]
    for j in range(2):
        mine=(lane<HEAD) if j==0 else (lane>=HEAD)
        gm=jnp.where(mine,g,jnp.zeros_like(g))
        band=[jnp.zeros((BLK,BLK),f4) for _ in range(3)]
        past=jnp.zeros((BLK,BLK),f4); near=jnp.zeros((BLK,BLK),f4)
        whole=dot(gm,vt)
        for s in range(nb):
            rows=slice(s*BLK,(s+1)*BLK)
            dp=whole[rows]
            p=p_ref[j,rows,:]
            ds=p*(dp-jnp.sum(p*dp,axis=1,keepdims=True))
            for c in range(nb):
                tile=ds[:,c*BLK:(c+1)*BLK]
                if c<s-1: past=past+tile
                elif c>s+1: near=near+tile
                else: band[c-s+1]=band[c-s+1]+tile
            dsb=ds.astype(bf)
            ds_s[rows,:]=dsb; pb_s[rows,:]=p.astype(bf)
        dq=dot(ds_s[...],koh)
        dkt=dot(qt,ds_s[...]); dvt=dot(gt,pb_s[...])
        outs.append((dq[:,:2*HEAD],dkt,dvt))
        r=dq[:,2*HEAD:]
        hi=r.astype(bf); lo=(r-hi.astype(f4)).astype(bf)
        gl=dot(oht_ref[...],jnp.concatenate([hi,lo],axis=1))
        gl=gl[:,:2*GRID]+gl[:,2*GRID:]
        for i in range(2):
            part=gl[i*GRID:(i+1)*GRID,i*GRID:(i+1)*GRID]
            part=pltpu.roll(jnp.concatenate([part,jnp.zeros((GRID,GRID),f4)],axis=1),0,1,stride=1,stride_axis=0)
            lay_ref[0,2*j+i:2*j+i+1,:]=jnp.sum(part,axis=0,keepdims=True)
        wide=jnp.concatenate(band+[jnp.zeros((BLK,BLK),f4)],axis=1)
        acc=wide[0:8]
        for i in range(1,BLK//8):
            acc=acc+pltpu.roll(wide[8*i:8*i+8],4*BLK-8*i,1)
        line=acc[0:1]
        for i in range(1,8):
            line=line+pltpu.roll(acc[i:i+1],4*BLK-i,1)
        rel_ref[0,j:j+1,0:4*BLK]=line
        rel_ref[0,j:j+1,4*BLK:5*BLK]=jnp.sum(near,axis=0,keepdims=True)
        rel_ref[0,j:j+1,5*BLK:6*BLK]=jnp.sum(past,axis=0,keepdims=True)
    d_ref[0]=jnp.where(lane<HEAD,outs[0][0],outs[1][0]).astype(bf)
    sub=lax.broadcasted_iota(jnp.int32,(2*HEAD,t),0)
    d_ref[1]=jnp.where(sub<HEAD,outs[0][1],outs[1][1]).astype(bf).T
    d_ref[2]=jnp.where(sub<HEAD,outs[0][2],outs[1][2]).astype(bf).T

def fwd(qkv,oh,ff,w,far,mask,lo,n):
    t=qkv.shape[0]; pairs=HEADS//2
    col=lambda off: pl.BlockSpec((t,2*HEAD),lambda i,off=off:(0,off+lo+i))
    return pl.pallas_call(fwd_kernel,grid=(n,),
        in_specs=[col(0),col(pairs),col(2*pairs),pl.BlockSpec((t,2*GRID),lambda i:(0,0)),
          pl.BlockSpec((2,2*GRID,4*GRID),lambda i:(lo+i,0,0)),pl.BlockSpec((1,2,4*BLK),lambda i:(lo+i,0,0)),
          pl.BlockSpec((1,2,2*BLK),lambda i:(lo+i,0,0)),pl.BlockSpec((t,t),lambda i:(0,0))],
        out_specs=[pl.BlockSpec((t,2*HEAD),lambda i:(0,i)),pl.BlockSpec((2,t,t),lambda i:(i,0,0))],
        out_shape=[jax.ShapeDtypeStruct((t,2*HEAD*n),bf),jax.ShapeDtypeStruct((2*n,t,t),f4)],
        compiler_params=pltpu.CompilerParams(vmem_limit_bytes=48<<20),
        cost_estimate=pl.CostEstimate(flops=7_000_000_000*n//8,bytes_accessed=24_000_000*n//8,transcendentals=4_200_000*n//8),
        name="attend_forward")(qkv,qkv,qkv,oh,ff,w,far,mask)

def bwd(qkv,g,oh,oht,p,lo,n):
    t=qkv.shape[0]; pairs=HEADS//2
    col=lambda off: pl.BlockSpec((t,2*HEAD),lambda i,off=off:(0,off+lo+i))
    return pl.pallas_call(bwd_kernel,grid=(n,),
        in_specs=[col(0),col(pairs),col(2*pairs),col(0),pl.BlockSpec((t,2*GRID),lambda i:(0,0)),pl.BlockSpec((2*GRID,t),lambda i:(0,0)),
          pl.BlockSpec((2,t,t),lambda i:(i,0,0))],
        out_specs=[pl.BlockSpec((3,t,2*HEAD),lambda i:(0,0,i)),pl.BlockSpec((1,2,6*BLK),lambda i:(i,0,0)),pl.BlockSpec((1,4,2*GRID),lambda i:(i,0,0))],
        out_shape=[jax.ShapeDtypeStruct((3,t,2*HEAD*n),bf),jax.ShapeDtypeStruct((n,2,6*BLK),f4),jax.ShapeDtypeStruct((n,4,2*GRID),f4)],
        scratch_shapes=[pltpu.VMEM((t,t),bf),pltpu.VMEM((t,t),bf)],
        compiler_params=pltpu.CompilerParams(vmem_limit_bytes=48<<20),
        cost_estimate=pl.CostEstimate(flops=9_000_000_000*n//8,bytes_accessed=24_000_000*n//8,transcendentals=0),
        name="attend_backward")(qkv,qkv,qkv,g,oh,oht,p)

HI=lax.Precision.HIGHEST
def hot(n):
    return (np_bucket(n)[None,:]==np.arange(32)[:,None]).astype(np.float32)
N_GRID=(np.arange(GRID)[:,None]-np.arange(GRID)[None,:]).reshape(-1)
_m=np.arange(512); N_BAND=128-np.where(_m>=385,_m-512,_m)
def tables(rel,lay):
    w=jnp.einsum("bh,bn->hn",rel,jnp.asarray(hot(N_BAND)),precision=HI).reshape(8,2,512)
    far=jnp.concatenate([jnp.broadcast_to(rel[15][:,None],(16,128)),jnp.broadcast_to(rel[31][:,None],(16,128))],1).reshape(8,2,256)
    f=[jnp.einsum("bh,bn->hn",lay[32*i:32*i+32],jnp.asarray(hot(N_GRID)),precision=HI).reshape(16,64,64) for i in range(2)]
    z=jnp.zeros((16,64,64),f4)
    full=jnp.concatenate([jnp.concatenate([f[0],z],2),jnp.concatenate([z,f[1]],2)],1)
    hi=full.astype(bf)
    hi32=lax.reduce_precision(full,8,7)
    lo=(full-hi32).astype(bf)
    return w,far,jnp.concatenate([hi,lo],2)
def table_grads(relsum,laysum):
    rs=relsum.reshape(16,768); ls=laysum.reshape(16,2,128)
    oh=hot(N_BAND); oh[:,384]=0
    e15=np.zeros((32,128),np.float32); e15[15]=1
    e31=np.zeros((32,128),np.float32); e31[31]=1
    C=np.concatenate([oh,e15,e31],1)
    grel=jnp.einsum("bn,hn->bh",jnp.asarray(C),rs,precision=HI)
    m=np.arange(128); nn=63-m
    oh2=hot(nn); oh2[:,127]=0
    glay=jnp.einsum("bn,hxn->xbh",jnp.asarray(oh2),ls,precision=HI).reshape(64,16)
    return grel,glay

epsilon = 1e-06
masked_score = -1e30
AXES = ("wide", "narrow")
VMEM_LIMIT = 58 << 20
TILE = 256


def tie(values, *after):
    return lax.optimization_barrier((values, after))[0]


class Cube:
    def __init__(self, mesh):
        self.n = mesh.shape["wide"] * mesh.shape["narrow"]
        self.bits = self.n.bit_length() - 1
        self.per_wide = mesh.shape["narrow"]
        self.far = self.n // 8

    def me(self):
        return (lax.axis_index("wide") * self.per_wide + lax.axis_index("narrow")).astype(jnp.int32)

    def swap(self, x, mask):
        return lax.ppermute(x, AXES, [(i, i ^ mask) for i in range(self.n)])

    def far_first(self, own):
        return [own[None], self.swap(own[None], self.n // 2)]

    def far_rest(self, blocks):
        for b in range(self.bits - 2, 2, -1):
            cur = jnp.concatenate(blocks, 0)
            blocks = [cur, self.swap(cur, 1 << b)]
        return blocks

    def far_rel(self):
        rel = [0]
        for b in range(self.bits - 1, 2, -1):
            rel = rel + [d ^ (1 << b) for d in rel]
        return rel

    def step_a(self, pair):
        return [self.swap(pair[0], 2), self.swap(pair[1], 4)]

    def step_b(self, pair):
        return [self.swap(pair[0], 4), self.swap(pair[1], 2)]

    def joined(self, pair, got):
        return [jnp.concatenate([x, g], 0) for x, g in zip(pair, got)]

    def step_core(self, pair):
        return [self.swap(x, 1) for x in pair]

    def pieces(self, pair, cores):
        out = []
        for x, g, masks in zip(pair, cores, ((2, 4), (4, 2))):
            rel = self.far_rel()
            for m in masks:
                rel = rel + [d ^ m for d in rel]
            out.append([(x, rel), (g, [d ^ 1 for d in rel])])
        return out

    def plan(self, parts, bands):
        flat, steps, col = [], [], 0
        for pieces in parts:
            mine = []
            for arr, rel in pieces:
                for j, d in enumerate(rel):
                    for k, (r0, r) in enumerate(bands):
                        mine.append((len(flat), j, d, r0, r, k, col, arr.shape[2]))
                flat.append(arr)
            col += pieces[0][0].shape[2]
            steps.append(mine)
        return flat, steps, col

    def assemble(self, parts, bands):
        flat, steps, col = self.plan(parts, bands)
        count = sum(len(x) for x in steps)

        def kernel(me_ref, *refs):
            outs, sem = refs[len(flat) : len(flat) + len(bands)], refs[-1]
            copies = []
            for at, j, d, r0, r, k, c0, w in [x for mine in steps for x in mine]:
                copies.append(
                    pltpu.make_async_copy(
                        refs[at].at[j, pl.ds(r0, r)],
                        outs[k].at[me_ref[0] ^ d, :, pl.ds(c0, w)],
                        sem.at[len(copies)],
                    )
                )
            for c in copies:
                c.start()
            for c in copies:
                c.wait()

        outs = pl.pallas_call(
            kernel,
            grid_spec=pltpu.PrefetchScalarGridSpec(
                num_scalar_prefetch=1,
                grid=(1,),
                in_specs=[pl.BlockSpec(memory_space=pl.ANY)] * len(flat),
                out_specs=[pl.BlockSpec((self.n, r, col), lambda i, m: (0, 0, 0)) for _, r in bands],
                scratch_shapes=[pltpu.SemaphoreType.DMA((count,))],
            ),
            out_shape=[jax.ShapeDtypeStruct((self.n, r, col), bf) for _, r in bands],
            compiler_params=pltpu.CompilerParams(vmem_limit_bytes=VMEM_LIMIT),
            cost_estimate=pl.CostEstimate(
                flops=0, bytes_accessed=4 * self.n * col * sum(r for _, r in bands), transcendentals=0
            ),
            name="assemble",
        )(self.me()[None], *flat)
        return [o.reshape(-1, col) for o in outs]

    def place(self, parts, into=None):
        arrays = [x for pieces in parts for x, _ in pieces]
        r, c = arrays[0].shape[1:]
        todo, at = [], 0
        for p, pieces in enumerate(parts):
            for _, rel in pieces:
                todo += [(at, j, d, p) for j, d in enumerate(rel)]
                at += 1
        count = len(todo)
        operands = arrays + ([] if into is None else [into])

        def kernel(me_ref, *refs):
            out, held, sem, out_sem = refs[len(operands) :]
            reads, writes = [], []
            for k, (at, j, d, p) in enumerate(todo):
                reads.append(pltpu.make_async_copy(refs[at].at[j], held.at[k], sem.at[k]))
                place = out.at[me_ref[0] ^ d, :, pl.ds(p * c, c)]
                writes.append(pltpu.make_async_copy(held.at[k], place, out_sem.at[k]))
            for copy in reads:
                copy.start()
            for read, write in zip(reads, writes):
                read.wait()
                write.start()
            for write in writes:
                write.wait()

        return pl.pallas_call(
            kernel,
            grid_spec=pltpu.PrefetchScalarGridSpec(
                num_scalar_prefetch=1,
                grid=(1,),
                in_specs=[pl.BlockSpec(memory_space=pl.ANY)] * len(operands),
                out_specs=pl.BlockSpec(memory_space=pl.ANY),
                scratch_shapes=[
                    pltpu.VMEM((count, r, c), bf),
                    pltpu.SemaphoreType.DMA((count,)),
                    pltpu.SemaphoreType.DMA((count,)),
                ],
            ),
            out_shape=jax.ShapeDtypeStruct((self.n, r, 2 * c), bf),
            input_output_aliases={} if into is None else {len(operands): 0},
            compiler_params=pltpu.CompilerParams(vmem_limit_bytes=VMEM_LIMIT),
            cost_estimate=pl.CostEstimate(flops=0, bytes_accessed=4 * count * r * c, transcendentals=0),
            name="place",
        )(self.me()[None], *operands)

    def project(self, x, parts):
        r = parts[0][0][0].shape[1]
        t, d = x.shape
        if r % 16:
            [whole] = self.assemble(parts, [(0, r)])
            return jnp.dot(x, whole, preferred_element_type=f4).astype(bf), whole
        flat, steps, col = self.plan(parts, [(0, r)])
        count = sum(len(m) for m in steps)
        tile = 512

        def kernel(me_ref, x_ref, *refs):
            y_ref, w_ref, held, sem, out_sem = refs[len(flat) :]
            todo, k = [], 0
            for mine in steps:
                copies = []
                for at, j, d_, _, _, _, c0, w in mine:
                    copies.append(
                        pltpu.make_async_copy(
                            refs[at].at[j], held.at[me_ref[0] ^ d_, :, pl.ds(c0, w)], sem.at[k]
                        )
                    )
                    k += 1
                for c in copies:
                    c.start()
                todo.append(copies)
            writes = []
            for mine, copies in zip(steps, todo):
                c0, w = mine[0][6], mine[0][7]
                for c in copies:
                    c.wait()
                write = pltpu.make_async_copy(
                    held.at[:, :, pl.ds(c0, w)], w_ref.at[:, :, pl.ds(c0, w)], out_sem.at[len(writes)]
                )
                write.start()
                writes.append(write)
                for c in range(c0, c0 + w, tile):
                    block = held[:, :, c : c + tile].reshape(d, tile)
                    y_ref[:, c : c + tile] = dot(x_ref[...], block).astype(bf)
            for write in writes:
                write.wait()

        y, whole = pl.pallas_call(
            kernel,
            grid_spec=pltpu.PrefetchScalarGridSpec(
                num_scalar_prefetch=1,
                grid=(1,),
                in_specs=[pl.BlockSpec((t, d), lambda i, m: (0, 0))]
                + [pl.BlockSpec(memory_space=pl.ANY)] * len(flat),
                out_specs=[pl.BlockSpec((t, col), lambda i, m: (0, 0)), pl.BlockSpec(memory_space=pl.ANY)],
                scratch_shapes=[
                    pltpu.VMEM((self.n, r, col), bf),
                    pltpu.SemaphoreType.DMA((count,)),
                    pltpu.SemaphoreType.DMA((len(steps),)),
                ],
            ),
            out_shape=[jax.ShapeDtypeStruct((t, col), bf), jax.ShapeDtypeStruct((self.n, r, col), bf)],
            compiler_params=pltpu.CompilerParams(vmem_limit_bytes=VMEM_LIMIT),
            cost_estimate=pl.CostEstimate(
                flops=2 * t * d * col, bytes_accessed=4 * d * col + 2 * t * (d + col), transcendentals=0
            ),
            name="project",
        )(self.me()[None], x, *flat)
        return y, whole.reshape(d, col)

    def gated(self, x, whole, grad_ffn, down):
        t, d = x.shape
        ff = down.shape[0]

        def kernel(x_ref, w_ref, g_ref, down_ref, inner_ref, grad_ref):
            both = dot(x_ref[...], w_ref[...])
            grad_inner = dot(g_ref[...], down_ref[...], NT)
            inner, gate, up = gate_math(both[:, :TILE], both[:, TILE:], grad_inner)
            inner_ref[...] = inner
            grad_ref[:, :TILE] = gate
            grad_ref[:, TILE:] = up

        rows = pl.BlockSpec((t, d), lambda i: (0, 0))
        return pl.pallas_call(
            kernel,
            grid=(ff // TILE,),
            in_specs=[
                rows,
                pl.BlockSpec((d, 2 * TILE), lambda i: (0, i)),
                rows,
                pl.BlockSpec((TILE, d), lambda i: (i, 0)),
            ],
            out_specs=[
                pl.BlockSpec((t, TILE), lambda i: (0, i)),
                pl.BlockSpec((t, 2 * TILE), lambda i: (0, i)),
            ],
            out_shape=[jax.ShapeDtypeStruct((t, ff), bf), jax.ShapeDtypeStruct((t, 2 * ff), bf)],
            compiler_params=pltpu.CompilerParams(vmem_limit_bytes=VMEM_LIMIT),
            cost_estimate=pl.CostEstimate(
                flops=6 * t * d * ff, bytes_accessed=6 * d * ff + 6 * t * ff, transcendentals=t * ff
            ),
            name="gated",
        )(x, whole, grad_ffn, down)

    def places(self, p, far_first=False):
        out, far = [0], [1 << b for b in range(self.bits - 1, 2, -1)]
        for m in ([2, 4] + far if far_first else far + [[2, 4], [4, 2]][p]) + [1]:
            out = out + [d ^ m for d in out]
        return out

    def terms(self, x, dy, width=None, into=None, far_first=False):
        t, rows = x.shape
        if dy.ndim == 2:
            dy = dy[None]
        r, each = rows // self.n, dy.shape[2]
        half = dy.shape[0] * each // 2
        n = self.n
        if r % 8:
            g = jnp.concatenate([jnp.einsum("tf,td->fd", x, y, preferred_element_type=f4).astype(bf) for y in dy], 1)
            g = g.reshape((2,) * self.bits + (r, -1))
            for b in range(self.bits):
                g = jnp.where((self.me() >> b) & 1 == 1, jnp.flip(g, self.bits - 1 - b), g)
            last = self.bits - 1
            both = []
            for p, near in enumerate(((last - 2, last - 1), (last - 1, last - 2))):
                far = range(last - 3, -1, -1)
                order = (last, *far, last - 2, last - 1) if far_first else (last, *near, *far)
                order = (*order, last + 1, last + 2)
                part = jnp.transpose(g[..., p * half : (p + 1) * half], order)
                both.append(part.reshape(n, r, half))
            both = jnp.stack(both)
            both = both[:, n // 2 :], both[:, : n // 2]
            if into is not None:
                return tuple(jnp.concatenate([a[..., : a.shape[-1] - half], b], -1) for a, b in zip(into, both))
            if width is not None:
                return tuple(jnp.pad(b, ((0, 0), (0, 0), (0, 0), (0, width - half))) for b in both)
            return both
        ordered = r % 16 == 0
        tile = max(c for c in range(128, half + 1, 128) if half % c == 0 and each % c == 0 and c * rows <= 1500000)
        chunk = 256
        per, across = half // tile, each // tile

        def kernel(me_ref, x_ref, y_ref, *refs):
            send_ref, keep_ref, turned, acc = refs[-4:]
            first = pl.program_id(0) == 0
            y_ = y_ref[0]

            def who(at):
                d0, d1 = self.places(0, far_first)[at], self.places(1, far_first)[at]
                return pl.multiple_of((me_ref[0] ^ jnp.where(first, d0, d1)) * r, r)

            if ordered:

                @pl.when((pl.program_id(0) == 0) & (pl.program_id(1) == 0))
                def _():
                    for c in range(0, rows, chunk):
                        acc[c : c + chunk, :] = x_ref[:, c : c + chunk].T

                @pl.when(pl.program_id(1) == 0)
                def _():
                    for at in range(n):
                        turned[at * r : (at + 1) * r, :] = acc[pl.ds(who(at), r), :]

                for c in range(0, rows, chunk):
                    out = dot(turned[c : c + chunk, :], y_).astype(bf)
                    for k in range(chunk // r):
                        at = c // r + k
                        ref = keep_ref if at < n // 2 else send_ref
                        ref[0, at % (n // 2)] = out[k * r : (k + 1) * r]
                return

            for c in range(0, rows, chunk):
                acc[c : c + chunk, :] = dot(x_ref[:, c : c + chunk], y_, (((0,), (0,)), ((), ())))
            for at in range(n):
                ref = keep_ref if at < n // 2 else send_ref
                ref[0, at % (n // 2)] = acc[pl.ds(who(at), r), :].astype(bf)

        if into is not None:
            width = into[0].shape[3]
        skip = 0 if into is None else (width - half) // tile
        out = pl.BlockSpec((1, n // 2, r, tile), lambda p, j, m: (p, 0, 0, skip + j))
        shape = jax.ShapeDtypeStruct((2, n // 2, r, width or half), bf)
        more = () if into is None else tuple(into)
        return pl.pallas_call(
            kernel,
            grid_spec=pltpu.PrefetchScalarGridSpec(
                num_scalar_prefetch=1,
                grid=(2, per),
                in_specs=[
                    pl.BlockSpec((t, rows), lambda p, j, m: (0, 0)),
                    pl.BlockSpec(
                        (1, t, tile), lambda p, j, m: ((p * per + j) // across, 0, (p * per + j) % across)
                    ),
                ]
                + [pl.BlockSpec(memory_space=pl.ANY)] * len(more),
                out_specs=[out, out],
                scratch_shapes=[
                    pltpu.VMEM((rows, t) if ordered else (8, 128), bf),
                    pltpu.VMEM((rows, t), bf) if ordered else pltpu.VMEM((rows, tile), f4),
                ],
            ),
            out_shape=[shape, shape],
            input_output_aliases={} if into is None else {3: 0, 4: 1},
            compiler_params=pltpu.CompilerParams(vmem_limit_bytes=VMEM_LIMIT),
            cost_estimate=pl.CostEstimate(
                flops=4 * t * rows * half, bytes_accessed=2 * (t * rows + 2 * t * half + 2 * rows * half), transcendentals=0
            ),
            name="terms",
        )(self.me()[None], x, dy, *more)

    def plus(self, a, b):
        return a.astype(f4) + b.astype(f4)

    def split_a(self, keep, got):
        h = self.n // 4

        def side(p, lo, hi):
            return self.plus(keep[p, lo:hi], got[p, lo:hi]).astype(bf)

        return [side(p, h, 2 * h) for p in range(2)], [side(p, 0, h) for p in range(2)]

    def halve(self, keep, got, kind):
        h = keep.shape[1] // 2
        return self.plus(keep[:, h:], got[:, h:]).astype(bf), self.plus(keep[:, :h], got[:, :h]).astype(kind)

    def send_a(self, sends):
        return [self.swap(sends[0], 4), self.swap(sends[1], 2)]

    def split_b(self, keeps, gots):
        h = self.n // 8
        sends = [self.plus(k[h:], g[h:]).astype(bf) for k, g in zip(keeps, gots)]
        return sends, [self.plus(k[:h], g[:h]) for k, g in zip(keeps, gots)]

    def send_b(self, sends):
        return [self.swap(sends[0], 2), self.swap(sends[1], 4)]

    def split_far(self, keeps, gots):
        h = self.far // 2

        def both(lo, hi):
            return jnp.concatenate([self.plus(k[lo:hi], g[lo:hi]) for k, g in zip(keeps, gots)], -1)

        return both(h, 2 * h).astype(bf), both(0, h)

    def far_step(self, keep, got):
        h = keep.shape[0] // 2
        return self.plus(keep[h:], got[h:]).astype(bf), self.plus(keep[:h], got[:h])

    def far_send(self, send):
        return self.swap(send, self.n // 2 // send.shape[0])

    def far_end(self, keep, got):
        while keep.shape[0] > 2:
            send, keep = self.far_step(keep, got)
            got = self.far_send(send)
        return self.far_step(keep, got)

    def total(self, own, got):
        return self.plus(own, got)[0]


def moved(name, moves, ins, outs):
    def kernel(*refs):
        for i, src, o, dst in moves:
            refs[len(ins) + o][dst] = refs[i][src]

    return pl.pallas_call(
        kernel,
        out_shape=[jax.ShapeDtypeStruct(x, bf) for x in outs],
        compiler_params=pltpu.CompilerParams(vmem_limit_bytes=VMEM_LIMIT),
        cost_estimate=pl.CostEstimate(
            flops=0, bytes_accessed=sum(2 * x.size for x in ins) + sum(2 * int(np.prod(x)) for x in outs), transcendentals=0
        ),
        name=name,
    )(*ins)


def packed(query, key, value, out, gate, up):
    every = slice(None)
    moves = []
    at = 0
    for i, x in enumerate((query, key, value)):
        moves.append((i, (every, every), 0, (every, slice(at, at + x.shape[1]))))
        at += x.shape[1]
    ff = gate.shape[1]
    for c in range(0, ff, TILE):
        moves.append((3, (every, slice(c, c + TILE)), 1, (every, slice(2 * c, 2 * c + TILE))))
        moves.append((4, (every, slice(c, c + TILE)), 1, (every, slice(2 * c + TILE, 2 * c + 2 * TILE))))
    moves.append((5, (every, every), 1, (every, slice(2 * ff, 2 * ff + out.shape[1]))))
    shapes = [(query.shape[0], at), (gate.shape[0], 2 * ff + out.shape[1])]
    return moved("pack", moves, (query, key, value, gate, up, out), shapes)


def stacked(blocks):
    ins, moves, at = [], [], 0
    half = blocks[0].shape[2] // 2
    for x in blocks:
        for p in range(2):
            cols = slice(p * half, (p + 1) * half)
            moves.append(
                (len(ins), (slice(None), slice(None), cols), p, (slice(at, at + x.shape[0]), slice(None), slice(None)))
            )
        ins.append(x)
        at += x.shape[0]
    return moved("stack", moves, tuple(ins), [(at, blocks[0].shape[1], half)] * 2)


def attention_shares(own, got, d):
    rows = own.shape[0]
    part, wide = 2 * d, 3 * d // 2

    def kernel(own_ref, got_ref, *outs):
        at = lambda x: part * (x // wide) + x % wide
        step = d // 2
        for k in range(4):
            for h in range(2):
                x = at(k * d + h * step) if k < 3 else part * h + wide
                cols = slice(x, x + step)
                outs[k][:, h * step : (h + 1) * step] = own_ref[:, cols] + got_ref[:, cols].astype(f4)

    return pl.pallas_call(
        kernel,
        out_shape=[jax.ShapeDtypeStruct((rows, d), f4)] * 4,
        compiler_params=pltpu.CompilerParams(vmem_limit_bytes=VMEM_LIMIT),
        cost_estimate=pl.CostEstimate(flops=4 * rows * d, bytes_accessed=40 * rows * d, transcendentals=0),
        name="shares",
    )(own, got)


def rms_norm(values, gains):
    factor = lax.rsqrt(jnp.mean(values * values, axis=-1, keepdims=True) + epsilon)
    return values * factor * gains


def gate_math(gate, up, grad_inner):
    c = 0.7978845608028654
    square = gate * gate
    t = jnp.tanh(c * gate * (1.0 + 0.044715 * square))
    half = 0.5 * (1.0 + t)
    act = gate * half
    slope = half + 0.5 * gate * (1.0 - t * t) * (c * (1.0 + 3.0 * 0.044715 * square))
    return (act * up).astype(bf), (grad_inner * up * slope).astype(bf), (grad_inner * act).astype(bf)


def make_body(cube):
    def body(
        tokens, gain_one, query_weight, key_weight, value_weight, out_weight, gain_two, gate_weight,
        up_weight, down_weight, relative_bias_table, layout_bias_table, doc_lengths, box_x, box_y, cotangent,
    ):
        row_count, d = tokens.shape
        pairs = HEADS // 2
        own1, own3 = packed(query_weight, key_weight, value_weight, out_weight, gate_weight, up_weight)
        own2 = down_weight
        guo_full = lax.all_gather(own3, AXES, axis=0, tiled=True)
        far1 = cube.far_first(own1)

        positions = jnp.arange(row_count, dtype=jnp.int32)
        slots = jnp.arange(doc_lengths.shape[1], dtype=jnp.int32)
        doc_ends = jnp.sum(jnp.where(slots[:, None] <= slots[None, :], doc_lengths[0][:, None], 0), axis=0)
        live_rows = positions < doc_ends[-1]
        doc_ids = jnp.sum((positions[:, None] >= doc_ends[None, :]).astype(jnp.int32), axis=1)
        seg_ids = jnp.where(live_rows, doc_ids, doc_lengths.shape[1] + positions)
        live_mask = live_rows.astype(f4)[:, None]
        mask = jnp.where(seg_ids[:, None] == seg_ids[None, :], 0.0, masked_score).astype(f4)
        levels = jnp.arange(GRID, dtype=jnp.int32)
        hots = jnp.concatenate([box_x[:, None] == levels, box_y[:, None] == levels], 1).astype(bf)
        down_hots = jnp.concatenate(
            [box_x[None] == levels[::-1, None], box_y[None] == levels[::-1, None]], 0
        ).astype(bf)
        bands, far, values = tables(relative_bias_table, layout_bias_table)
        inputs_wide = tokens.astype(f4)
        normed_wide, norm_one_back = jax.vjp(rms_norm, inputs_wide, gain_one)
        normed = normed_wide.astype(bf)
        grad_output = cotangent.astype(f4)
        grad_ffn = (live_mask * grad_output).astype(bf)

        far1, own2, normed, mask, hots, down_hots, bands, far, values, grad_ffn = tie(
            (far1, own2, normed, mask, hots, down_hots, bands, far, values, grad_ffn)
        )
        far1 = cube.far_rest(far1)
        far1, own2 = tie((far1, own2))
        pair1 = stacked(far1)
        own2 = tie(own2, pair1)
        got1 = cube.step_a(pair1)
        far2 = cube.far_first(own2)
        got1, far2 = tie((got1, far2))
        pair1 = cube.joined(pair1, got1)
        got1 = cube.step_b(pair1)
        far2 = cube.far_rest(tie(far2, pair1))
        got1, far2 = tie((got1, far2))
        pair1 = cube.joined(pair1, got1)
        core1 = cube.step_core(pair1)
        pair2 = stacked(far2)
        got2 = cube.step_a(pair2)
        normed_ = tie(normed, pair2)
        qkv, qkv_full = cube.project(normed_, cube.pieces(pair1, core1))
        got2, qkv = tie((got2, qkv))
        pair2 = cube.joined(pair2, got2)
        got2, early = cube.step_b(pair2), cube.step_core(pair2)
        qkv_ = tie(qkv, pair2)
        attended, probs = fwd(qkv_, hots, values, bands, far, mask, 0, pairs)
        got2, early, attended = tie((got2, early, attended))
        late = cube.step_core(got2)
        near, other = [], []
        for p, (ma, mb) in enumerate(((2, 4), (4, 2))):
            rel = cube.far_rel()
            rel = rel + [x ^ ma for x in rel]
            more = [x ^ mb for x in rel]
            near.append([(pair2[p], rel), (early[p], [x ^ 1 for x in rel])])
            other.append([(got2[p], more), (late[p], [x ^ 1 for x in more])])
        down_full = cube.place(near)
        guo_full, attended = tie((guo_full, attended))
        ff2 = 2 * gate_weight.shape[1]
        gu_full, out_full = guo_full[:, :ff2], guo_full[:, ff2:]
        branch = jnp.dot(attended, out_full, preferred_element_type=f4)
        hidden = inputs_wide + live_mask * branch
        normed_two_wide, norm_two_back = jax.vjp(rms_norm, hidden, gain_two)
        normed_two = normed_two_wide.astype(bf)
        down_full = cube.place(other, down_full).reshape(-1, d)
        inner_rows, grad_gu = cube.gated(normed_two, guo_full, grad_ffn, down_full)

        send_d, keep_d = cube.terms(inner_rows, grad_ffn, far_first=True)
        got_d = cube.swap(send_d, 1)
        grad_gu_ = tie(grad_gu, send_d)
        send_g, keep_g = cube.terms(normed_two, grad_gu_)
        got_d, send_g, keep_g = tie((got_d, send_g, keep_g))
        got_g = cube.swap(send_g, 1)
        send_d, keep_d = cube.halve(keep_d, got_d, bf)
        got_d = cube.swap(send_d, 8)
        gu_full_, grad_gu_ = tie((gu_full, grad_gu_), send_g, send_d)
        grad_normed_two = jnp.einsum("tf,df->td", grad_gu_, gu_full_, preferred_element_type=f4)
        got_g, grad_normed_two = tie((got_g, grad_normed_two))
        sends_g, keeps_g = cube.split_a(keep_g, got_g)
        sends_g, grad_normed_two = tie((sends_g, grad_normed_two))
        got_g = cube.send_a(sends_g)
        grad_hidden_part, grad_gain_two = norm_two_back(grad_normed_two)
        grad_hidden = grad_output + grad_hidden_part
        grad_branch = (live_mask * grad_hidden).astype(bf)
        grad_attended = jnp.einsum("td,ed->te", grad_branch, out_full, preferred_element_type=f4).astype(bf)
        grad_qkv, rel_sums, lay_sums = bwd(qkv, grad_attended, hots, down_hots, probs, 0, pairs)
        got_d, grad_qkv = tie((got_d, grad_qkv))
        for b in range(4, cube.bits):
            send_d, keep_d = cube.halve(keep_d, got_d, f4)
            got_d = cube.swap(send_d, 1 << b)
        grad_qkv = tie(grad_qkv, send_d)
        send_q, keep_q = cube.terms(normed, grad_qkv, 2 * d)
        send_q, keep_q = cube.terms(attended, grad_branch, into=(send_q, keep_q))
        got_g, send_q, keep_q = tie((got_g, send_q, keep_q))
        sends_g, keeps_g = cube.split_b(keeps_g, got_g)
        got_g = cube.send_b(sends_g)
        got_q = cube.swap(send_q, 1)
        grad_qkv = tie(grad_qkv, sends_g)
        grad_normed = jnp.zeros((), f4)
        for i in range(3):
            grad_normed = grad_normed + jnp.einsum(
                "te,de->td", grad_qkv[i], qkv_full[:, i * d : (i + 1) * d], preferred_element_type=f4
            )
        grad_input_part, grad_gain_one = norm_one_back(grad_normed)
        grad_tokens = grad_hidden + grad_input_part
        grad_rel_table, grad_layout_table = table_grads(rel_sums, lay_sums)
        small = jnp.concatenate(
            [grad_gain_one, grad_gain_two, grad_rel_table.T.reshape(-1), grad_layout_table.T.reshape(-1)]
        ).reshape(-1, 128)
        got_q, grad_tokens, small = tie((got_q, grad_tokens, small))
        got_s = cube.swap(small, 1)
        sends_q, keeps_q = cube.split_a(keep_q, got_q)
        got_g, sends_q, grad_tokens, small, got_s = tie((got_g, sends_q, grad_tokens, small, got_s))
        small = small + got_s
        got_q = cube.send_a(sends_q)
        keeps_g, got_g, small = tie((keeps_g, got_g, small), sends_q)
        send_g, own_g = cube.split_far(keeps_g, got_g)
        far_g = cube.far_send(send_g)
        got_s = cube.swap(small, 8)
        inner_ = tie(inner_rows, send_g)
        ffn_rows = jnp.dot(inner_, down_full, preferred_element_type=f4)
        block_out = (hidden + live_mask * ffn_rows).astype(bf)
        far_g, block_out, small, got_s = tie((far_g, block_out, small, got_s))
        small = small + got_s
        send_g, own_g = cube.far_end(own_g, far_g)
        far_g = cube.far_send(send_g)
        got_q, small = tie((got_q, small), send_g)
        sends_q, keeps_q = cube.split_b(keeps_q, got_q)
        got_q = cube.send_b(sends_q)
        got_s = cube.swap(small, 2)
        got_q, got_d, small, got_s = tie((got_q, got_d, small, got_s))
        send_q, own_q = cube.split_far(keeps_q, got_q)
        far_q = cube.far_send(send_q)
        keep_d, got_d = tie((keep_d, got_d), send_q)
        send_d, keep_d = cube.halve(keep_d, got_d, f4)
        got_d = cube.swap(send_d, 4)
        small = small + got_s
        for b in range(4, cube.bits):
            got_s = cube.swap(small, 1 << b)
            if b < cube.bits - 1:
                small = small + got_s
        own_g, far_g = tie((own_g, far_g), send_q)
        share_gu = cube.total(own_g, far_g)
        far_q, got_d, small, got_s = tie((far_q, got_d, small, got_s))
        small = small + got_s
        send_q, own_q = cube.far_end(own_q, far_q)
        far_q = cube.far_send(send_q)
        keep_d, got_d = tie((keep_d, got_d), send_q)
        send_d, keep_d = cube.halve(keep_d, got_d, f4)
        got_d = cube.swap(send_d, 2)
        share_down = jnp.concatenate([cube.plus(keep_d[p, 0], got_d[p, 0]) for p in range(2)], 1)
        small = (small + cube.swap(small, 4)).reshape(-1)
        c = gate_weight.shape[1]
        share_gate = jnp.concatenate([share_gu[:, 2 * i : 2 * i + TILE] for i in range(0, c, TILE)], 1)
        share_up = jnp.concatenate([share_gu[:, 2 * i + TILE : 2 * i + 2 * TILE] for i in range(0, c, TILE)], 1)
        rel_n, lay_n = relative_bias_table.size, layout_bias_table.size
        grad_rel = small[2 * d : 2 * d + rel_n].reshape(relative_bias_table.shape[::-1]).T
        grad_lay = small[2 * d + rel_n : 2 * d + rel_n + lay_n].reshape(layout_bias_table.shape[::-1]).T
        gains_one, gains_two = small[:d], small[d : 2 * d]
        gains_one, gains_two, grad_rel, grad_lay, share_down, far_q = tie(
            (gains_one, gains_two, grad_rel, grad_lay, share_down, far_q)
        )
        share_query, share_key, share_value, share_out = attention_shares(own_q[0], far_q[0], d)
        return (
            block_out,
            grad_tokens,
            gains_one,
            share_query,
            share_key,
            share_value,
            share_out,
            gains_two,
            share_gate,
            share_up,
            share_down,
            grad_rel,
            grad_lay,
        )

    return body


def solution(mesh):
    rows = P(AXES, None)
    line = P(AXES)
    whole = P()
    return jax.shard_map(
        make_body(Cube(mesh)),
        mesh=mesh,
        in_specs=(
            rows, whole, rows, rows, rows, rows, whole, rows, rows, rows, whole, whole, rows, line, line, rows,
        ),
        out_specs=(
            rows, rows, whole, rows, rows, rows, rows, whole, rows, rows, rows, whole, whole,
        ),
        check_vma=False,
    )
```
